128 devices in a mesh: dp: 8 (over x, y_hi), tensor: 16 (over z, y_lo, core).
Axes of the slice: x: 4, y: 4 (y_hi: 2, y_lo: 2; y = y_hi * 2 + y_lo), z: 4, core: 2. Of those that a mesh axis runs over, the one named last changes fastest.
Arguments:
- tokens: bfloat16 [16, 256, 8192], P('dp'), may hold values from -6 to 6
- segments: int32 [16, 256], P('dp'), may hold values from 0 to 3, never falling along the last dimension, each value on 1 to 128 neighbouring positions
- norm_gain: float32 [8192], replicated, may hold values from 0.25 to 3.5
- q_weight: bfloat16 [8192, 4096], P('dp', 'tensor'), may hold values from -1.3479223 to 1.3479223
- kv_weight: bfloat16 [2, 8192, 512], P(None, 'dp'), may hold values from -0.055242717 to 0.055242717
- o_weight: bfloat16 [4096, 8192], P('tensor', 'dp'), may hold values from -0.09375 to 0.09375
- basis_query: bfloat16 [8, 8192, 4096], P(None, 'dp', 'tensor'), may hold values from -11 to 11
- basis_output: bfloat16 [8, 4096, 8192], P(None, 'tensor', 'dp'), may hold values from -11 to 11
Outputs:
- next_query: bfloat16 [8192, 4096], P('dp', 'tensor')
- next_output: bfloat16 [4096, 8192], P('tensor', 'dp')
- coefficients: float32 [9], replicated
The draws below stay inside these ranges and needn't reach their ends.
Inputs may be any that keep to these rules, and one draw needn't show every extreme that they name: `segments`: segment numbers never fall along a sequence.
All inputs are finite; a program needn't handle non-finite values.
Results may differ from the reference program's by a relative error of at most 0.018.
Values may be sent and summed in bfloat16 or wider, within the bound.
A program may use at most 192 MiB of HBM per device.

```python
import math
import jax
import jax.numpy as jnp
import numpy as np
from jax import lax

D = 8192
HD = 128
QH = 32
KVH = 4
LEN = 256
K = 8
SEQUENCES = 16
N_DP = 8
N_TENSOR = 16


def feature_ramp(low, high):
    return low + (high - low) * jnp.arange(D, dtype=jnp.float32) / (D - 1.0)


def shared_projections(key):
    base_key = jax.random.fold_in(key, 4242)
    kv_width = KVH * HD
    key_part = jnp.clip(jax.random.normal(jax.random.fold_in(base_key, 1), (D, kv_width), jnp.float32), -5.0, 5.0) / math.sqrt(D)
    value_part = jnp.clip(jax.random.normal(jax.random.fold_in(base_key, 2), (D, kv_width), jnp.float32), -5.0, 5.0) / math.sqrt(D)
    query_noise = jnp.clip(jax.random.normal(jax.random.fold_in(base_key, 3), (D, QH * HD), jnp.float32), -5.0, 5.0) / math.sqrt(D)
    query_part = query_noise
    return (query_part, jnp.stack([key_part, value_part]))


def basis_vectors(key, out_shape):
    common = jnp.clip(jax.random.normal(jax.random.fold_in(key, 2), out_shape[1:], jnp.float32), -4.0, 4.0)
    independent = jnp.clip(jax.random.normal(jax.random.fold_in(key, 1), out_shape, jnp.float32), -4.0, 4.0)
    return ((independent + 0.6 * common[None]) / math.sqrt(1.36), feature_ramp(0.4, 2.0))


def draw_norm_gain(key, part):
    jitter = jax.random.uniform(jax.random.fold_in(key, 77), (D,), jnp.float32, 0.85, 1.15)
    return jitter * feature_ramp(0.5, 2.0)


def draw_q_weight(key, part):
    return shared_projections(key)[0].astype(jnp.bfloat16)


def draw_kv_weight(key, part):
    return shared_projections(key)[1].astype(jnp.bfloat16)


def draw_basis_query(key, part):
    values, ramp = basis_vectors(jax.random.fold_in(key, 11), (K, D, QH * HD))
    return (values * ramp[None, :, None]).astype(jnp.bfloat16)


def draw_basis_output(key, part):
    values, ramp = basis_vectors(jax.random.fold_in(key, 13), (K, QH * HD, D))
    return (values * ramp[None, None, :]).astype(jnp.bfloat16)


def steps_of(rng, dims, cuts, least, top_value):
    def one(axis_at, parts):
        steps = jax.random.uniform(jax.random.fold_in(jax.random.fold_in(rng, 6), axis_at), (parts,), jnp.float32, least / len(cuts), top_value / len(cuts))
        return jnp.repeat(jnp.exp(steps), dims[axis_at] // parts).reshape((-1,) + (1,) * (len(dims) - axis_at - 1))

    level = one(*cuts[0])
    for cut in cuts[1:]:
        level = level * one(*cut)
    return level


def profile(count, total, reach, lean):
    portions = [(1 << 20) // math.isqrt(standing ** lean) + 1 for standing in range(2, count + 1)]
    rest, holding = total - reach - (count - 1), [1] * (count - 1)
    while rest > 0:
        candidates = [i for i in range(count - 1) if holding[i] < reach]
        whole, remaining = sum([portions[i] for i in candidates]), rest
        for i in candidates:
            more = min(reach - holding[i], max(1, remaining * portions[i] // whole), rest)
            holding[i] = holding[i] + more
            rest = rest - more
    return np.array([reach] + holding)


def uneven(stream_key, count, total, reach, skew):
    if count == 2:
        one = jax.random.randint(stream_key, (), max(1, total - reach), min(reach, total - 1) + 1)
        return jnp.stack([one, total - one])
    tallies = jnp.asarray(profile(count, total, reach, skew), jnp.int32)
    pairs = (count - 1) // 2
    donor, receiver = tallies[1:1 + 2 * pairs:2], tallies[2:2 + 2 * pairs:2]
    slack = jnp.minimum(donor - 1, reach - receiver)
    passed = jax.random.randint(jax.random.fold_in(stream_key, 1), (pairs,), 0, 1 << 20) % (slack + 1)
    tallies = tallies.at[1:1 + 2 * pairs:2].set(donor - passed).at[2:2 + 2 * pairs:2].set(receiver + passed)
    return tallies[jax.random.permutation(jax.random.fold_in(stream_key, 2), count)]


def gaussian(own_key, shape, scale, limit, pieces=(), held_as=jnp.bfloat16):
    values = jax.random.normal(own_key, shape, jnp.float32) * scale
    if len(pieces) > 0:
        values = steps_of(own_key, shape, pieces, -0.22, 0.18) * values
    return jnp.clip(values, min=-limit, max=limit).astype(held_as)


def setup_inputs(seed: int = 0) -> dict:
    arg_keys = jax.random.split(jax.random.key(seed), 9)
    tokens = gaussian(arg_keys[0], (SEQUENCES, LEN, D), 1.0, 6.0, ((0, 8),))
    segments = jax.vmap(lambda own: jnp.searchsorted(jnp.cumsum(uneven(own, 4, LEN, LEN // 2, 0)), jnp.arange(LEN), side="right"))(jax.random.split(arg_keys[1], SEQUENCES)).reshape((SEQUENCES, LEN)).astype(jnp.int32)
    norm_gain = draw_norm_gain(jax.random.fold_in(arg_keys[8], 71), 0)
    q_weight = draw_q_weight(jax.random.fold_in(arg_keys[8], 71), 0)
    kv_weight = draw_kv_weight(jax.random.fold_in(arg_keys[8], 71), 0)
    o_weight = gaussian(arg_keys[5], (QH * HD, D), (QH * HD) ** -0.5, 0.09375, ((0, 16), (1, 8)))
    basis_query = draw_basis_query(jax.random.fold_in(arg_keys[8], 71), 0)
    basis_output = draw_basis_output(jax.random.fold_in(arg_keys[8], 71), 0)
    return {"tokens": tokens, "segments": segments, "norm_gain": norm_gain, "q_weight": q_weight, "kv_weight": kv_weight, "o_weight": o_weight, "basis_query": basis_query, "basis_output": basis_output}


PRECISE = lax.Precision.HIGHEST
ROPE_BASE = 500000.0
NORM_EPS = 1e-05
BETA_EPS = 1e-06

def rope_tables(length, head_width):
    half_width = head_width // 2
    frequency = jnp.exp(jnp.arange(half_width, dtype=jnp.float32) * (-2.0 * math.log(ROPE_BASE) / head_width))
    angles = jnp.arange(length, dtype=jnp.float32)[:, None] * frequency[None, :]
    return (jnp.cos(angles), jnp.sin(angles))

def rotate(vectors, cosine_table, sine_table):
    half_width = vectors.shape[-1] // 2
    front_half = vectors[..., :half_width]
    back_half = vectors[..., half_width:]
    return jnp.concatenate([front_half * cosine_table - back_half * sine_table, front_half * sine_table + back_half * cosine_table], axis=-1)

def attend(query, key_states, values, allowed):
    length = query.shape[1]
    head_width = query.shape[-1]
    cosine_table, sine_table = rope_tables(length, head_width)
    query = rotate(query, cosine_table[:, None, :], sine_table[:, None, :])
    key_states = rotate(key_states, cosine_table, sine_table)
    scores = jnp.einsum('slgd,smd->sglm', query, key_states, precision=PRECISE) * head_width ** (-0.5)
    scores = jnp.where(allowed[:, None, :, :], scores, -1e+30)
    row_max = lax.stop_gradient(lax.optimization_barrier(jnp.max(scores, axis=-1, keepdims=True)))
    weights = jnp.exp(scores - row_max)
    probabilities = weights / lax.optimization_barrier(jnp.sum(weights, axis=-1, keepdims=True))
    return jnp.einsum('sglm,smd->slgd', probabilities, values, precision=PRECISE)

def allowed_pairs(segments):
    length = segments.shape[1]
    position = jnp.arange(length, dtype=jnp.int32)
    causal = position[:, None] >= position[None, :]
    return jnp.logical_and(segments[:, :, None] == segments[:, None, :], causal[None])

def rms_normed(tokens, norm_gain):
    flat_rows = tokens.reshape(-1, tokens.shape[-1]).astype(jnp.float32)
    inv_rms = lax.rsqrt(lax.optimization_barrier(jnp.mean(flat_rows * flat_rows, axis=1, keepdims=True)) + NORM_EPS)
    return (flat_rows * inv_rms * norm_gain[None, :]).astype(jnp.bfloat16)

def rounded_sum(block_term, term_count, out_shape):

    def add_term(running, block_index):
        rounded = lax.optimization_barrier(block_term(block_index).astype(jnp.bfloat16))
        return (running + rounded.astype(jnp.float32), None)
    running, _ = lax.scan(add_term, jnp.zeros(out_shape, jnp.float32), jnp.arange(term_count, dtype=jnp.int32))
    return running

def reference(tokens, segments, norm_gain, q_weight, kv_weight, o_weight, basis_query, basis_output):
    seq_count, length, model_width = tokens.shape
    qwidth = QH * HD
    group_size = QH // KVH
    row_count = seq_count * length
    block_rows = row_count // N_DP
    col_count = qwidth // N_TENSOR
    query_scale = D ** (-0.5)
    output_scale = qwidth ** (-0.5)
    gn_scale = qwidth / row_count
    param_count = 2.0 * D * qwidth
    normed = rms_normed(tokens, norm_gain)
    dir_query = basis_query[K - 1]
    dir_output = basis_output[K - 1]
    query = jnp.dot(normed, q_weight, preferred_element_type=jnp.float32).astype(jnp.bfloat16)
    tangent = (jnp.dot(normed, dir_query, preferred_element_type=jnp.float32) * query_scale).astype(jnp.bfloat16)
    key_states = jnp.dot(normed, kv_weight[0], preferred_element_type=jnp.float32).astype(jnp.bfloat16)
    values = jnp.dot(normed, kv_weight[1], preferred_element_type=jnp.float32).astype(jnp.bfloat16)
    allowed = allowed_pairs(segments)
    query_wide = query.astype(jnp.float32).reshape(seq_count, length, KVH, group_size, HD)
    tangent_wide = tangent.astype(jnp.float32).reshape(seq_count, length, KVH, group_size, HD)
    key_wide = key_states.astype(jnp.float32).reshape(seq_count, length, KVH, HD)
    value_wide = values.astype(jnp.float32).reshape(seq_count, length, KVH, HD)

    def forward(query_arg, tangent_arg, key_arg, value_arg):
        return jax.jvp(lambda moving: attend(moving, key_arg, value_arg, allowed), (query_arg,), (tangent_arg,))
    heads_out, tangent_heads = jax.vmap(forward, in_axes=(2, 2, 2, 2), out_axes=2)(query_wide, tangent_wide, key_wide, value_wide)
    heads_out = heads_out.reshape(row_count, qwidth).astype(jnp.bfloat16)
    tangent_heads = tangent_heads.reshape(row_count, qwidth).astype(jnp.bfloat16)

    def head_term(block_index):
        offset = block_index * col_count
        part_heads = lax.dynamic_slice_in_dim(heads_out, offset, col_count, 1)
        part_tangent = lax.dynamic_slice_in_dim(tangent_heads, offset, col_count, 1)
        part_dir = lax.dynamic_slice_in_dim(dir_output, offset, col_count, 0)
        part_weight = lax.dynamic_slice_in_dim(o_weight, offset, col_count, 0)
        return jnp.dot(part_heads, part_dir, preferred_element_type=jnp.float32) * output_scale + jnp.dot(part_tangent, part_weight, preferred_element_type=jnp.float32)
    tangent_out = rounded_sum(head_term, N_TENSOR, (row_count, D)).astype(jnp.bfloat16)
    cot_heads = lax.dot_general(tangent_out, o_weight, (((1,), (1,)), ((), ())), preferred_element_type=jnp.float32)
    cot_heads = cot_heads.reshape(seq_count, length, KVH, group_size, HD)

    def backward(query_arg, key_arg, value_arg, cot_arg):
        _, pullback = jax.vjp(lambda moving: attend(moving, key_arg, value_arg, allowed), query_arg)
        return pullback(cot_arg)[0]
    cot_query = jax.vmap(backward, in_axes=(2, 2, 2, 2), out_axes=2)(query_wide, key_wide, value_wide, cot_heads)
    cot_query = cot_query.reshape(row_count, qwidth).astype(jnp.bfloat16)

    def query_term(block_index):
        left_rows = lax.dynamic_slice_in_dim(normed, block_index * block_rows, block_rows, 0)
        right_rows = lax.dynamic_slice_in_dim(cot_query, block_index * block_rows, block_rows, 0)
        return lax.dot_general(left_rows, right_rows, (((0,), (0,)), ((), ())), preferred_element_type=jnp.float32) * (gn_scale * query_scale)

    def output_term(block_index):
        left_rows = lax.dynamic_slice_in_dim(heads_out, block_index * block_rows, block_rows, 0)
        right_rows = lax.dynamic_slice_in_dim(tangent_out, block_index * block_rows, block_rows, 0)
        return lax.dot_general(left_rows, right_rows, (((0,), (0,)), ((), ())), preferred_element_type=jnp.float32) * (gn_scale * output_scale)
    gn_query = rounded_sum(query_term, N_DP, (D, qwidth))
    gn_output = rounded_sum(output_term, N_DP, (qwidth, D))

    def products(vec_query, vec_output):

        def per_vector(basis_pair):
            return jnp.sum(basis_pair[0].astype(jnp.float32) * vec_query) + jnp.sum(basis_pair[1].astype(jnp.float32) * vec_output)
        return lax.map(per_vector, (basis_query, basis_output)) / param_count

    def remove(vec_query, vec_output, weights_now):

        def subtract(carried, basis_item):
            coefficient, part_query, part_output = basis_item
            return ((carried[0] - coefficient * part_query.astype(jnp.float32), carried[1] - coefficient * part_output.astype(jnp.float32)), None)
        carried, _ = lax.scan(subtract, (vec_query, vec_output), (weights_now, basis_query, basis_output))
        return carried
    first_coeffs = products(gn_query, gn_output)
    kept_query, kept_output = remove(gn_query, gn_output, first_coeffs)
    second_coeffs = products(kept_query, kept_output)
    clean_query, clean_output = remove(kept_query, kept_output, second_coeffs)
    squares = (jnp.sum(clean_query * clean_query) + jnp.sum(clean_output * clean_output)) / param_count
    beta = jnp.sqrt(squares + BETA_EPS)
    coefficients = jnp.concatenate([first_coeffs + second_coeffs, beta[None]])
    return ((clean_query / beta).astype(jnp.bfloat16), (clean_output / beta).astype(jnp.bfloat16), coefficients)
```

```python
import functools
import math

import jax
import jax.numpy as jnp
from jax import lax
from jax.experimental import pallas as pl
from jax.experimental.pallas import tpu as pltpu
from jax.sharding import Mesh
from jax.sharding import PartitionSpec as P

D = 8192
HD = 128
QH = 32
KVH = 4
K = 8
DP = ("dp_0", "dp_1")
TENSOR = ("tensor_0", "tensor_1", "tensor_2")
DP_TENSOR = ("dp_0", "dp_1", "tensor_0", "tensor_1", "tensor_2")


PRECISE = lax.Precision.HIGHEST
ROPE_BASE = 500000.0
NORM_EPS = 1e-05
BETA_EPS = 1e-06


MESH = pl.DeviceIdType.MESH
VMEM_BYTES = 58 * 1024 * 1024
X1, X3, X2, YH = (1, 0, 0, 0, 0), (3, 0, 0, 0, 0), (2, 0, 0, 0, 0), (0, 1, 0, 0, 0)
Z1, Z3, YL, CORE = (0, 0, 1, 0, 0), (0, 0, 3, 0, 0), (0, 0, 0, 1, 0), (0, 0, 0, 0, 1)
BF = jnp.bfloat16
F32 = jnp.float32


def position():
    return [lax.axis_index(a) for a in DP_TENSOR]


def flipped(value, mask):
    if mask == 0:
        return value
    if mask == 1:
        return value + 1 - 2 * lax.rem(value, 2)
    if mask == 2:
        return lax.rem(value + 2, 4)
    return 3 - value


def peer(here, masks):
    return tuple(flipped(v, m) for v, m in zip(here, masks))


def greet(here, peers):
    barrier = pltpu.get_barrier_semaphore()
    for masks in peers:
        pl.semaphore_signal(barrier, inc=1, device_id=peer(here, masks), device_id_type=MESH)
    pl.semaphore_wait(barrier, len(peers))


def send(src, dst, send_sem, recv_sem, here, masks):
    copy = pltpu.make_async_remote_copy(
        src_ref=src,
        dst_ref=dst,
        send_sem=send_sem,
        recv_sem=recv_sem,
        device_id=peer(here, masks),
        device_id_type=MESH,
    )
    copy.start()
    return copy


def dp_source(here, first, second, third, kind):
    x, yh = here[0], here[1]
    low, high = (first, third) if kind == 0 else (third, first)
    x = x + low * (1 - 2 * lax.rem(x, 2))
    x = x + high * (3 - 2 * x)
    yh = yh + second * (1 - 2 * yh)
    return x * 2 + yh


STAGES = ((X1, YH, X3), (X3, YH, X1))


def sent_together(arrays, axis, dim, along):
    ends, at = ([], 0)
    for a in arrays[:-1]:
        at += a.shape[along]
        ends.append(at)
    both = jnp.concatenate(arrays, axis=along)
    return tuple(jnp.split(lax.all_gather(both, axis, axis=dim, tiled=True), ends, axis=along))


def filled_up(lines, count):
    spare = -len(lines) % count
    return jnp.pad(lines, [(0, spare)] + [(0, 0)] * (lines.ndim - 1))


def total_of(value, axis):
    lines = value.reshape(-1, *value.shape[1:][-1:])
    own = lax.psum_scatter(
        filled_up(lines, lax.axis_size(axis)), axis, scatter_dimension=0, tiled=True
    )
    whole = lax.all_gather(own, axis).reshape(-1, *lines.shape[1:])
    return lax.slice_in_dim(whole, 0, len(lines)).reshape(value.shape)


def rope_tables(length, head_width):
    half_width = head_width // 2
    frequency = jnp.exp(
        jnp.arange(half_width, dtype=jnp.float32) * (-2.0 * math.log(ROPE_BASE) / head_width)
    )
    angles = jnp.arange(length, dtype=jnp.float32)[:, None] * frequency[None, :]
    return (jnp.cos(angles), jnp.sin(angles))


def rotate(vectors, cosine_table, sine_table):
    half_width = vectors.shape[-1] // 2
    front_half = vectors[..., :half_width]
    back_half = vectors[..., half_width:]
    return jnp.concatenate(
        [
            front_half * cosine_table - back_half * sine_table,
            front_half * sine_table + back_half * cosine_table,
        ],
        axis=-1,
    )


def attend(query, key_states, values, allowed):
    length = query.shape[1]
    head_width = query.shape[-1]
    cosine_table, sine_table = rope_tables(length, head_width)
    query = rotate(query, cosine_table[:, None, :], sine_table[:, None, :])
    key_states = rotate(key_states, cosine_table, sine_table)
    scores = jnp.einsum("slgd,smd->sglm", query, key_states, precision=PRECISE) * head_width ** (
        -0.5
    )
    scores = jnp.where(allowed[:, None, :, :], scores, -1e30)
    row_max = lax.stop_gradient(jnp.max(scores, axis=-1, keepdims=True))
    weights = jnp.exp(scores - row_max)
    probabilities = weights / jnp.sum(weights, axis=-1, keepdims=True)
    return jnp.einsum("sglm,smd->slgd", probabilities, values, precision=PRECISE)


def allowed_pairs(segments):
    length = segments.shape[1]
    position = jnp.arange(length, dtype=jnp.int32)
    causal = position[:, None] >= position[None, :]
    return jnp.logical_and(segments[:, :, None] == segments[:, None, :], causal[None])


def block_products(left_rows, right_rows, block_count, factor):
    left_blocks = left_rows.reshape(block_count, -1, left_rows.shape[1])
    right_blocks = right_rows.reshape(block_count, -1, right_rows.shape[1])
    terms = (
        jnp.einsum("nta,ntb->nab", left_blocks, right_blocks, preferred_element_type=jnp.float32)
        * factor
    )
    rounded = lax.optimization_barrier(terms.astype(jnp.bfloat16))
    return jnp.sum(rounded.astype(jnp.float32), axis=0)


SUPER = (0, 1, 0, 1, 2, 3, 2, 3)
HALF = (0, 0, 1, 1, 0, 0, 1, 1)


def project_kernel(
    tok, gain, q_w, vec_q, kv_w, vec_o,
    q_out, t_out, k_out, v_out, normed_out, gram_out,
    x, buf, acc, mine, theirs, vq, vo, load, sent, got,
):
    here = position()
    core = here[4]
    kv_head = here[2]
    for_rows = []
    for s in range(4):
        rows = pl.ds(s * 256, 256)
        kv_cols = pl.ds(pl.multiple_of(kv_head * HD, HD), HD)
        parts = (
            (q_w.at[rows], buf.at[s, 0, :, pl.ds(0, 256)]),
            (vec_q.at[K - 1, rows], buf.at[s, 0, :, pl.ds(256, 256)]),
            (kv_w.at[core, rows, kv_cols], buf.at[s, 0, :, pl.ds(512, 128)]),
        )
        for n, (src, dst) in enumerate(parts):
            copy = pltpu.make_async_copy(src, dst, load.at[3 * s + n])
            copy.start()
            for_rows.append(copy)
    tok_copy = pltpu.make_async_copy(tok, x, load.at[12])
    tok_copy.start()
    vq_copy = pltpu.make_async_copy(vec_q, vq, load.at[13])
    vq_copy.start()
    vo_copy = pltpu.make_async_copy(vec_o, vo, load.at[14])
    vo_copy.start()
    greet(here, (X1, X3, YH, CORE))
    for copy in for_rows:
        copy.wait()

    def start_stage(stage, k):
        s, rows = SUPER[k], pl.ds(HALF[k] * 128, 128)
        n = 1 << stage
        at = stage * 8 + k
        return send(
            buf.at[s, pl.ds(0, n), rows],
            buf.at[s, pl.ds(n, n), rows],
            sent.at[at],
            got.at[at],
            here,
            STAGES[s % 2][stage],
        )

    first = [start_stage(0, k) for k in range(8)]

    def norm_rows(lo, hi):
        def step(i, carry):
            rows = pl.ds(pl.multiple_of(i * 16, 16), 16)
            total = jnp.zeros((16, 1), F32)
            for c in range(8):
                part = x[rows, pl.ds(c * 1024, 1024)].astype(F32)
                total += jnp.sum(part * part, axis=1, keepdims=True)
            inv = lax.rsqrt(total / D + NORM_EPS)
            for c in range(8):
                cols = pl.ds(c * 1024, 1024)
                x[rows, cols] = (x[rows, cols].astype(F32) * inv * gain[:, cols]).astype(BF)
            return carry

        lax.fori_loop(lo // 16, hi // 16, step, 0)

    def dots(s, lo, hi):
        def step(p, carry):
            source = dp_source(here, lax.rem(p, 2), lax.rem(p // 2, 2), p // 4, s % 2)
            cols = pl.ds(pl.multiple_of(source * 1024 + s * 256, 256), 256)
            acc[...] += jnp.dot(x[:, cols], buf[s, p], preferred_element_type=F32)
            return carry

        lax.fori_loop(lo, hi, step, 0)

    def gram():
        pairs = [(i, j) for i in range(K) for j in range(i, K)]

        def tile(ref, rows, cols, carry):
            b = [ref[j, rows, cols].astype(F32) for j in range(K)]
            out = []
            for (i, j), a in zip(pairs, carry):
                p = b[i] * b[j]
                out.append(a + (p[:8] + p[8:]))
            return tuple(out)

        def step_q(r, carry):
            rows = pl.ds(pl.multiple_of(r * 16, 16), 16)
            for h in range(2):
                carry = tile(vq, rows, pl.ds(h * 128, 128), carry)
            return carry

        def step_o(r, carry):
            rows = pl.ds(pl.multiple_of(r * 16, 16), 16)
            for h in range(8):
                carry = tile(vo, rows, pl.ds(h * 128, 128), carry)
            return carry

        carry = tuple(jnp.zeros((8, 128), F32) for _ in pairs)
        carry = lax.fori_loop(0, 64, step_q, carry)
        carry = lax.fori_loop(0, 16, step_o, carry)
        for (i, j), a in zip(pairs, carry):
            line = jnp.sum(a, axis=0, keepdims=True)
            gram_out[pl.ds(i * 8 + j, 1)] = line
            if i != j:
                gram_out[pl.ds(j * 8 + i, 1)] = line

    acc[...] = jnp.zeros_like(acc)
    second, third = [], []
    out_copy = None
    for k in range(8):
        first[k].wait_recv()
        second.append(start_stage(1, k))
        if k == 0:
            tok_copy.wait()
            norm_rows(0, 256)
        if k >= 1:
            second[k - 1].wait_recv()
            third.append(start_stage(2, k - 1))
        if k == 1:
            norm_rows(256, 512)
            out_copy = pltpu.make_async_copy(x, normed_out, load.at[15])
            out_copy.start()
        if k == 2:
            vq_copy.wait()
            vo_copy.wait()
            gram()
        if k == 4:
            dots(0, 0, 4)
        if k == 5:
            dots(1, 0, 4)
        if k == 7:
            dots(2, 0, 4)
    second[7].wait_recv()
    third.append(start_stage(2, 7))
    dots(3, 0, 4)
    for s, (k0, k1) in enumerate(((0, 2), (1, 3), (4, 6), (5, 7))):
        third[k0].wait_recv()
        third[k1].wait_recv()
        dots(s, 4, 8)
    mine[...] = acc[:, pl.ds(512, 128)].astype(BF)
    swap = send(mine, theirs, sent.at[24], got.at[24], here, CORE)
    q_out[...] = acc[:, pl.ds(0, 256)].astype(BF)
    t_out[...] = (acc[:, pl.ds(256, 256)] * (D ** (-0.5))).astype(BF)
    swap.wait()
    own = mine[...].astype(F32)
    other = theirs[...].astype(F32)
    first_core = core == 0
    k_out[...] = jnp.where(first_core, own, other).astype(BF)
    v_out[...] = jnp.where(first_core, other, own).astype(BF)
    for copy in first + second + third:
        copy.wait_send()
    out_copy.wait()


def any_specs(n):
    return [pl.BlockSpec(memory_space=pl.ANY) for _ in range(n)]


def vmem_specs(n):
    return [pl.BlockSpec(memory_space=pltpu.VMEM) for _ in range(n)]


def project(tokens, norm_gain, q_weight, basis_query, kv_weight, basis_output):
    shape = jax.ShapeDtypeStruct
    return pl.pallas_call(
        project_kernel,
        out_shape=(
            shape((512, 256), BF),
            shape((512, 256), BF),
            shape((512, HD), BF),
            shape((512, HD), BF),
            shape((512, D), BF),
            shape((64, 128), F32),
        ),
        in_specs=any_specs(1) + vmem_specs(1) + any_specs(4),
        out_specs=tuple(vmem_specs(4) + any_specs(1) + vmem_specs(1)),
        scratch_shapes=[
            pltpu.VMEM((512, D), BF),
            pltpu.VMEM((4, 8, 256, 640), BF),
            pltpu.VMEM((512, 640), F32),
            pltpu.VMEM((512, HD), BF),
            pltpu.VMEM((512, HD), BF),
            pltpu.VMEM((K, 1024, 256), BF),
            pltpu.VMEM((K, 256, 1024), BF),
            pltpu.SemaphoreType.DMA((16,)),
            pltpu.SemaphoreType.DMA((25,)),
            pltpu.SemaphoreType.DMA((25,)),
        ],
        compiler_params=pltpu.CompilerParams(
            collective_id=0, has_side_effects=True, vmem_limit_bytes=VMEM_BYTES
        ),
        name="project",
    )(tokens, norm_gain, q_weight, basis_query, kv_weight, basis_output)


def query_grad_kernel(factor, normed, cot, out, part, r1, r2, r3, sent, got):
    here = position()
    greet(here, (X1, X3, YH))
    copies = []

    def product(low, mid, high):
        source = dp_source(here, low, mid, high, 0)
        cols = pl.ds(pl.multiple_of(source * 1024, 1024), 1024)
        block = jnp.dot(cot[...], normed[:, cols], preferred_element_type=F32) * factor
        block = block.astype(BF)
        for c in range(8):
            place = low + 2 * mid + 4 * high if c % 2 == 0 else high + 2 * mid + 4 * low
            part[c, place] = block[:, c * 128 : (c + 1) * 128]

    def start(stage, c, src, dst):
        at = stage * 8 + c
        copy = send(src, dst, sent.at[at], got.at[at], here, STAGES[c % 2][2 - stage])
        copies.append(copy)
        return copy

    def start_first(c):
        return start(0, c, part.at[c, pl.ds(4, 4)], r1.at[c])

    product(1, 0, 1)
    product(1, 1, 1)
    product(0, 0, 1)
    product(0, 1, 1)
    one = {c: start_first(c) for c in (0, 2, 4, 6)}
    product(1, 0, 0)
    product(1, 1, 0)
    one.update({c: start_first(c) for c in (1, 3, 5, 7)})
    product(0, 0, 0)
    product(0, 1, 0)

    def added(c, n, ref):
        part[c, pl.ds(0, n)] = (
            part[c, pl.ds(0, n)].astype(F32) + ref[c].astype(F32)
        ).astype(BF)

    two, three = {}, {}
    for c in range(8):
        one[c].wait_recv()
        added(c, 4, r1)
        two[c] = start(1, c, part.at[c, pl.ds(2, 2)], r2.at[c])
        if c >= 1:
            two[c - 1].wait_recv()
            added(c - 1, 2, r2)
            three[c - 1] = start(2, c - 1, part.at[c - 1, pl.ds(1, 1)], r3.at[c - 1])
    two[7].wait_recv()
    added(7, 2, r2)
    three[7] = start(2, 7, part.at[7, pl.ds(1, 1)], r3.at[7])
    for c in range(8):
        three[c].wait_recv()
        total = part[c, 0].astype(F32) + r3[c, 0].astype(F32)
        out[pl.ds(c * 128, 128), :] = total.T
    for copy in copies:
        copy.wait_send()


def query_grad(normed, cot_rows, factor):
    return pl.pallas_call(
        functools.partial(query_grad_kernel, factor),
        out_shape=jax.ShapeDtypeStruct((1024, 256), F32),
        in_specs=vmem_specs(2),
        out_specs=pl.BlockSpec(memory_space=pltpu.VMEM),
        scratch_shapes=[
            pltpu.VMEM((8, 8, 256, 128), BF),
            pltpu.VMEM((8, 4, 256, 128), BF),
            pltpu.VMEM((8, 2, 256, 128), BF),
            pltpu.VMEM((8, 1, 256, 128), BF),
            pltpu.SemaphoreType.DMA((24,)),
            pltpu.SemaphoreType.DMA((24,)),
        ],
        compiler_params=pltpu.CompilerParams(
            collective_id=1, has_side_effects=True, vmem_limit_bytes=VMEM_BYTES
        ),
        name="query_grad",
    )(normed, cot_rows)


DP_PEERS = [(x, yh, 0, 0, 0) for x in range(4) for yh in range(2) if x or yh]
TENSOR_PEERS = [(0, 0, z, yl, c) for z in range(4) for yl in range(2) for c in range(2) if z or yl or c]


def sum_over(here, slots_dp, slots_tensor, staged, sent, got, at):
    dp = here[0] * 2 + here[1]
    tensor = here[2] * 4 + here[3] * 2 + here[4]

    def exchange(slots, own, peers, base):
        copies = []
        for n, masks in enumerate(peers):
            ref = slots.at[own]
            copies.append(send(ref, ref, sent.at[base + n], got.at[base + n], here, masks))
        return copies

    one = exchange(slots_dp, dp, DP_PEERS, at)
    for copy in one:
        copy.wait_recv()
    total = slots_dp[0]
    for n in range(1, 8):
        total = total + slots_dp[n]
    slots_tensor[tensor] = total
    two = exchange(slots_tensor, tensor, TENSOR_PEERS, at + 7)
    for copy in two:
        copy.wait_recv()
    total = slots_tensor[0]
    for n in range(1, 16):
        total = total + slots_tensor[n]
    for copy in one + two:
        copy.wait_send()
    return total


def clean_kernel(
    count, gq, go, vq, vo, gram, next_q, next_o, coeffs,
    cq, co, s1, s2, u1, u2, sent, got,
):
    here = position()
    dp = here[0] * 2 + here[1]
    greet(here, DP_PEERS + TENSOR_PEERS)

    def over_tiles(visit, carry):
        def step_q(r, state):
            rows = pl.ds(pl.multiple_of(r * 16, 16), 16)
            for h in range(2):
                state = visit(gq, vq, cq, rows, pl.ds(h * 128, 128), state)
            return state

        def step_o(r, state):
            rows = pl.ds(pl.multiple_of(r * 16, 16), 16)
            for h in range(8):
                state = visit(go, vo, co, rows, pl.ds(h * 128, 128), state)
            return state

        carry = lax.fori_loop(0, 64, step_q, carry)
        return lax.fori_loop(0, 16, step_o, carry)

    def against_basis(g, v, c, rows, cols, state):
        here_g = g[rows, cols]
        out = []
        for j in range(K):
            p = here_g * v[j, rows, cols].astype(F32)
            out.append(state[j] + (p[:8] + p[8:]))
        return tuple(out)

    zero = jnp.zeros((8, 128), F32)
    firsts = over_tiles(against_basis, (zero,) * K)
    s1[dp, pl.ds(0, 64)] = gram[...]
    for j in range(K):
        s1[dp, pl.ds(64 + j, 1)] = jnp.sum(firsts[j], axis=0, keepdims=True)
    total = sum_over(here, s1, s2, None, sent, got, 0)
    lines = jnp.sum(total, axis=1, keepdims=True) / count
    first = lines[64:72]
    second = first
    for i in range(K):
        second = second - lines[8 * i : 8 * i + 8] * first[i : i + 1]
    both = first + second
    weights = [jnp.broadcast_to(both[j : j + 1], (16, 128)) for j in range(K)]

    def cleaned(g, v, c, rows, cols, state):
        value = g[rows, cols]
        for j in range(K):
            value = value - weights[j] * v[j, rows, cols].astype(F32)
        c[rows, cols] = value
        p = value * value
        return state + (p[:8] + p[8:])

    u1[dp] = over_tiles(cleaned, zero)
    squares = sum_over(here, u1, u2, None, sent, got, 22)
    squares = jnp.sum(jnp.sum(squares, axis=1, keepdims=True), axis=0, keepdims=True) / count
    beta = jnp.sqrt(squares + BETA_EPS)
    next_q[...] = (cq[...] / beta).astype(BF)
    next_o[...] = (co[...] / beta).astype(BF)
    coeffs[pl.ds(0, 8)] = jnp.broadcast_to(both, (8, 128))
    coeffs[pl.ds(8, 8)] = jnp.broadcast_to(beta, (8, 128))


def clean(gn_query, gn_output, basis_query, basis_output, gram, count):
    shape = jax.ShapeDtypeStruct
    return pl.pallas_call(
        functools.partial(clean_kernel, count),
        out_shape=(shape((1024, 256), BF), shape((256, 1024), BF), shape((16, 128), F32)),
        in_specs=vmem_specs(5),
        out_specs=tuple(vmem_specs(3)),
        scratch_shapes=[
            pltpu.VMEM((1024, 256), F32),
            pltpu.VMEM((256, 1024), F32),
            pltpu.VMEM((8, 72, 128), F32),
            pltpu.VMEM((16, 72, 128), F32),
            pltpu.VMEM((8, 8, 128), F32),
            pltpu.VMEM((16, 8, 128), F32),
            pltpu.SemaphoreType.DMA((44,)),
            pltpu.SemaphoreType.DMA((44,)),
        ],
        compiler_params=pltpu.CompilerParams(
            collective_id=2, has_side_effects=True, vmem_limit_bytes=VMEM_BYTES
        ),
        name="clean",
    )(gn_query, gn_output, basis_query, basis_output, gram)


def body(tokens, segments, norm_gain, q_weight, kv_weight, o_weight, basis_query, basis_output):
    groups = lax.axis_size(DP)
    seq_count, length, model_width = tokens.shape
    row_count = seq_count * length
    col_count = q_weight.shape[1]
    heads_dev = col_count // HD
    group_size = QH // KVH
    qwidth = QH * HD
    query_scale = D ** (-0.5)
    output_scale = qwidth ** (-0.5)
    gn_scale = qwidth / (row_count * groups)
    param_count = 2.0 * D * qwidth
    dir_output = basis_output[K - 1]
    query, tangent, key_states, values, normed, gram = project(
        tokens.reshape(row_count, model_width),
        norm_gain.reshape(1, model_width),
        q_weight,
        basis_query,
        kv_weight,
        basis_output,
    )
    allowed = allowed_pairs(segments)
    query_wide = query.astype(jnp.float32).reshape(seq_count, length, heads_dev, HD)
    tangent_wide = tangent.astype(jnp.float32).reshape(seq_count, length, heads_dev, HD)
    key_wide = key_states.astype(jnp.float32).reshape(seq_count, length, HD)
    value_wide = values.astype(jnp.float32).reshape(seq_count, length, HD)

    def attend_here(moving):
        return attend(moving, key_wide, value_wide, allowed)

    heads_out, tangent_heads = jax.jvp(attend_here, (query_wide,), (tangent_wide,))
    heads_out = heads_out.reshape(row_count, col_count).astype(jnp.bfloat16)
    tangent_heads = tangent_heads.reshape(row_count, col_count).astype(jnp.bfloat16)
    all_heads, all_tangent = sent_together((heads_out, tangent_heads), DP, 0, 1)
    group_term = jnp.dot(
        all_heads, dir_output, preferred_element_type=jnp.float32
    ) * output_scale + jnp.dot(all_tangent, o_weight, preferred_element_type=jnp.float32)
    tangent_columns = (
        total_of(group_term.astype(jnp.bfloat16), TENSOR).astype(jnp.float32).astype(jnp.bfloat16)
    )
    cot_heads = lax.psum_scatter(
        lax.dot_general(
            tangent_columns, o_weight, (((1,), (1,)), ((), ())), preferred_element_type=jnp.float32
        ).astype(jnp.bfloat16),
        DP,
        scatter_dimension=0,
        tiled=True,
    ).astype(jnp.float32)
    gn_output = block_products(all_heads, tangent_columns, groups, gn_scale * output_scale)
    _, pullback = jax.vjp(attend_here, query_wide)
    cot_query = pullback(cot_heads.reshape(seq_count, length, heads_dev, HD))[0]
    cot_query = cot_query.reshape(row_count, col_count).astype(jnp.bfloat16)
    gn_query = query_grad(normed, cot_query.T, gn_scale * query_scale)
    next_query, next_output, lines = clean(
        gn_query, gn_output, basis_query, basis_output, gram, param_count
    )
    return (next_query, next_output, lines[:9, 0])


def solution(mesh):
    finer = Mesh(
        mesh.devices.reshape(4, 2, 4, 2, 2), ("dp_0", "dp_1", "tensor_0", "tensor_1", "tensor_2")
    )
    placed = (
        P(DP, None, None),
        P(DP, None),
        P(),
        P(DP, TENSOR),
        P(None, DP, None),
        P(TENSOR, DP),
        P(None, DP, TENSOR),
        P(None, TENSOR, DP),
    )
    return jax.shard_map(
        body,
        mesh=finer,
        in_specs=placed,
        out_specs=(P(DP, TENSOR), P(TENSOR, DP), P()),
        check_vma=False,
    )
```

```python
import functools
import math

import jax
import jax.numpy as jnp
from jax import lax
from jax.experimental import pallas as pl
from jax.experimental.pallas import tpu as pltpu
from jax.sharding import Mesh
from jax.sharding import PartitionSpec as P

D = 8192
HD = 128
QH = 32
KVH = 4
K = 8
DP = ("dp_0", "dp_1")
TENSOR = ("tensor_0", "tensor_1", "tensor_2")
DP_TENSOR = ("dp_0", "dp_1", "tensor_0", "tensor_1", "tensor_2")


PRECISE = lax.Precision.HIGHEST
ROPE_BASE = 500000.0
NORM_EPS = 1e-05
BETA_EPS = 1e-06


MESH = pl.DeviceIdType.MESH
VMEM_BYTES = 58 * 1024 * 1024
X1, X3, X2, YH = (1, 0, 0, 0, 0), (3, 0, 0, 0, 0), (2, 0, 0, 0, 0), (0, 1, 0, 0, 0)
Z1, Z3, YL, CORE = (0, 0, 1, 0, 0), (0, 0, 3, 0, 0), (0, 0, 0, 1, 0), (0, 0, 0, 0, 1)
BF = jnp.bfloat16
F32 = jnp.float32


def position():
    return [lax.axis_index(a) for a in DP_TENSOR]


def flipped(value, mask):
    if mask == 0:
        return value
    if mask == 1:
        return value + 1 - 2 * lax.rem(value, 2)
    if mask == 2:
        return lax.rem(value + 2, 4)
    return 3 - value


def peer(here, masks):
    return tuple(flipped(v, m) for v, m in zip(here, masks))


def greet(here, peers):
    barrier = pltpu.get_barrier_semaphore()
    for masks in peers:
        pl.semaphore_signal(barrier, inc=1, device_id=peer(here, masks), device_id_type=MESH)
    pl.semaphore_wait(barrier, len(peers))


def send(src, dst, send_sem, recv_sem, here, masks):
    copy = pltpu.make_async_remote_copy(
        src_ref=src,
        dst_ref=dst,
        send_sem=send_sem,
        recv_sem=recv_sem,
        device_id=peer(here, masks),
        device_id_type=MESH,
    )
    copy.start()
    return copy


def dp_source(here, first, second, third, kind):
    x, yh = here[0], here[1]
    low, high = (first, third) if kind == 0 else (third, first)
    x = x + low * (1 - 2 * lax.rem(x, 2))
    x = x + high * (3 - 2 * x)
    yh = yh + second * (1 - 2 * yh)
    return x * 2 + yh


STAGES = ((X1, YH, X3), (X3, YH, X1))
OUT_STAGES = ((YL, Z1, Z3, CORE), (YL, Z3, Z1, CORE))


DP_PEERS = [(x, yh, 0, 0, 0) for x in range(4) for yh in range(2) if x or yh]
TENSOR_PEERS = [(0, 0, z, yl, c) for z in range(4) for yl in range(2) for c in range(2) if z or yl or c]


def z_place(mask, kind):
    one, three = {0: (0, 0), 1: (1, 0), 3: (0, 1), 2: (1, 1)}[mask]
    return one + 2 * three if kind == 0 else three + 2 * one


def out_place(r, kind):
    mz, ml, mc = r // 4, r // 2 % 2, r % 2
    return ml + 2 * z_place(mz, kind) + 8 * mc


def tensor_masks(r):
    return (0, 0, r // 4, r // 2 % 2, r % 2)


def rope_tables(length, head_width):
    half_width = head_width // 2
    frequency = jnp.exp(
        jnp.arange(half_width, dtype=jnp.float32) * (-2.0 * math.log(ROPE_BASE) / head_width)
    )
    angles = jnp.arange(length, dtype=jnp.float32)[:, None] * frequency[None, :]
    return (jnp.cos(angles), jnp.sin(angles))


def rotate(vectors, cosine_table, sine_table):
    half_width = vectors.shape[-1] // 2
    front_half = vectors[..., :half_width]
    back_half = vectors[..., half_width:]
    return jnp.concatenate(
        [
            front_half * cosine_table - back_half * sine_table,
            front_half * sine_table + back_half * cosine_table,
        ],
        axis=-1,
    )


def attend(query, key_states, values, allowed):
    length = query.shape[1]
    head_width = query.shape[-1]
    cosine_table, sine_table = rope_tables(length, head_width)
    query = rotate(query, cosine_table[:, None, :], sine_table[:, None, :])
    key_states = rotate(key_states, cosine_table, sine_table)
    scores = jnp.einsum("slgd,smd->sglm", query, key_states, precision=PRECISE) * head_width ** (
        -0.5
    )
    scores = jnp.where(allowed[:, None, :, :], scores, -1e30)
    row_max = lax.stop_gradient(jnp.max(scores, axis=-1, keepdims=True))
    weights = jnp.exp(scores - row_max)
    probabilities = weights / jnp.sum(weights, axis=-1, keepdims=True)
    return jnp.einsum("sglm,smd->slgd", probabilities, values, precision=PRECISE)


def allowed_pairs(segments):
    length = segments.shape[1]
    position = jnp.arange(length, dtype=jnp.int32)
    causal = position[:, None] >= position[None, :]
    return jnp.logical_and(segments[:, :, None] == segments[:, None, :], causal[None])


SUPER = (0, 1, 0, 1, 2, 3, 2, 3)
HALF = (0, 0, 1, 1, 0, 0, 1, 1)


def project_kernel(
    tok, gain, q_w, vec_q, kv_w, vec_o, o_w,
    q_out, t_out, k_out, v_out, normed_out, gram_out, wall,
    x, buf, acc, mine, theirs, vq, vo, load, sent, got,
):
    here = position()
    core = here[4]
    kv_head = here[2]
    for_rows = []
    for s in range(4):
        rows = pl.ds(s * 256, 256)
        kv_cols = pl.ds(pl.multiple_of(kv_head * HD, HD), HD)
        parts = (
            (q_w.at[rows], buf.at[s, 0, :, pl.ds(0, 256)]),
            (vec_q.at[K - 1, rows], buf.at[s, 0, :, pl.ds(256, 256)]),
            (kv_w.at[core, rows, kv_cols], buf.at[s, 0, :, pl.ds(512, 128)]),
        )
        for n, (src, dst) in enumerate(parts):
            copy = pltpu.make_async_copy(src, dst, load.at[3 * s + n])
            copy.start()
            for_rows.append(copy)
    own_out = []
    for kind, src in enumerate((vec_o.at[K - 1], o_w)):
        copy = pltpu.make_async_copy(src, wall.at[kind, 0], load.at[16 + kind])
        copy.start()
        own_out.append(copy)
    tok_copy = pltpu.make_async_copy(tok, x, load.at[12])
    tok_copy.start()
    vq_copy = pltpu.make_async_copy(vec_q, vq, load.at[13])
    vq_copy.start()
    vo_copy = pltpu.make_async_copy(vec_o, vo, load.at[14])
    vo_copy.start()
    greet(here, (X1, X3, YH, CORE, Z1, Z3, YL))
    for copy in for_rows:
        copy.wait()

    def start_stage(stage, k):
        s, rows = SUPER[k], pl.ds(HALF[k] * 128, 128)
        n = 1 << stage
        at = stage * 8 + k
        return send(
            buf.at[s, pl.ds(0, n), rows],
            buf.at[s, pl.ds(n, n), rows],
            sent.at[at],
            got.at[at],
            here,
            STAGES[s % 2][stage],
        )

    first = [start_stage(0, k) for k in range(8)]
    out_copies = {}

    def start_out(stage, kind, half):
        n = 1 << stage
        rows = pl.ds(half * 128, 128)
        at = 25 + stage * 4 + kind * 2 + half
        out_copies[stage, kind, half] = send(
            wall.at[kind, pl.ds(0, n), rows],
            wall.at[kind, pl.ds(n, n), rows],
            sent.at[at],
            got.at[at],
            here,
            OUT_STAGES[kind][stage],
        )

    def next_out(stage, half):
        for kind in range(2):
            out_copies[stage, kind, half].wait_recv()
            start_out(stage + 1, kind, half)

    for copy in own_out:
        copy.wait()
    for half in range(2):
        for kind in range(2):
            start_out(0, kind, half)

    def norm_rows(lo, hi):
        def step(i, carry):
            rows = pl.ds(pl.multiple_of(i * 16, 16), 16)
            total = jnp.zeros((16, 1), F32)
            for c in range(8):
                part = x[rows, pl.ds(c * 1024, 1024)].astype(F32)
                total += jnp.sum(part * part, axis=1, keepdims=True)
            inv = lax.rsqrt(total / D + NORM_EPS)
            for c in range(8):
                cols = pl.ds(c * 1024, 1024)
                x[rows, cols] = (x[rows, cols].astype(F32) * inv * gain[:, cols]).astype(BF)
            return carry

        lax.fori_loop(lo // 16, hi // 16, step, 0)

    def dots(s, lo, hi):
        def step(p, carry):
            source = dp_source(here, lax.rem(p, 2), lax.rem(p // 2, 2), p // 4, s % 2)
            cols = pl.ds(pl.multiple_of(source * 1024 + s * 256, 256), 256)
            acc[...] += jnp.dot(x[:, cols], buf[s, p], preferred_element_type=F32)
            return carry

        lax.fori_loop(lo, hi, step, 0)

    def gram():
        pairs = [(i, j) for i in range(K) for j in range(i, K)]

        def tile(ref, rows, cols, carry):
            b = [ref[j, rows, cols].astype(F32) for j in range(K)]
            out = []
            for (i, j), a in zip(pairs, carry):
                p = b[i] * b[j]
                out.append(a + (p[:8] + p[8:]))
            return tuple(out)

        def step_q(r, carry):
            rows = pl.ds(pl.multiple_of(r * 16, 16), 16)
            for h in range(2):
                carry = tile(vq, rows, pl.ds(h * 128, 128), carry)
            return carry

        def step_o(r, carry):
            rows = pl.ds(pl.multiple_of(r * 16, 16), 16)
            for h in range(8):
                carry = tile(vo, rows, pl.ds(h * 128, 128), carry)
            return carry

        carry = tuple(jnp.zeros((8, 128), F32) for _ in pairs)
        carry = lax.fori_loop(0, 64, step_q, carry)
        carry = lax.fori_loop(0, 16, step_o, carry)
        for (i, j), a in zip(pairs, carry):
            line = jnp.sum(a, axis=0, keepdims=True)
            gram_out[pl.ds(i * 8 + j, 1)] = line
            if i != j:
                gram_out[pl.ds(j * 8 + i, 1)] = line

    acc[...] = jnp.zeros_like(acc)
    second, third = [], []
    out_copy = None
    for k in range(8):
        first[k].wait_recv()
        second.append(start_stage(1, k))
        if k == 0:
            tok_copy.wait()
            norm_rows(0, 256)
        if k >= 1:
            second[k - 1].wait_recv()
            third.append(start_stage(2, k - 1))
        if k == 1:
            norm_rows(256, 512)
            out_copy = pltpu.make_async_copy(x, normed_out, load.at[15])
            out_copy.start()
        if k == 2:
            vq_copy.wait()
            vo_copy.wait()
            gram()
        if k < 2:
            next_out(0, k)
        if k == 2:
            next_out(1, 0)
        if k == 4:
            next_out(1, 1)
        if k == 6:
            next_out(2, 0)
        if k == 4:
            dots(0, 0, 4)
        if k == 5:
            dots(1, 0, 4)
        if k == 7:
            dots(2, 0, 4)
    second[7].wait_recv()
    third.append(start_stage(2, 7))
    next_out(2, 1)
    dots(3, 0, 4)
    for s, (k0, k1) in enumerate(((0, 2), (1, 3), (4, 6), (5, 7))):
        third[k0].wait_recv()
        third[k1].wait_recv()
        dots(s, 4, 8)
    mine[...] = acc[:, pl.ds(512, 128)].astype(BF)
    swap = send(mine, theirs, sent.at[24], got.at[24], here, CORE)
    q_out[...] = acc[:, pl.ds(0, 256)].astype(BF)
    t_out[...] = (acc[:, pl.ds(256, 256)] * (D ** (-0.5))).astype(BF)
    swap.wait()
    own = mine[...].astype(F32)
    other = theirs[...].astype(F32)
    first_core = core == 0
    k_out[...] = jnp.where(first_core, own, other).astype(BF)
    v_out[...] = jnp.where(first_core, other, own).astype(BF)
    for copy in first + second + third:
        copy.wait_send()
    for (stage, kind, half), copy in out_copies.items():
        copy.wait_send()
        if stage == 3:
            copy.wait_recv()
    out_copy.wait()


def any_specs(n):
    return [pl.BlockSpec(memory_space=pl.ANY) for _ in range(n)]


def vmem_specs(n):
    return [pl.BlockSpec(memory_space=pltpu.VMEM) for _ in range(n)]


def project(tokens, norm_gain, q_weight, basis_query, kv_weight, basis_output, o_weight):
    shape = jax.ShapeDtypeStruct
    return pl.pallas_call(
        project_kernel,
        out_shape=(
            shape((512, 256), BF),
            shape((512, 256), BF),
            shape((512, HD), BF),
            shape((512, HD), BF),
            shape((512, D), BF),
            shape((64, 128), F32),
            shape((2, 16, 256, 1024), BF),
        ),
        in_specs=any_specs(1) + vmem_specs(1) + any_specs(5),
        out_specs=tuple(vmem_specs(4) + any_specs(1) + vmem_specs(1) + any_specs(1)),
        scratch_shapes=[
            pltpu.VMEM((512, D), BF),
            pltpu.VMEM((4, 8, 256, 640), BF),
            pltpu.VMEM((512, 640), F32),
            pltpu.VMEM((512, HD), BF),
            pltpu.VMEM((512, HD), BF),
            pltpu.VMEM((K, 1024, 256), BF),
            pltpu.VMEM((K, 256, 1024), BF),
            pltpu.SemaphoreType.DMA((18,)),
            pltpu.SemaphoreType.DMA((41,)),
            pltpu.SemaphoreType.DMA((41,)),
        ],
        compiler_params=pltpu.CompilerParams(
            collective_id=0, has_side_effects=True, vmem_limit_bytes=VMEM_BYTES
        ),
        name="project",
    )(tokens, norm_gain, q_weight, basis_query, kv_weight, basis_output, o_weight)


def output_kernel(
    h, wall, cot, gp_out,
    w, g, acc, tb, cs, c1, c2, c3, gp, load, sent, got,
):
    here = position()
    tensor = here[2] * 4 + here[3] * 2 + here[4]
    loads = []
    for kind in (0, 1):
        copy = pltpu.make_async_copy(wall.at[kind], w.at[kind], load.at[kind])
        copy.start()
        loads.append(copy)
    greet(here, [X1, X3, YH] + TENSOR_PEERS)
    copies = []

    def start(at, src, dst, masks):
        copy = send(src, dst, sent.at[at], got.at[at], here, masks)
        copies.append(copy)
        return copy

    def index_of(r):
        z, yl, c = peer(here[2:], tensor_masks(r)[2:])
        return z * 4 + yl * 2 + c

    spread = {
        r: start(r, h.at[index_of(r)], g.at[:, r, 0], tensor_masks(r)) for r in range(1, 16)
    }
    g[:, 0, 0] = h[tensor]

    def gather(stage, rg, kind):
        n = 1 << stage
        group = pl.ds(rg * 4, 4)
        return start(
            16 + stage * 8 + rg * 2 + kind,
            g.at[kind, group, pl.ds(0, n)],
            g.at[kind, group, pl.ds(n, n)],
            STAGES[kind][stage],
        )

    one, two, three = {}, {}, {}
    for rg in range(4):
        for r in range(rg * 4, rg * 4 + 4):
            if r:
                spread[r].wait_recv()
        for kind in range(2):
            one[rg, kind] = gather(0, rg, kind)
    order = [(rg, kind) for rg in range(4) for kind in range(2)]
    for n, key in enumerate(order):
        one[key].wait_recv()
        two[key] = gather(1, *key)
        if n >= 1:
            two[order[n - 1]].wait_recv()
            three[order[n - 1]] = gather(2, *order[n - 1])
    two[order[7]].wait_recv()
    three[order[7]] = gather(2, *order[7])

    def rows_of(r, cols):
        parts = [g[kind, r, :, :, cols].reshape(128, 256) for kind in range(2)]
        return jnp.concatenate(parts, axis=0)

    for copy in loads:
        copy.wait()
    acc[...] = jnp.zeros_like(acc)
    for rg in range(4):
        three[rg, 0].wait_recv()
        three[rg, 1].wait_recv()
        for r in range(rg * 4, rg * 4 + 4):
            acc[...] += jnp.dot(
                rows_of(r, pl.ds(0, 256)), w[0, out_place(r, 0)], preferred_element_type=F32
            ) + jnp.dot(
                rows_of(r, pl.ds(256, 256)), w[1, out_place(r, 1)], preferred_element_type=F32
            )
    tb[...] = acc[...].astype(BF)

    def scatter(stage, key, src, dst):
        rg, kind = key
        return start(40 + stage * 8 + rg * 2 + kind, src, dst, STAGES[kind][2 - stage])

    one, two, three = {}, {}, {}
    for rg in range(4):
        group = pl.ds(rg * 4, 4)
        for r in range(rg * 4, rg * 4 + 4):
            part = lax.dot_general(
                tb[...],
                w[1, out_place(r, 1)],
                (((1,), (1,)), ((), ())),
                preferred_element_type=F32,
            ).astype(BF)
            for kind in range(2):
                cs[kind, r] = part[kind * 128 : kind * 128 + 128].reshape(8, 16, 256)
        for kind in range(2):
            one[rg, kind] = scatter(
                0, (rg, kind), cs.at[kind, group, pl.ds(4, 4)], c1.at[kind, group]
            )

    def added(key, n, ref):
        rg, kind = key
        group = pl.ds(rg * 4, 4)
        cs[kind, group, pl.ds(0, n)] = (
            cs[kind, group, pl.ds(0, n)].astype(F32) + ref[kind, group].astype(F32)
        ).astype(BF)

    def output_grad(r):
        mz, ml, mc = r // 4, r // 2 % 2, r % 2
        block = lax.dot_general(
            rows_of(r, pl.ds(0, 256)),
            tb[...],
            (((0,), (0,)), ((), ())),
            preferred_element_type=F32,
        ).astype(BF)
        for kind in range(2):
            gp[mc, kind, z_place(mz, kind), ml] = block[:, kind * 512 : kind * 512 + 512]

    def second(key):
        rg, kind = key
        one[key].wait_recv()
        added(key, 4, c1)
        group = pl.ds(rg * 4, 4)
        two[key] = scatter(1, key, cs.at[kind, group, pl.ds(2, 2)], c2.at[kind, group])

    def third(key):
        rg, kind = key
        two[key].wait_recv()
        added(key, 2, c2)
        group = pl.ds(rg * 4, 4)
        three[key] = scatter(2, key, cs.at[kind, group, pl.ds(1, 1)], c3.at[kind, group])

    for n, key in enumerate(order):
        second(key)
        if n >= 1:
            third(order[n - 1])
        output_grad(2 * n)
        output_grad(2 * n + 1)
    third(order[7])
    back = {}
    for rg in range(4):
        for kind in range(2):
            three[rg, kind].wait_recv()
            added((rg, kind), 1, c3)
        for r in range(rg * 4, rg * 4 + 4):
            if r:
                back[r] = start(64 + r, cs.at[:, r, 0], cot.at[tensor], tensor_masks(r))
    cot[tensor] = cs[:, 0, 0]
    gp_copy = pltpu.make_async_copy(gp, gp_out, load.at[2])
    gp_copy.start()
    for r in range(1, 16):
        back[r].wait_recv()
    for copy in copies:
        copy.wait_send()
    gp_copy.wait()


def output_side(heads, wall):
    shape = jax.ShapeDtypeStruct
    return pl.pallas_call(
        output_kernel,
        out_shape=(shape((16, 2, 16, 256), BF), shape((2, 2, 4, 2, 256, 512), BF)),
        in_specs=vmem_specs(1) + any_specs(1),
        out_specs=tuple(vmem_specs(1) + any_specs(1)),
        scratch_shapes=[
            pltpu.VMEM((2, 16, 256, 1024), BF),
            pltpu.VMEM((2, 16, 8, 16, 512), BF),
            pltpu.VMEM((256, 1024), F32),
            pltpu.VMEM((256, 1024), BF),
            pltpu.VMEM((2, 16, 8, 16, 256), BF),
            pltpu.VMEM((2, 16, 4, 16, 256), BF),
            pltpu.VMEM((2, 16, 2, 16, 256), BF),
            pltpu.VMEM((2, 16, 1, 16, 256), BF),
            pltpu.VMEM((2, 2, 4, 2, 256, 512), BF),
            pltpu.SemaphoreType.DMA((3,)),
            pltpu.SemaphoreType.DMA((80,)),
            pltpu.SemaphoreType.DMA((80,)),
        ],
        compiler_params=pltpu.CompilerParams(
            collective_id=3, has_side_effects=True, vmem_limit_bytes=VMEM_BYTES
        ),
        name="output_side",
    )(heads, wall)


def grads_kernel(
    factor, normed, cot, gp, out_q, out_o,
    part, r1, r2, r3, own, rc, z1, z2, y1, load, sent, got,
):
    here = position()
    load_own = pltpu.make_async_copy(gp.at[0], own, load.at[0])
    load_own.start()
    greet(here, (X1, X3, YH, CORE, Z1, Z3, YL))
    copies = []

    def keep(copy):
        copies.append(copy)
        return copy

    def rows_at(j):
        return pl.ds(j // 2 * 64, 64)

    def start_out(stage, j, src, dst):
        at = 24 + stage * 8 + j
        masks = (CORE, (Z3, Z1)[j % 2], (Z1, Z3)[j % 2], YL)[stage]
        return keep(send(src, dst, sent.at[at], got.at[at], here, masks))

    over_core = [
        start_out(0, j, gp.at[1, j % 2, :, :, rows_at(j)], rc.at[j % 2, :, :, rows_at(j)])
        for j in range(8)
    ]
    z_high, z_low, over_y = {}, {}, {}

    def out_high(j):
        kind, rows = j % 2, rows_at(j)
        over_core[j].wait_recv()
        own[kind, :, :, rows] = (
            own[kind, :, :, rows].astype(F32) + rc[kind, :, :, rows].astype(F32)
        ).astype(BF)
        z_high[j] = start_out(1, j, own.at[kind, pl.ds(2, 2), :, rows], z1.at[kind, :, :, rows])

    def out_low(j):
        kind, rows = j % 2, rows_at(j)
        z_high[j].wait_recv()
        own[kind, pl.ds(0, 2), :, rows] = (
            own[kind, pl.ds(0, 2), :, rows].astype(F32) + z1[kind, :, :, rows].astype(F32)
        ).astype(BF)
        z_low[j] = start_out(2, j, own.at[kind, 1, :, rows], z2.at[kind, :, rows])

    def out_y(j):
        kind, rows = j % 2, rows_at(j)
        z_low[j].wait_recv()
        own[kind, 0, :, rows] = (
            own[kind, 0, :, rows].astype(F32) + z2[kind, :, rows].astype(F32)
        ).astype(BF)
        over_y[j] = start_out(3, j, own.at[kind, 0, 1, rows], y1.at[kind, rows])

    def out_end(j):
        kind, rows = j % 2, rows_at(j)
        over_y[j].wait_recv()
        out_o[rows, pl.ds(kind * 512, 512)] = own[kind, 0, 0, rows].astype(F32) + y1[
            kind, rows
        ].astype(F32)

    def product(low, mid, high):
        source = dp_source(here, low, mid, high, 0)
        cols = pl.ds(pl.multiple_of(source * 1024, 1024), 1024)
        block = jnp.dot(cot[...], normed[:, cols], preferred_element_type=F32) * factor
        block = block.astype(BF)
        for c in range(8):
            place = low + 2 * mid + 4 * high if c % 2 == 0 else high + 2 * mid + 4 * low
            part[c, place] = block[:, c * 128 : (c + 1) * 128]

    def start(stage, c, src, dst):
        at = stage * 8 + c
        return keep(send(src, dst, sent.at[at], got.at[at], here, STAGES[c % 2][2 - stage]))

    def start_first(c):
        return start(0, c, part.at[c, pl.ds(4, 4)], r1.at[c])

    product(1, 0, 1)
    product(1, 1, 1)
    product(0, 0, 1)
    product(0, 1, 1)
    one = {c: start_first(c) for c in (0, 2, 4, 6)}
    load_own.wait()
    out_high(0)
    product(1, 0, 0)
    product(1, 1, 0)
    one.update({c: start_first(c) for c in (1, 3, 5, 7)})
    out_high(1)
    product(0, 0, 0)
    product(0, 1, 0)

    def added(c, n, ref):
        part[c, pl.ds(0, n)] = (
            part[c, pl.ds(0, n)].astype(F32) + ref[c].astype(F32)
        ).astype(BF)

    two, three = {}, {}

    def q_two(c):
        one[c].wait_recv()
        added(c, 4, r1)
        two[c] = start(1, c, part.at[c, pl.ds(2, 2)], r2.at[c])

    def q_three(c):
        two[c].wait_recv()
        added(c, 2, r2)
        three[c] = start(2, c, part.at[c, pl.ds(1, 1)], r3.at[c])

    def q_end(c):
        three[c].wait_recv()
        total = part[c, 0].astype(F32) + r3[c, 0].astype(F32)
        out_q[pl.ds(c * 128, 128), :] = total.T

    lagged = (
        (q_two, 0), (out_high, -2), (q_three, 1), (out_low, 0),
        (q_end, 2), (out_y, 1), (out_end, 2),
    )
    for n in range(-2, 8 + 3):
        for action, lag in lagged:
            j = n - lag
            if action is out_high and j < 2:
                continue
            if n >= 0 and 0 <= j < 8:
                action(j)
    for copy in copies:
        copy.wait_send()


def grads(normed, cot_rows, partials, factor):
    shape = jax.ShapeDtypeStruct
    return pl.pallas_call(
        functools.partial(grads_kernel, factor),
        out_shape=(shape((1024, 256), F32), shape((256, 1024), F32)),
        in_specs=vmem_specs(2) + any_specs(1),
        out_specs=tuple(vmem_specs(2)),
        scratch_shapes=[
            pltpu.VMEM((8, 8, 256, 128), BF),
            pltpu.VMEM((8, 4, 256, 128), BF),
            pltpu.VMEM((8, 2, 256, 128), BF),
            pltpu.VMEM((8, 1, 256, 128), BF),
            pltpu.VMEM((2, 4, 2, 256, 512), BF),
            pltpu.VMEM((2, 4, 2, 256, 512), BF),
            pltpu.VMEM((2, 2, 2, 256, 512), BF),
            pltpu.VMEM((2, 2, 256, 512), BF),
            pltpu.VMEM((2, 256, 512), BF),
            pltpu.SemaphoreType.DMA((1,)),
            pltpu.SemaphoreType.DMA((56,)),
            pltpu.SemaphoreType.DMA((56,)),
        ],
        compiler_params=pltpu.CompilerParams(
            collective_id=1, has_side_effects=True, vmem_limit_bytes=VMEM_BYTES
        ),
        name="grads",
    )(normed, cot_rows, partials)


def sum_over(here, slots_dp, slots_tensor, staged, sent, got, at):
    dp = here[0] * 2 + here[1]
    tensor = here[2] * 4 + here[3] * 2 + here[4]

    def exchange(slots, own, peers, base):
        copies = []
        for n, masks in enumerate(peers):
            ref = slots.at[own]
            copies.append(send(ref, ref, sent.at[base + n], got.at[base + n], here, masks))
        return copies

    one = exchange(slots_dp, dp, DP_PEERS, at)
    for copy in one:
        copy.wait_recv()
    total = slots_dp[0]
    for n in range(1, 8):
        total = total + slots_dp[n]
    slots_tensor[tensor] = total
    two = exchange(slots_tensor, tensor, TENSOR_PEERS, at + 7)
    for copy in two:
        copy.wait_recv()
    total = slots_tensor[0]
    for n in range(1, 16):
        total = total + slots_tensor[n]
    for copy in one + two:
        copy.wait_send()
    return total


def clean_kernel(
    count, gq, go, vq, vo, gram, next_q, next_o, coeffs,
    cq, co, s1, s2, u1, u2, sent, got,
):
    here = position()
    dp = here[0] * 2 + here[1]
    greet(here, DP_PEERS + TENSOR_PEERS)

    def over_tiles(visit, carry):
        def step_q(r, state):
            rows = pl.ds(pl.multiple_of(r * 16, 16), 16)
            for h in range(2):
                state = visit(gq, vq, cq, rows, pl.ds(h * 128, 128), state)
            return state

        def step_o(r, state):
            rows = pl.ds(pl.multiple_of(r * 16, 16), 16)
            for h in range(8):
                state = visit(go, vo, co, rows, pl.ds(h * 128, 128), state)
            return state

        carry = lax.fori_loop(0, 64, step_q, carry)
        return lax.fori_loop(0, 16, step_o, carry)

    def against_basis(g, v, c, rows, cols, state):
        here_g = g[rows, cols]
        out = []
        for j in range(K):
            p = here_g * v[j, rows, cols].astype(F32)
            out.append(state[j] + (p[:8] + p[8:]))
        return tuple(out)

    zero = jnp.zeros((8, 128), F32)
    firsts = over_tiles(against_basis, (zero,) * K)
    s1[dp, pl.ds(0, 64)] = gram[...]
    for j in range(K):
        s1[dp, pl.ds(64 + j, 1)] = jnp.sum(firsts[j], axis=0, keepdims=True)
    total = sum_over(here, s1, s2, None, sent, got, 0)
    lines = jnp.sum(total, axis=1, keepdims=True) / count
    first = lines[64:72]
    second = first
    for i in range(K):
        second = second - lines[8 * i : 8 * i + 8] * first[i : i + 1]
    both = first + second
    weights = [jnp.broadcast_to(both[j : j + 1], (16, 128)) for j in range(K)]

    def cleaned(g, v, c, rows, cols, state):
        value = g[rows, cols]
        for j in range(K):
            value = value - weights[j] * v[j, rows, cols].astype(F32)
        c[rows, cols] = value
        p = value * value
        return state + (p[:8] + p[8:])

    u1[dp] = over_tiles(cleaned, zero)
    squares = sum_over(here, u1, u2, None, sent, got, 22)
    squares = jnp.sum(jnp.sum(squares, axis=1, keepdims=True), axis=0, keepdims=True) / count
    beta = jnp.sqrt(squares + BETA_EPS)
    next_q[...] = (cq[...] / beta).astype(BF)
    next_o[...] = (co[...] / beta).astype(BF)
    coeffs[pl.ds(0, 8)] = jnp.broadcast_to(both, (8, 128))
    coeffs[pl.ds(8, 8)] = jnp.broadcast_to(beta, (8, 128))


def clean(gn_query, gn_output, basis_query, basis_output, gram, count):
    shape = jax.ShapeDtypeStruct
    return pl.pallas_call(
        functools.partial(clean_kernel, count),
        out_shape=(shape((1024, 256), BF), shape((256, 1024), BF), shape((16, 128), F32)),
        in_specs=vmem_specs(5),
        out_specs=tuple(vmem_specs(3)),
        scratch_shapes=[
            pltpu.VMEM((1024, 256), F32),
            pltpu.VMEM((256, 1024), F32),
            pltpu.VMEM((8, 72, 128), F32),
            pltpu.VMEM((16, 72, 128), F32),
            pltpu.VMEM((8, 8, 128), F32),
            pltpu.VMEM((16, 8, 128), F32),
            pltpu.SemaphoreType.DMA((44,)),
            pltpu.SemaphoreType.DMA((44,)),
        ],
        compiler_params=pltpu.CompilerParams(
            collective_id=2, has_side_effects=True, vmem_limit_bytes=VMEM_BYTES
        ),
        name="clean",
    )(gn_query, gn_output, basis_query, basis_output, gram)


def body(tokens, segments, norm_gain, q_weight, kv_weight, o_weight, basis_query, basis_output):
    groups = lax.axis_size(DP)
    seq_count, length, model_width = tokens.shape
    row_count = seq_count * length
    col_count = q_weight.shape[1]
    heads_dev = col_count // HD
    group_size = QH // KVH
    qwidth = QH * HD
    query_scale = D ** (-0.5)
    output_scale = qwidth ** (-0.5)
    gn_scale = qwidth / (row_count * groups)
    param_count = 2.0 * D * qwidth
    query, tangent, key_states, values, normed, gram, wall = project(
        tokens.reshape(row_count, model_width),
        norm_gain.reshape(1, model_width),
        q_weight,
        basis_query,
        kv_weight,
        basis_output,
        o_weight,
    )
    allowed = allowed_pairs(segments)
    query_wide = query.astype(jnp.float32).reshape(seq_count, length, heads_dev, HD)
    tangent_wide = tangent.astype(jnp.float32).reshape(seq_count, length, heads_dev, HD)
    key_wide = key_states.astype(jnp.float32).reshape(seq_count, length, HD)
    value_wide = values.astype(jnp.float32).reshape(seq_count, length, HD)

    def attend_here(moving):
        return attend(moving, key_wide, value_wide, allowed)

    heads_out, tangent_heads = jax.jvp(attend_here, (query_wide,), (tangent_wide,))
    heads_out = heads_out.reshape(row_count, col_count).astype(jnp.bfloat16)
    tangent_heads = tangent_heads.reshape(row_count, col_count).astype(jnp.bfloat16)
    heads_out = heads_out * jnp.bfloat16(output_scale)
    both_heads = jnp.concatenate([heads_out, tangent_heads], axis=1)
    cot_heads, partials = output_side(both_heads.reshape(16, 2, 16, 2 * col_count), wall)
    cot_heads = cot_heads.astype(jnp.float32)
    _, pullback = jax.vjp(attend_here, query_wide)
    cot_query = pullback(cot_heads.reshape(seq_count, length, heads_dev, HD))[0]
    cot_query = cot_query.reshape(row_count, col_count).astype(jnp.bfloat16)
    gn_query, gn_output = grads(normed, cot_query.T, partials, gn_scale * query_scale)
    next_query, next_output, lines = clean(
        gn_query, gn_output, basis_query, basis_output, gram, param_count
    )
    return (next_query, next_output, lines[:9, 0])


def solution(mesh):
    finer = Mesh(
        mesh.devices.reshape(4, 2, 4, 2, 2), ("dp_0", "dp_1", "tensor_0", "tensor_1", "tensor_2")
    )
    placed = (
        P(DP, None, None),
        P(DP, None),
        P(),
        P(DP, TENSOR),
        P(None, DP, None),
        P(TENSOR, DP),
        P(None, DP, TENSOR),
        P(None, TENSOR, DP),
    )
    return jax.shard_map(
        body,
        mesh=finer,
        in_specs=placed,
        out_specs=(P(DP, TENSOR), P(TENSOR, DP), P()),
        check_vma=False,
    )
```

```python
import functools
import math

import jax
import jax.numpy as jnp
from jax import lax
from jax.experimental import pallas as pl
from jax.experimental.pallas import tpu as pltpu
from jax.sharding import Mesh
from jax.sharding import PartitionSpec as P

D = 8192
HD = 128
QH = 32
KVH = 4
K = 8
DP = ("dp_0", "dp_1")
TENSOR = ("tensor_0", "tensor_1", "tensor_2")
DP_TENSOR = ("dp_0", "dp_1", "tensor_0", "tensor_1", "tensor_2")


PRECISE = lax.Precision.HIGHEST
ROPE_BASE = 500000.0
NORM_EPS = 1e-05
BETA_EPS = 1e-06


MESH = pl.DeviceIdType.MESH
VMEM_BYTES = 58 * 1024 * 1024
X1, X3, X2, YH = (1, 0, 0, 0, 0), (3, 0, 0, 0, 0), (2, 0, 0, 0, 0), (0, 1, 0, 0, 0)
Z1, Z3, YL, CORE = (0, 0, 1, 0, 0), (0, 0, 3, 0, 0), (0, 0, 0, 1, 0), (0, 0, 0, 0, 1)
BF = jnp.bfloat16
F32 = jnp.float32


def position():
    return [lax.axis_index(a) for a in DP_TENSOR]


def flipped(value, mask):
    if mask == 0:
        return value
    if mask == 1:
        return value + 1 - 2 * lax.rem(value, 2)
    if mask == 2:
        return lax.rem(value + 2, 4)
    return 3 - value


def peer(here, masks):
    return tuple(flipped(v, m) for v, m in zip(here, masks))


def greet(here, peers):
    barrier = pltpu.get_barrier_semaphore()
    for masks in peers:
        pl.semaphore_signal(barrier, inc=1, device_id=peer(here, masks), device_id_type=MESH)
    pl.semaphore_wait(barrier, len(peers))


def send(src, dst, send_sem, recv_sem, here, masks):
    copy = pltpu.make_async_remote_copy(
        src_ref=src,
        dst_ref=dst,
        send_sem=send_sem,
        recv_sem=recv_sem,
        device_id=peer(here, masks),
        device_id_type=MESH,
    )
    copy.start()
    return copy


def dp_source(here, bits, stages):
    x, yh = here[0], here[1]
    for bit, masks in zip(bits, stages):
        if masks[0] == 1:
            x = x + bit * (1 - 2 * lax.rem(x, 2))
        elif masks[0] == 3:
            x = x + bit * (3 - 2 * x)
        else:
            yh = yh + bit * (1 - 2 * yh)
    return x * 2 + yh


STAGES = ((X1, YH, X3), (X3, YH, X1))
IN_STAGES = ((X1, YH, X3), (X3, YH, X1), (X1, YH, X3), (X3, YH, X1))
OUT_STAGES = ((YL, Z1, Z3), (YL, Z3, Z1))


DP_PEERS = [(x, yh, 0, 0, 0) for x in range(4) for yh in range(2) if x or yh]
TENSOR_PEERS = [(0, 0, z, yl, c) for z in range(4) for yl in range(2) for c in range(2) if z or yl or c]


def z_place(mask, kind):
    one, three = {0: (0, 0), 1: (1, 0), 3: (0, 1), 2: (1, 1)}[mask]
    return one + 2 * three if kind == 0 else three + 2 * one


def out_place(r, kind):
    mz, ml = r // 2, r % 2
    return ml + 2 * z_place(mz, kind)


def same_core_masks(r):
    return (0, 0, r // 2, r % 2, 0)


def rope_tables(length, head_width):
    half_width = head_width // 2
    frequency = jnp.exp(
        jnp.arange(half_width, dtype=jnp.float32) * (-2.0 * math.log(ROPE_BASE) / head_width)
    )
    angles = jnp.arange(length, dtype=jnp.float32)[:, None] * frequency[None, :]
    return (jnp.cos(angles), jnp.sin(angles))


def rotate(vectors, cosine_table, sine_table):
    half_width = vectors.shape[-1] // 2
    front_half = vectors[..., :half_width]
    back_half = vectors[..., half_width:]
    return jnp.concatenate(
        [
            front_half * cosine_table - back_half * sine_table,
            front_half * sine_table + back_half * cosine_table,
        ],
        axis=-1,
    )


def attend(query, key_states, values, allowed):
    length = query.shape[1]
    head_width = query.shape[-1]
    cosine_table, sine_table = rope_tables(length, head_width)
    query = rotate(query, cosine_table[:, None, :], sine_table[:, None, :])
    key_states = rotate(key_states, cosine_table, sine_table)
    scores = jnp.einsum("slgd,smd->sglm", query, key_states, precision=PRECISE) * head_width ** (
        -0.5
    )
    scores = jnp.where(allowed[:, None, :, :], scores, -1e30)
    row_max = lax.stop_gradient(jnp.max(scores, axis=-1, keepdims=True))
    weights = jnp.exp(scores - row_max)
    probabilities = weights / jnp.sum(weights, axis=-1, keepdims=True)
    return jnp.einsum("sglm,smd->slgd", probabilities, values, precision=PRECISE)


def allowed_pairs(segments):
    length = segments.shape[1]
    position = jnp.arange(length, dtype=jnp.int32)
    causal = position[:, None] >= position[None, :]
    return jnp.logical_and(segments[:, :, None] == segments[:, None, :], causal[None])


SUPER = (0, 1) * 4 + (2, 3) * 4
PIECE = (0, 0, 1, 1, 2, 2, 3, 3) * 2


def project_kernel(
    count, tok, gain, q_w, vec_q, kv_w, vec_o, o_w,
    q_out, t_out, k_out, v_out, normed_out, gram_out, wall,
    x, buf, acc, mine, theirs, vq, vo, w, g1, g2, load, sent, got,
):
    here = position()
    core = here[4]
    kv_head = here[2]
    for_rows = []
    for s in range(4):
        rows = pl.ds(s * 256, 256)
        kv_cols = pl.ds(pl.multiple_of(kv_head * HD, HD), HD)
        parts = (
            (q_w.at[rows], buf.at[s, 0, :, pl.ds(0, 256)]),
            (vec_q.at[K - 1, rows], buf.at[s, 0, :, pl.ds(256, 256)]),
            (kv_w.at[core, rows, kv_cols], buf.at[s, 0, :, pl.ds(512, 128)]),
        )
        for n, (src, dst) in enumerate(parts):
            copy = pltpu.make_async_copy(src, dst, load.at[3 * s + n])
            copy.start()
            for_rows.append(copy)
    own_out = []
    for kind, src in enumerate((vec_o.at[K - 1], o_w)):
        copy = pltpu.make_async_copy(src, w.at[kind, 0], load.at[16 + kind])
        copy.start()
        own_out.append(copy)
    greet(here, DP_PEERS + TENSOR_PEERS)
    for copy in for_rows:
        copy.wait()

    def start_stage(stage, k):
        s, rows = SUPER[k], pl.ds(PIECE[k] * 64, 64)
        n = 1 << stage
        at = stage * 16 + k
        return send(
            buf.at[s, pl.ds(0, n), rows],
            buf.at[s, pl.ds(n, n), rows],
            sent.at[at],
            got.at[at],
            here,
            IN_STAGES[s][stage],
        )

    out_copies = {}

    def start_out(stage, kind, piece):
        n = 1 << stage
        rows = pl.ds(piece * 64, 64)
        at = 49 + stage * 8 + kind * 4 + piece
        out_copies[stage, kind, piece] = send(
            w.at[kind, pl.ds(0, n), rows],
            w.at[kind, pl.ds(n, n), rows],
            sent.at[at],
            got.at[at],
            here,
            OUT_STAGES[kind][stage],
        )

    def next_out(stage, piece):
        for kind in range(2):
            out_copies[stage, kind, piece].wait_recv()
            start_out(stage + 1, kind, piece)

    for copy in own_out:
        copy.wait()
    for kind in range(2):
        start_out(0, kind, 0)
    first = [start_stage(0, k) for k in range(16)]
    tok_copy = pltpu.make_async_copy(tok, x, load.at[12])
    tok_copy.start()
    vq_copy = pltpu.make_async_copy(vec_q, vq, load.at[13])
    vq_copy.start()
    vo_copy = pltpu.make_async_copy(vec_o, vo, load.at[14])
    vo_copy.start()
    wall_copies = []

    def keep_wall(kind, lo):
        copy = pltpu.make_async_copy(
            w.at[kind, pl.ds(lo, 4)], wall.at[kind, pl.ds(lo, 4)], load.at[18 + kind + lo // 2]
        )
        copy.start()
        wall_copies.append(copy)

    dp = here[0] * 2 + here[1]
    tensor = here[2] * 4 + here[3] * 2 + here[4]

    def exchange(slots, own, peers, base):
        ref = slots.at[own]
        return [
            send(ref, ref, sent.at[base + n], got.at[base + n], here, masks)
            for n, masks in enumerate(peers)
        ]

    def norm_rows(lo, hi):
        def step(i, carry):
            rows = pl.ds(pl.multiple_of(i * 16, 16), 16)
            total = jnp.zeros((16, 1), F32)
            for c in range(8):
                part = x[rows, pl.ds(c * 1024, 1024)].astype(F32)
                total += jnp.sum(part * part, axis=1, keepdims=True)
            inv = lax.rsqrt(total / D + NORM_EPS)
            for c in range(8):
                cols = pl.ds(c * 1024, 1024)
                x[rows, cols] = (x[rows, cols].astype(F32) * inv * gain[:, cols]).astype(BF)
            return carry

        lax.fori_loop(lo // 16, hi // 16, step, 0)

    def dots(s, lo, hi):
        def step(p, carry):
            bits = (lax.rem(p, 2), lax.rem(p // 2, 2), p // 4)
            source = dp_source(here, bits, IN_STAGES[s])
            cols = pl.ds(pl.multiple_of(source * 1024 + s * 256, 256), 256)
            acc[...] += jnp.dot(x[:, cols], buf[s, p], preferred_element_type=F32)
            return carry

        lax.fori_loop(lo, hi, step, 0)

    def gram():
        pairs = [(i, j) for i in range(K) for j in range(i, K)]

        def tile(ref, rows, cols, carry):
            b = [ref[j, rows, cols].astype(F32) for j in range(K)]
            out = []
            for (i, j), a in zip(pairs, carry):
                p = b[i] * b[j]
                out.append(a + (p[:8] + p[8:]))
            return tuple(out)

        def step_q(r, carry):
            rows = pl.ds(pl.multiple_of(r * 16, 16), 16)
            for h in range(2):
                carry = tile(vq, rows, pl.ds(h * 128, 128), carry)
            return carry

        def step_o(r, carry):
            rows = pl.ds(pl.multiple_of(r * 16, 16), 16)
            for h in range(8):
                carry = tile(vo, rows, pl.ds(h * 128, 128), carry)
            return carry

        carry = tuple(jnp.zeros((8, 128), F32) for _ in pairs)
        carry = lax.fori_loop(0, 64, step_q, carry)
        carry = lax.fori_loop(0, 16, step_o, carry)
        lane = lax.broadcasted_iota(jnp.int32, (8, 128), 1)
        row = lax.broadcasted_iota(jnp.int32, (8, 128), 0)
        tile_sum = jnp.zeros((8, 128), F32)
        for (i, j), a in zip(pairs, carry):
            value = jnp.sum(jnp.sum(a, axis=0, keepdims=True), axis=1, keepdims=True)
            hit = jnp.logical_or(
                jnp.logical_and(lane == i, row == j), jnp.logical_and(lane == j, row == i)
            )
            tile_sum = tile_sum + jnp.where(hit, value, 0.0)
        g1[dp] = tile_sum

    acc[...] = jnp.zeros_like(acc)
    second, third = [], []
    out_steps = {
        1: (0, 0), 2: (0, 1), 4: (0, 2), 6: (0, 3), 3: (1, 0), 5: (1, 1), 7: (1, 2), 9: (1, 3)
    }
    for k in range(16):
        first[k].wait_recv()
        second.append(start_stage(1, k))
        if k >= 1:
            second[k - 1].wait_recv()
            third.append(start_stage(2, k - 1))
        if k in out_steps:
            stage, piece = out_steps[k]
            next_out(stage, piece)
        if k in (0, 2, 4):
            start_out(0, 0, k // 2 + 1)
            start_out(0, 1, k // 2 + 1)
        if k == 0:
            tok_copy.wait()
            norm_rows(0, 256)
        if k == 1:
            norm_rows(256, 512)
            out_copy = pltpu.make_async_copy(x, normed_out, load.at[15])
            out_copy.start()
        if k == 2:
            vq_copy.wait()
            vo_copy.wait()
            gram()
            over_dp = exchange(g1, dp, DP_PEERS, 73)
        if k == 8:
            dots(0, 0, 4)
        if k == 9:
            dots(1, 0, 4)
        if k == 10:
            keep_wall(0, 0)
            keep_wall(1, 0)
            for copy in over_dp:
                copy.wait_recv()
            total = g1[0]
            for n in range(1, 8):
                total = total + g1[n]
            g2[tensor] = total
            over_tensor = exchange(g2, tensor, TENSOR_PEERS, 80)
        if k == 13:
            for n in (0, 2, 4, 6):
                third[n].wait_recv()
            dots(0, 4, 8)
        if k == 14:
            for n in (1, 3, 5, 7):
                third[n].wait_recv()
            dots(1, 4, 8)
        if k == 15:
            dots(2, 0, 4)
    second[15].wait_recv()
    third.append(start_stage(2, 15))
    dots(3, 0, 4)
    for s in (2, 3):
        for n in range(8, 16):
            if SUPER[n] == s:
                third[n].wait_recv()
        dots(s, 4, 8)
    mine[...] = acc[:, pl.ds(512, 128)].astype(BF)
    swap = send(mine, theirs, sent.at[48], got.at[48], here, CORE)
    q_out[...] = acc[:, pl.ds(0, 256)].astype(BF)
    t_out[...] = (acc[:, pl.ds(256, 256)] * (D ** (-0.5))).astype(BF)
    swap.wait()
    own = mine[...].astype(F32)
    other = theirs[...].astype(F32)
    first_core = core == 0
    k_out[...] = jnp.where(first_core, own, other).astype(BF)
    v_out[...] = jnp.where(first_core, other, own).astype(BF)
    for kind in range(2):
        for piece in range(4):
            out_copies[2, kind, piece].wait_recv()
        keep_wall(kind, 4)
    for copy in over_tensor:
        copy.wait_recv()
    total = g2[0]
    for n in range(1, 16):
        total = total + g2[n]
    gram_out[...] = total / count
    for copy in first + second + third + list(out_copies.values()) + over_dp + over_tensor:
        copy.wait_send()
    for copy in wall_copies:
        copy.wait()
    out_copy.wait()


def any_specs(n):
    return [pl.BlockSpec(memory_space=pl.ANY) for _ in range(n)]


def vmem_specs(n):
    return [pl.BlockSpec(memory_space=pltpu.VMEM) for _ in range(n)]


def project(tokens, norm_gain, q_weight, basis_query, kv_weight, basis_output, o_weight, count):
    shape = jax.ShapeDtypeStruct
    return pl.pallas_call(
        functools.partial(project_kernel, count),
        out_shape=(
            shape((512, 256), BF),
            shape((512, 256), BF),
            shape((512, HD), BF),
            shape((512, HD), BF),
            shape((512, D), BF),
            shape((8, 128), F32),
            shape((2, 8, 256, 1024), BF),
        ),
        in_specs=any_specs(1) + vmem_specs(1) + any_specs(5),
        out_specs=tuple(vmem_specs(4) + any_specs(1) + vmem_specs(1) + any_specs(1)),
        scratch_shapes=[
            pltpu.VMEM((512, D), BF),
            pltpu.VMEM((4, 8, 256, 640), BF),
            pltpu.VMEM((512, 640), F32),
            pltpu.VMEM((512, HD), BF),
            pltpu.VMEM((512, HD), BF),
            pltpu.VMEM((K, 1024, 256), BF),
            pltpu.VMEM((K, 256, 1024), BF),
            pltpu.VMEM((2, 8, 256, 1024), BF),
            pltpu.VMEM((8, 8, 128), F32),
            pltpu.VMEM((16, 8, 128), F32),
            pltpu.SemaphoreType.DMA((22,)),
            pltpu.SemaphoreType.DMA((95,)),
            pltpu.SemaphoreType.DMA((95,)),
        ],
        compiler_params=pltpu.CompilerParams(
            collective_id=0, has_side_effects=True, vmem_limit_bytes=VMEM_BYTES
        ),
        name="project",
    )(tokens, norm_gain, q_weight, basis_query, kv_weight, basis_output, o_weight)


def output_kernel(
    h, wall, cot, gp_out,
    w, g, acc, tb, mine, theirs, cs, c1, c2, c3, gp, load, sent, got,
):
    here = position()
    place = here[2] * 2 + here[3]
    loads = []
    for kind in (0, 1):
        copy = pltpu.make_async_copy(wall.at[kind], w.at[kind], load.at[kind])
        copy.start()
        loads.append(copy)
    greet(here, [X1, X3, YH, CORE] + [same_core_masks(r) for r in range(1, 8)])
    copies = []

    def start(at, src, dst, masks):
        copy = send(src, dst, sent.at[at], got.at[at], here, masks)
        copies.append(copy)
        return copy

    def index_of(r):
        z, yl = peer(here[2:4], same_core_masks(r)[2:4])
        return z * 2 + yl

    spread = {
        r: start(r, h.at[index_of(r)], g.at[:, r, 0], same_core_masks(r)) for r in range(1, 8)
    }
    g[:, 0, 0] = h[place]

    def gather(stage, rg, kind):
        n = 1 << stage
        group = pl.ds(rg * 2, 2)
        return start(
            8 + stage * 8 + rg * 2 + kind,
            g.at[kind, group, pl.ds(0, n)],
            g.at[kind, group, pl.ds(n, n)],
            STAGES[kind][stage],
        )

    one, two, three = {}, {}, {}
    for rg in range(4):
        for r in (rg * 2, rg * 2 + 1):
            if r:
                spread[r].wait_recv()
        for kind in range(2):
            one[rg, kind] = gather(0, rg, kind)
    order = [(rg, kind) for rg in range(4) for kind in range(2)]
    for n, key in enumerate(order):
        one[key].wait_recv()
        two[key] = gather(1, *key)
        if n >= 1:
            two[order[n - 1]].wait_recv()
            three[order[n - 1]] = gather(2, *order[n - 1])
    two[order[7]].wait_recv()
    three[order[7]] = gather(2, *order[7])

    def rows_of(r, cols):
        parts = [g[kind, r, :, :, cols].reshape(256, 256) for kind in range(2)]
        return jnp.concatenate(parts, axis=0)

    for copy in loads:
        copy.wait()
    acc[...] = jnp.zeros_like(acc)
    for rg in range(4):
        three[rg, 0].wait_recv()
        three[rg, 1].wait_recv()
        for r in (rg * 2, rg * 2 + 1):
            acc[...] += jnp.dot(
                rows_of(r, pl.ds(0, 256)), w[0, out_place(r, 0)], preferred_element_type=F32
            ) + jnp.dot(
                rows_of(r, pl.ds(256, 256)), w[1, out_place(r, 1)], preferred_element_type=F32
            )
    swaps = []
    for half in range(2):
        rows = pl.ds(half * 256, 256)
        mine[rows] = acc[rows].astype(BF)
        swaps.append(start(56 + half, mine.at[rows], theirs.at[rows], CORE))
    for half in range(2):
        rows = pl.ds(half * 256, 256)
        swaps[half].wait_recv()
        tb[rows] = (mine[rows].astype(F32) + theirs[rows].astype(F32)).astype(BF)

    def scatter(stage, key, src, dst):
        rg, kind = key
        return start(32 + stage * 8 + rg * 2 + kind, src, dst, STAGES[kind][2 - stage])

    one, two, three = {}, {}, {}
    for rg in range(4):
        group = pl.ds(rg * 2, 2)
        for r in (rg * 2, rg * 2 + 1):
            part = lax.dot_general(
                tb[...],
                w[1, out_place(r, 1)],
                (((1,), (1,)), ((), ())),
                preferred_element_type=F32,
            ).astype(BF)
            for kind in range(2):
                cs[kind, r] = part[kind * 256 : kind * 256 + 256].reshape(8, 32, 256)
        for kind in range(2):
            one[rg, kind] = scatter(
                0, (rg, kind), cs.at[kind, group, pl.ds(4, 4)], c1.at[kind, group]
            )

    def added(key, n, ref):
        rg, kind = key
        group = pl.ds(rg * 2, 2)
        cs[kind, group, pl.ds(0, n)] = (
            cs[kind, group, pl.ds(0, n)].astype(F32) + ref[kind, group].astype(F32)
        ).astype(BF)

    def output_grad(r):
        mz, ml = r // 2, r % 2
        block = lax.dot_general(
            rows_of(r, pl.ds(0, 256)),
            tb[...],
            (((0,), (0,)), ((), ())),
            preferred_element_type=F32,
        ).astype(BF)
        for kind in range(2):
            gp[kind, z_place(mz, kind), ml] = block[:, kind * 512 : kind * 512 + 512]

    def second(key):
        rg, kind = key
        one[key].wait_recv()
        added(key, 4, c1)
        group = pl.ds(rg * 2, 2)
        two[key] = scatter(1, key, cs.at[kind, group, pl.ds(2, 2)], c2.at[kind, group])

    def third(key):
        rg, kind = key
        two[key].wait_recv()
        added(key, 2, c2)
        group = pl.ds(rg * 2, 2)
        three[key] = scatter(2, key, cs.at[kind, group, pl.ds(1, 1)], c3.at[kind, group])

    for n, key in enumerate(order):
        second(key)
        if n >= 1:
            third(order[n - 1])
        output_grad(n)
    third(order[7])
    back = {}
    for rg in range(4):
        for kind in range(2):
            three[rg, kind].wait_recv()
            added((rg, kind), 1, c3)
        for r in (rg * 2, rg * 2 + 1):
            if r:
                back[r] = start(r + 58, cs.at[:, r, 0], cot.at[place], same_core_masks(r))
    cot[place] = cs[:, 0, 0]
    gp_copy = pltpu.make_async_copy(gp, gp_out, load.at[2])
    gp_copy.start()
    for r in range(1, 8):
        back[r].wait_recv()
    for copy in copies:
        copy.wait_send()
    gp_copy.wait()


def output_side(heads, wall):
    shape = jax.ShapeDtypeStruct
    return pl.pallas_call(
        output_kernel,
        out_shape=(shape((8, 2, 32, 256), BF), shape((2, 4, 2, 256, 512), BF)),
        in_specs=vmem_specs(1) + any_specs(1),
        out_specs=tuple(vmem_specs(1) + any_specs(1)),
        scratch_shapes=[
            pltpu.VMEM((2, 8, 256, 1024), BF),
            pltpu.VMEM((2, 8, 8, 32, 512), BF),
            pltpu.VMEM((512, 1024), F32),
            pltpu.VMEM((512, 1024), BF),
            pltpu.VMEM((512, 1024), BF),
            pltpu.VMEM((512, 1024), BF),
            pltpu.VMEM((2, 8, 8, 32, 256), BF),
            pltpu.VMEM((2, 8, 4, 32, 256), BF),
            pltpu.VMEM((2, 8, 2, 32, 256), BF),
            pltpu.VMEM((2, 8, 1, 32, 256), BF),
            pltpu.VMEM((2, 4, 2, 256, 512), BF),
            pltpu.SemaphoreType.DMA((3,)),
            pltpu.SemaphoreType.DMA((66,)),
            pltpu.SemaphoreType.DMA((66,)),
        ],
        compiler_params=pltpu.CompilerParams(
            collective_id=3, has_side_effects=True, vmem_limit_bytes=VMEM_BYTES
        ),
        name="output_side",
    )(heads, wall)


def tail_kernel(
    factor, count, normed_hbm, cot, gp, gram, vec_q, vec_o, clean_q, clean_o, coeffs,
    normed, part, r1, r2, r3, own, z1, z2, y1, vq, vo, gq, go, facc,
    s1, s2, u1, u2, load, sent, got,
):
    here = position()
    dp = here[0] * 2 + here[1]
    tensor = here[2] * 4 + here[3] * 2 + here[4]
    loads = []

    def fetch(src, dst):
        copy = pltpu.make_async_copy(src, dst, load.at[len(loads)])
        copy.start()
        loads.append(copy)

    fetch(gp, own)
    fetch(normed_hbm, normed)
    greet(here, DP_PEERS + TENSOR_PEERS)
    copies = []

    def keep(copy):
        copies.append(copy)
        return copy

    def rows_at(j):
        return pl.ds(j // 2 * 64, 64)

    def start_out(stage, j, src, dst):
        at = 24 + stage * 8 + j
        masks = ((Z3, Z1)[j % 2], (Z1, Z3)[j % 2], YL)[stage]
        return keep(send(src, dst, sent.at[at], got.at[at], here, masks))

    z_high, z_low, over_y = {}, {}, {}

    def out_high(j):
        kind, rows = j % 2, rows_at(j)
        z_high[j] = start_out(0, j, own.at[kind, pl.ds(2, 2), :, rows], z1.at[kind, :, :, rows])

    def out_low(j):
        kind, rows = j % 2, rows_at(j)
        z_high[j].wait_recv()
        own[kind, pl.ds(0, 2), :, rows] = (
            own[kind, pl.ds(0, 2), :, rows].astype(F32) + z1[kind, :, :, rows].astype(F32)
        ).astype(BF)
        z_low[j] = start_out(1, j, own.at[kind, 1, :, rows], z2.at[kind, :, rows])

    def out_y(j):
        kind, rows = j % 2, rows_at(j)
        z_low[j].wait_recv()
        own[kind, 0, :, rows] = (
            own[kind, 0, :, rows].astype(F32) + z2[kind, :, rows].astype(F32)
        ).astype(BF)
        over_y[j] = start_out(2, j, own.at[kind, 0, 1, rows], y1.at[kind, rows])

    def against(g, v, row0, tiles, col0, col_tiles):
        def step(i, state):
            rows = pl.ds(pl.multiple_of(row0 + i * 16, 16), 16)
            for h in range(col_tiles):
                cols = pl.ds(col0 + h * 128, 128)
                here_g = g[rows, cols]
                out = []
                for j in range(K):
                    p = here_g * v[j, rows, cols].astype(F32)
                    out.append(state[j] + (p[:8] + p[8:]))
                state = tuple(out)
            return state

        state = lax.fori_loop(0, tiles, step, tuple(facc[j] for j in range(K)))
        for j in range(K):
            facc[j] = state[j]

    def out_end(j):
        kind, rows = j % 2, rows_at(j)
        over_y[j].wait_recv()
        go[rows, pl.ds(kind * 512, 512)] = own[kind, 0, 0, rows].astype(F32) + y1[
            kind, rows
        ].astype(F32)
        against(go, vo, j // 2 * 64, 4, kind * 512, 4)

    def product(low, mid, high):
        source = dp_source(here, (low, mid, high), STAGES[0])
        cols = pl.ds(pl.multiple_of(source * 1024, 1024), 1024)
        block = jnp.dot(cot[...], normed[:, cols], preferred_element_type=F32) * factor
        block = block.astype(BF)
        for c in range(8):
            place = low + 2 * mid + 4 * high if c % 2 == 0 else high + 2 * mid + 4 * low
            part[c, place] = block[:, c * 128 : (c + 1) * 128]

    def start(stage, c, src, dst):
        at = stage * 8 + c
        return keep(send(src, dst, sent.at[at], got.at[at], here, STAGES[c % 2][2 - stage]))

    one, two, three = {}, {}, {}

    def q_one(c):
        one[c] = start(0, c, part.at[c, pl.ds(4, 4)], r1.at[c])

    loads[0].wait()
    for j in range(8):
        out_high(j)
    loads[1].wait()
    fetch(vec_q, vq)
    fetch(vec_o, vo)
    product(1, 0, 1)
    product(1, 1, 1)
    product(0, 0, 1)
    product(0, 1, 1)
    for c in (0, 2, 4, 6):
        q_one(c)
    product(1, 0, 0)
    product(1, 1, 0)
    for c in (1, 3, 5, 7):
        q_one(c)
    product(0, 0, 0)
    product(0, 1, 0)
    facc[...] = jnp.zeros_like(facc)

    def added(c, n, ref):
        part[c, pl.ds(0, n)] = (
            part[c, pl.ds(0, n)].astype(F32) + ref[c].astype(F32)
        ).astype(BF)

    def q_two(c):
        one[c].wait_recv()
        added(c, 4, r1)
        two[c] = start(1, c, part.at[c, pl.ds(2, 2)], r2.at[c])

    def q_three(c):
        two[c].wait_recv()
        added(c, 2, r2)
        three[c] = start(2, c, part.at[c, pl.ds(1, 1)], r3.at[c])

    def q_end(c):
        three[c].wait_recv()
        total = part[c, 0].astype(F32) + r3[c, 0].astype(F32)
        gq[pl.ds(c * 128, 128), :] = total.T
        against(gq, vq, c * 128, 8, 0, 2)

    lagged = ((q_two, 0), (out_low, 0), (q_three, 1), (out_y, 1), (q_end, 2), (out_end, 2))
    for n in range(8 + 2):
        if n == 2:
            loads[2].wait()
            loads[3].wait()
        for action, lag in lagged:
            if 0 <= n - lag < 8:
                action(n - lag)

    def exchange(slots, own_slot, peers, base):
        ref = slots.at[own_slot]
        return [
            keep(send(ref, ref, sent.at[base + n], got.at[base + n], here, masks))
            for n, masks in enumerate(peers)
        ]

    def sum_over(over_dp, over_tensor, base):
        for copy in exchange(over_dp, dp, DP_PEERS, base):
            copy.wait_recv()
        total = over_dp[0]
        for n in range(1, 8):
            total = total + over_dp[n]
        over_tensor[tensor] = total
        for copy in exchange(over_tensor, tensor, TENSOR_PEERS, base + 7):
            copy.wait_recv()
        total = over_tensor[0]
        for n in range(1, 16):
            total = total + over_tensor[n]
        return total

    for j in range(K):
        s1[dp, pl.ds(j, 1)] = jnp.sum(facc[j], axis=0, keepdims=True)
    first = jnp.sum(sum_over(s1, s2, 48), axis=1, keepdims=True) / count
    second = first
    for i in range(K):
        second = second - gram[:, pl.ds(i, 1)] * first[i : i + 1]
    both = first + second
    weights = [jnp.broadcast_to(both[j : j + 1], (16, 128)) for j in range(K)]

    def cleaned(g, v, c, row_tiles, col_tiles, state):
        def step(r, state):
            rows = pl.ds(pl.multiple_of(r * 16, 16), 16)
            for h in range(col_tiles):
                cols = pl.ds(h * 128, 128)
                value = g[rows, cols]
                for j in range(K):
                    value = value - weights[j] * v[j, rows, cols].astype(F32)
                c[rows, cols] = value
                p = value * value
                state = state + (p[:8] + p[8:])
            return state

        return lax.fori_loop(0, row_tiles, step, state)

    state = cleaned(gq, vq, clean_q, 64, 2, jnp.zeros((8, 128), F32))
    u1[dp] = cleaned(go, vo, clean_o, 16, 8, state)
    squares = sum_over(u1, u2, 70)
    squares = jnp.sum(jnp.sum(squares, axis=1, keepdims=True), axis=0, keepdims=True) / count
    beta = jnp.sqrt(squares + BETA_EPS)
    coeffs[pl.ds(0, 8)] = jnp.broadcast_to(both, (8, 128))
    coeffs[pl.ds(8, 8)] = jnp.broadcast_to(beta, (8, 128))
    for copy in copies:
        copy.wait_send()


def tail(normed, cot_rows, partials, gram, basis_query, basis_output, factor, count):
    shape = jax.ShapeDtypeStruct
    return pl.pallas_call(
        functools.partial(tail_kernel, factor, count),
        out_shape=(shape((1024, 256), F32), shape((256, 1024), F32), shape((16, 128), F32)),
        in_specs=any_specs(1) + vmem_specs(1) + any_specs(1) + vmem_specs(1) + any_specs(2),
        out_specs=tuple(vmem_specs(3)),
        scratch_shapes=[
            pltpu.VMEM((512, D), BF),
            pltpu.VMEM((8, 8, 256, 128), BF),
            pltpu.VMEM((8, 4, 256, 128), BF),
            pltpu.VMEM((8, 2, 256, 128), BF),
            pltpu.VMEM((8, 1, 256, 128), BF),
            pltpu.VMEM((2, 4, 2, 256, 512), BF),
            pltpu.VMEM((2, 2, 2, 256, 512), BF),
            pltpu.VMEM((2, 2, 256, 512), BF),
            pltpu.VMEM((2, 256, 512), BF),
            pltpu.VMEM((K, 1024, 256), BF),
            pltpu.VMEM((K, 256, 1024), BF),
            pltpu.VMEM((1024, 256), F32),
            pltpu.VMEM((256, 1024), F32),
            pltpu.VMEM((K, 8, 128), F32),
            pltpu.VMEM((8, 8, 128), F32),
            pltpu.VMEM((16, 8, 128), F32),
            pltpu.VMEM((8, 8, 128), F32),
            pltpu.VMEM((16, 8, 128), F32),
            pltpu.SemaphoreType.DMA((4,)),
            pltpu.SemaphoreType.DMA((92,)),
            pltpu.SemaphoreType.DMA((92,)),
        ],
        compiler_params=pltpu.CompilerParams(
            collective_id=1, has_side_effects=True, vmem_limit_bytes=VMEM_BYTES
        ),
        name="tail",
    )(normed, cot_rows, partials, gram, basis_query, basis_output)


def body(tokens, segments, norm_gain, q_weight, kv_weight, o_weight, basis_query, basis_output):
    groups = lax.axis_size(DP)
    seq_count, length, model_width = tokens.shape
    row_count = seq_count * length
    col_count = q_weight.shape[1]
    heads_dev = col_count // HD
    group_size = QH // KVH
    qwidth = QH * HD
    query_scale = D ** (-0.5)
    output_scale = qwidth ** (-0.5)
    gn_scale = qwidth / (row_count * groups)
    param_count = 2.0 * D * qwidth
    query, tangent, key_states, values, normed, gram, wall = project(
        tokens.reshape(row_count, model_width),
        norm_gain.reshape(1, model_width),
        q_weight,
        basis_query,
        kv_weight,
        basis_output,
        o_weight,
        param_count,
    )
    allowed = allowed_pairs(segments)
    query_wide = query.astype(jnp.float32).reshape(seq_count, length, heads_dev, HD)
    tangent_wide = tangent.astype(jnp.float32).reshape(seq_count, length, heads_dev, HD)
    key_wide = key_states.astype(jnp.float32).reshape(seq_count, length, HD)
    value_wide = values.astype(jnp.float32).reshape(seq_count, length, HD)

    def attend_here(moving):
        return attend(moving, key_wide, value_wide, allowed)

    heads_out, tangent_heads = jax.jvp(attend_here, (query_wide,), (tangent_wide,))
    heads_out = heads_out.reshape(row_count, col_count).astype(jnp.bfloat16)
    tangent_heads = tangent_heads.reshape(row_count, col_count).astype(jnp.bfloat16)
    heads_out = heads_out * jnp.bfloat16(output_scale)
    both_heads = jnp.concatenate([heads_out, tangent_heads], axis=1)
    cot_heads, partials = output_side(both_heads.reshape(8, 2, 32, 2 * col_count), wall)
    cot_heads = cot_heads.astype(jnp.float32)
    _, pullback = jax.vjp(attend_here, query_wide)
    cot_query = pullback(cot_heads.reshape(seq_count, length, heads_dev, HD))[0]
    cot_query = cot_query.reshape(row_count, col_count).astype(jnp.bfloat16)
    clean_query, clean_output, lines = tail(
        normed,
        cot_query.T,
        partials,
        gram,
        basis_query,
        basis_output,
        gn_scale * query_scale,
        param_count,
    )
    beta = lines[8, 0]
    return (
        (clean_query / beta).astype(jnp.bfloat16),
        (clean_output / beta).astype(jnp.bfloat16),
        lines[:9, 0],
    )


def solution(mesh):
    finer = Mesh(
        mesh.devices.reshape(4, 2, 4, 2, 2), ("dp_0", "dp_1", "tensor_0", "tensor_1", "tensor_2")
    )
    placed = (
        P(DP, None, None),
        P(DP, None),
        P(),
        P(DP, TENSOR),
        P(None, DP, None),
        P(TENSOR, DP),
        P(None, DP, TENSOR),
        P(None, TENSOR, DP),
    )
    return jax.shard_map(
        body,
        mesh=finer,
        in_specs=placed,
        out_specs=(P(DP, TENSOR), P(TENSOR, DP), P()),
        check_vma=False,
    )
```

```python
import functools
import math

import jax
import jax.numpy as jnp
from jax import lax
from jax.experimental import pallas as pl
from jax.experimental.pallas import tpu as pltpu
from jax.sharding import Mesh
from jax.sharding import PartitionSpec as P

D = 8192
HD = 128
QH = 32
KVH = 4
K = 8
DP = ("dp_0", "dp_1")
TENSOR = ("tensor_0", "tensor_1", "tensor_2")
DP_TENSOR = ("dp_0", "dp_1", "tensor_0", "tensor_1", "tensor_2")


PRECISE = lax.Precision.HIGHEST
ROPE_BASE = 500000.0
NORM_EPS = 1e-05
BETA_EPS = 1e-06


MESH = pl.DeviceIdType.MESH
VMEM_BYTES = 58 * 1024 * 1024
X1, X3, X2, YH = (1, 0, 0, 0, 0), (3, 0, 0, 0, 0), (2, 0, 0, 0, 0), (0, 1, 0, 0, 0)
Z1, Z3, YL, CORE = (0, 0, 1, 0, 0), (0, 0, 3, 0, 0), (0, 0, 0, 1, 0), (0, 0, 0, 0, 1)
BF = jnp.bfloat16
F32 = jnp.float32


def position():
    return [lax.axis_index(a) for a in DP_TENSOR]


def flipped(value, mask):
    if mask == 0:
        return value
    if mask == 1:
        return value + 1 - 2 * lax.rem(value, 2)
    if mask == 2:
        return lax.rem(value + 2, 4)
    return 3 - value


def peer(here, masks):
    return tuple(flipped(v, m) for v, m in zip(here, masks))


def greet(here, peers):
    barrier = pltpu.get_barrier_semaphore()
    for masks in peers:
        pl.semaphore_signal(barrier, inc=1, device_id=peer(here, masks), device_id_type=MESH)


def greeted(peers):
    pl.semaphore_wait(pltpu.get_barrier_semaphore(), len(peers))


def send(src, dst, send_sem, recv_sem, here, masks):
    copy = pltpu.make_async_remote_copy(
        src_ref=src,
        dst_ref=dst,
        send_sem=send_sem,
        recv_sem=recv_sem,
        device_id=peer(here, masks),
        device_id_type=MESH,
    )
    copy.start()
    return copy


def dp_source(here, bits, stages):
    x, yh = here[0], here[1]
    for bit, masks in zip(bits, stages):
        if masks[0] == 1:
            x = x + bit * (1 - 2 * lax.rem(x, 2))
        elif masks[0] == 3:
            x = x + bit * (3 - 2 * x)
        else:
            yh = yh + bit * (1 - 2 * yh)
    return x * 2 + yh


STAGES = ((X1, YH, X3), (X3, YH, X1))
IN_STAGES = ((X1, YH, X3), (X3, YH, X1), (X1, YH, X3), (X3, YH, X1))
OUT_STAGES = ((YL, Z1, Z3), (YL, Z3, Z1))


XY_PEERS = [
    (x, yh, 0, yl, 0) for x in range(4) for yh in range(2) for yl in range(2) if x or yh or yl
]
ZC_PEERS = [(0, 0, z, 0, c) for z in range(4) for c in range(2) if z or c]


def z_place(mask, kind):
    one, three = {0: (0, 0), 1: (1, 0), 3: (0, 1), 2: (1, 1)}[mask]
    return one + 2 * three if kind == 0 else three + 2 * one


def out_place(r, kind):
    mz, ml = r // 2, r % 2
    return ml + 2 * z_place(mz, kind)


def same_core_masks(r):
    return (0, 0, r // 2, r % 2, 0)


def rope_tables(length, head_width):
    half_width = head_width // 2
    frequency = jnp.exp(
        jnp.arange(half_width, dtype=jnp.float32) * (-2.0 * math.log(ROPE_BASE) / head_width)
    )
    angles = jnp.arange(length, dtype=jnp.float32)[:, None] * frequency[None, :]
    return (jnp.cos(angles), jnp.sin(angles))


def rotated(vectors, cos_twice, sin_signed):
    return vectors * cos_twice + pltpu.roll(vectors, HD // 2, 1) * sin_signed


def rotated_back(vectors, cos_twice, sin_signed):
    return vectors * cos_twice - pltpu.roll(vectors, HD // 2, 1) * sin_signed


def dot_wide(a, b, a_dim, b_dim):
    return lax.dot_general(
        a, b, (((a_dim,), (b_dim,)), ((), ())), precision=PRECISE, preferred_element_type=F32
    )


def attend_both(q, t, k, v, allowed, cos_twice, sin_signed, h, probs):
    scale = HD ** (-0.5)
    for s in range(2):
        rows = pl.ds(s * 256, 256)
        keys = rotated(k[rows].astype(F32), cos_twice[...], sin_signed[...])
        values = v[rows].astype(F32)
        mask = allowed[s].astype(F32) > 0.5
        for head in range(2):
            cols = pl.ds(head * HD, HD)
            moving = rotated(q[rows, cols].astype(F32), cos_twice[...], sin_signed[...])
            along = rotated(t[rows, cols].astype(F32), cos_twice[...], sin_signed[...])
            scores = jnp.where(mask, dot_wide(moving, keys, 1, 1) * scale, -1e30)
            weights = jnp.exp(scores - jnp.max(scores, axis=1, keepdims=True))
            p = weights / jnp.sum(weights, axis=1, keepdims=True)
            probs[2 * s + head] = p
            slope = jnp.where(mask, dot_wide(along, keys, 1, 1) * scale, 0.0)
            dp = p * (slope - jnp.sum(p * slope, axis=1, keepdims=True))
            heads = dot_wide(p, values, 1, 0).astype(BF).astype(F32) * ((QH * HD) ** (-0.5))
            tangents = dot_wide(dp, values, 1, 0)
            h[pl.ds(4 * s, 4), :, :, cols] = heads.astype(BF).reshape(4, 2, 32, HD)
            h[pl.ds(4 * s, 4), :, :, pl.ds(256 + head * HD, HD)] = tangents.astype(BF).reshape(
                4, 2, 32, HD
            )


def attend_back(cot, k, v, probs, cos_twice, sin_signed, out):
    scale = HD ** (-0.5)
    for s in range(2):
        rows = pl.ds(s * 256, 256)
        keys = rotated(k[rows].astype(F32), cos_twice[...], sin_signed[...])
        values = v[rows].astype(F32)
        for head in range(2):
            cols = pl.ds(head * HD, HD)
            given = cot[pl.ds(4 * s, 4), :, :, cols].reshape(256, HD).astype(F32)
            p = probs[2 * s + head]
            slope = dot_wide(given, values, 1, 1)
            ds = p * (slope - jnp.sum(p * slope, axis=1, keepdims=True))
            moving = rotated_back(dot_wide(ds, keys, 1, 0) * scale, cos_twice[...], sin_signed[...])
            out[cols, rows] = moving.T.astype(BF)


def allowed_pairs(segments):
    length = segments.shape[1]
    position = jnp.arange(length, dtype=jnp.int32)
    causal = position[:, None] >= position[None, :]
    return jnp.logical_and(segments[:, :, None] == segments[:, None, :], causal[None])


SUPER = (0, 1) * 4 + (2, 3) * 4
PIECE = (0, 0, 1, 1, 2, 2, 3, 3) * 2


def project_kernel(
    count, tok, gain, q_w, vec_q, kv_w, vec_o, o_w,
    q_out, t_out, k_out, v_out, normed_out, gram_out, wall,
    x, buf, acc, mine, theirs, vq, vo, w, g1, g2, load, sent, got,
):
    here = position()
    core = here[4]
    kv_head = here[2]
    for_rows = []
    for s in range(4):
        rows = pl.ds(s * 256, 256)
        kv_cols = pl.ds(pl.multiple_of(kv_head * HD, HD), HD)
        parts = (
            (q_w.at[rows], buf.at[s, 0, :, pl.ds(0, 256)]),
            (vec_q.at[K - 1, rows], buf.at[s, 0, :, pl.ds(256, 256)]),
            (kv_w.at[core, rows, kv_cols], buf.at[s, 0, :, pl.ds(512, 128)]),
        )
        for n, (src, dst) in enumerate(parts):
            copy = pltpu.make_async_copy(src, dst, load.at[3 * s + n])
            copy.start()
            for_rows.append(copy)
    own_out = []
    for kind, src in enumerate((vec_o.at[K - 1], o_w)):
        copy = pltpu.make_async_copy(src, w.at[kind, 0], load.at[16 + kind])
        copy.start()
        own_out.append(copy)
    greet(here, XY_PEERS + ZC_PEERS)
    greeted(XY_PEERS + ZC_PEERS)
    for copy in for_rows:
        copy.wait()

    def start_stage(stage, k):
        s, rows = SUPER[k], pl.ds(PIECE[k] * 64, 64)
        n = 1 << stage
        at = stage * 16 + k
        return send(
            buf.at[s, pl.ds(0, n), rows],
            buf.at[s, pl.ds(n, n), rows],
            sent.at[at],
            got.at[at],
            here,
            IN_STAGES[s][stage],
        )

    out_copies = {}

    def start_out(stage, kind, piece):
        n = 1 << stage
        rows = pl.ds(piece * 64, 64)
        at = 49 + stage * 8 + kind * 4 + piece
        out_copies[stage, kind, piece] = send(
            w.at[kind, pl.ds(0, n), rows],
            w.at[kind, pl.ds(n, n), rows],
            sent.at[at],
            got.at[at],
            here,
            OUT_STAGES[kind][stage],
        )

    def next_out(stage, piece):
        for kind in range(2):
            out_copies[stage, kind, piece].wait_recv()
            start_out(stage + 1, kind, piece)

    for copy in own_out:
        copy.wait()
    for kind in range(2):
        start_out(0, kind, 0)
    first = [start_stage(0, k) for k in range(16)]
    tok_copy = pltpu.make_async_copy(tok, x, load.at[12])
    tok_copy.start()
    vq_copy = pltpu.make_async_copy(vec_q, vq, load.at[13])
    vq_copy.start()
    vo_copy = pltpu.make_async_copy(vec_o, vo, load.at[14])
    vo_copy.start()
    wall_copies = []

    def keep_wall(kind, lo):
        copy = pltpu.make_async_copy(
            w.at[kind, pl.ds(lo, 4)], wall.at[kind, pl.ds(lo, 4)], load.at[18 + kind + lo // 2]
        )
        copy.start()
        wall_copies.append(copy)

    xy_own = here[0] * 4 + here[1] * 2 + here[3]
    zc_own = here[2] * 2 + here[4]

    def exchange(slots, own, peers, base):
        ref = slots.at[own]
        return [
            send(ref, ref, sent.at[base + n], got.at[base + n], here, masks)
            for n, masks in enumerate(peers)
        ]

    def norm_rows(lo, hi):
        def step(i, carry):
            rows = pl.ds(pl.multiple_of(i * 16, 16), 16)
            total = jnp.zeros((16, 1), F32)
            for c in range(8):
                part = x[rows, pl.ds(c * 1024, 1024)].astype(F32)
                total += jnp.sum(part * part, axis=1, keepdims=True)
            inv = lax.rsqrt(total / D + NORM_EPS)
            for c in range(8):
                cols = pl.ds(c * 1024, 1024)
                x[rows, cols] = (x[rows, cols].astype(F32) * inv * gain[:, cols]).astype(BF)
            return carry

        lax.fori_loop(lo // 16, hi // 16, step, 0)

    def dots(s, lo, hi):
        def step(p, carry):
            bits = (lax.rem(p, 2), lax.rem(p // 2, 2), p // 4)
            source = dp_source(here, bits, IN_STAGES[s])
            cols = pl.ds(pl.multiple_of(source * 1024 + s * 256, 256), 256)
            acc[...] += jnp.dot(x[:, cols], buf[s, p], preferred_element_type=F32)
            return carry

        lax.fori_loop(lo, hi, step, 0)

    def gram():
        pairs = [(i, j) for i in range(K) for j in range(i, K)]

        def tile(ref, rows, cols, carry):
            b = [ref[j, rows, cols].astype(F32) for j in range(K)]
            out = []
            for (i, j), a in zip(pairs, carry):
                p = b[i] * b[j]
                out.append(a + (p[:8] + p[8:]))
            return tuple(out)

        def step_q(r, carry):
            rows = pl.ds(pl.multiple_of(r * 16, 16), 16)
            for h in range(2):
                carry = tile(vq, rows, pl.ds(h * 128, 128), carry)
            return carry

        def step_o(r, carry):
            rows = pl.ds(pl.multiple_of(r * 16, 16), 16)
            for h in range(8):
                carry = tile(vo, rows, pl.ds(h * 128, 128), carry)
            return carry

        carry = tuple(jnp.zeros((8, 128), F32) for _ in pairs)
        carry = lax.fori_loop(0, 64, step_q, carry)
        carry = lax.fori_loop(0, 16, step_o, carry)
        lane = lax.broadcasted_iota(jnp.int32, (8, 128), 1)
        row = lax.broadcasted_iota(jnp.int32, (8, 128), 0)
        tile_sum = jnp.zeros((8, 128), F32)
        for (i, j), a in zip(pairs, carry):
            value = jnp.sum(jnp.sum(a, axis=0, keepdims=True), axis=1, keepdims=True)
            hit = jnp.logical_or(
                jnp.logical_and(lane == i, row == j), jnp.logical_and(lane == j, row == i)
            )
            tile_sum = tile_sum + jnp.where(hit, value, 0.0)
        g1[xy_own] = tile_sum

    acc[...] = jnp.zeros_like(acc)
    second, third = [], []
    out_steps = {
        1: (0, 0), 2: (0, 1), 4: (0, 2), 6: (0, 3), 3: (1, 0), 5: (1, 1), 7: (1, 2), 9: (1, 3)
    }
    for k in range(16):
        first[k].wait_recv()
        second.append(start_stage(1, k))
        if k >= 1:
            second[k - 1].wait_recv()
            third.append(start_stage(2, k - 1))
        if k in out_steps:
            stage, piece = out_steps[k]
            next_out(stage, piece)
        if k in (0, 2, 4):
            start_out(0, 0, k // 2 + 1)
            start_out(0, 1, k // 2 + 1)
        if k == 0:
            tok_copy.wait()
            norm_rows(0, 256)
        if k == 1:
            norm_rows(256, 512)
            out_copy = pltpu.make_async_copy(x, normed_out, load.at[15])
            out_copy.start()
        if k == 2:
            vq_copy.wait()
            vo_copy.wait()
            gram()
            over_xy = exchange(g1, xy_own, XY_PEERS, 73)
        if k == 8:
            dots(0, 0, 4)
        if k == 9:
            dots(1, 0, 4)
        if k == 10:
            keep_wall(0, 0)
            keep_wall(1, 0)
            for copy in over_xy:
                copy.wait_recv()
            total = g1[0]
            for n in range(1, 16):
                total = total + g1[n]
            g2[zc_own] = total
            over_zc = exchange(g2, zc_own, ZC_PEERS, 88)
        if k == 13:
            for n in (0, 2, 4, 6):
                third[n].wait_recv()
            dots(0, 4, 8)
        if k == 14:
            for n in (1, 3, 5, 7):
                third[n].wait_recv()
            dots(1, 4, 8)
        if k == 15:
            dots(2, 0, 4)
    second[15].wait_recv()
    third.append(start_stage(2, 15))
    dots(3, 0, 4)
    for s in (2, 3):
        for n in range(8, 16):
            if SUPER[n] == s:
                third[n].wait_recv()
        dots(s, 4, 8)
    mine[...] = acc[:, pl.ds(512, 128)].astype(BF)
    swap = send(mine, theirs, sent.at[48], got.at[48], here, CORE)
    q_out[...] = acc[:, pl.ds(0, 256)].astype(BF)
    t_out[...] = (acc[:, pl.ds(256, 256)] * (D ** (-0.5))).astype(BF)
    swap.wait()
    own = mine[...].astype(F32)
    other = theirs[...].astype(F32)
    first_core = core == 0
    k_out[...] = jnp.where(first_core, own, other).astype(BF)
    v_out[...] = jnp.where(first_core, other, own).astype(BF)
    for kind in range(2):
        for piece in range(4):
            out_copies[2, kind, piece].wait_recv()
        keep_wall(kind, 4)
    for copy in over_zc:
        copy.wait_recv()
    total = g2[0]
    for n in range(1, 8):
        total = total + g2[n]
    gram_out[...] = total / count
    for copy in first + second + third + list(out_copies.values()) + over_xy + over_zc:
        copy.wait_send()
    for copy in wall_copies:
        copy.wait()
    out_copy.wait()


def any_specs(n):
    return [pl.BlockSpec(memory_space=pl.ANY) for _ in range(n)]


def vmem_specs(n):
    return [pl.BlockSpec(memory_space=pltpu.VMEM) for _ in range(n)]


def project(tokens, norm_gain, q_weight, basis_query, kv_weight, basis_output, o_weight, count):
    shape = jax.ShapeDtypeStruct
    return pl.pallas_call(
        functools.partial(project_kernel, count),
        out_shape=(
            shape((512, 256), BF),
            shape((512, 256), BF),
            shape((512, HD), BF),
            shape((512, HD), BF),
            shape((512, D), BF),
            shape((8, 128), F32),
            shape((2, 8, 256, 1024), BF),
        ),
        in_specs=any_specs(1) + vmem_specs(1) + any_specs(5),
        out_specs=tuple(vmem_specs(4) + any_specs(1) + vmem_specs(1) + any_specs(1)),
        scratch_shapes=[
            pltpu.VMEM((512, D), BF),
            pltpu.VMEM((4, 8, 256, 640), BF),
            pltpu.VMEM((512, 640), F32),
            pltpu.VMEM((512, HD), BF),
            pltpu.VMEM((512, HD), BF),
            pltpu.VMEM((K, 1024, 256), BF),
            pltpu.VMEM((K, 256, 1024), BF),
            pltpu.VMEM((2, 8, 256, 1024), BF),
            pltpu.VMEM((16, 8, 128), F32),
            pltpu.VMEM((8, 8, 128), F32),
            pltpu.SemaphoreType.DMA((22,)),
            pltpu.SemaphoreType.DMA((95,)),
            pltpu.SemaphoreType.DMA((95,)),
        ],
        compiler_params=pltpu.CompilerParams(
            collective_id=0, has_side_effects=True, vmem_limit_bytes=VMEM_BYTES
        ),
        name="project",
    )(tokens, norm_gain, q_weight, basis_query, kv_weight, basis_output, o_weight)


def output_kernel(
    q, t, k, v, allowed, cos_twice, sin_signed, wall, cot, gp_out, probs,
    h, w, g, acc, tb, mine, theirs, cs, c1, c2, c3, gp, load, sent, got,
):
    here = position()
    place = here[2] * 2 + here[3]
    loads = []
    for kind in (0, 1):
        copy = pltpu.make_async_copy(wall.at[kind], w.at[kind], load.at[kind])
        copy.start()
        loads.append(copy)
    peers = [X1, X3, YH, CORE] + [same_core_masks(r) for r in range(1, 8)]
    greet(here, peers)
    attend_both(q, t, k, v, allowed, cos_twice, sin_signed, h, probs)
    greeted(peers)
    copies = []

    def start(at, src, dst, masks):
        copy = send(src, dst, sent.at[at], got.at[at], here, masks)
        copies.append(copy)
        return copy

    def index_of(r):
        z, yl = peer(here[2:4], same_core_masks(r)[2:4])
        return z * 2 + yl

    spread = {
        r: start(r, h.at[index_of(r)], g.at[:, r, 0], same_core_masks(r)) for r in range(1, 8)
    }
    g[:, 0, 0] = h[place]

    def gather(stage, rg, kind):
        n = 1 << stage
        group = pl.ds(rg * 2, 2)
        return start(
            8 + stage * 8 + rg * 2 + kind,
            g.at[kind, group, pl.ds(0, n)],
            g.at[kind, group, pl.ds(n, n)],
            STAGES[kind][stage],
        )

    one, two, three = {}, {}, {}
    for rg in range(4):
        for r in (rg * 2, rg * 2 + 1):
            if r:
                spread[r].wait_recv()
        for kind in range(2):
            one[rg, kind] = gather(0, rg, kind)
    order = [(rg, kind) for rg in range(4) for kind in range(2)]
    for n, key in enumerate(order):
        one[key].wait_recv()
        two[key] = gather(1, *key)
        if n >= 1:
            two[order[n - 1]].wait_recv()
            three[order[n - 1]] = gather(2, *order[n - 1])
    two[order[7]].wait_recv()
    three[order[7]] = gather(2, *order[7])

    def rows_of(r, cols):
        parts = [g[kind, r, :, :, cols].reshape(256, 256) for kind in range(2)]
        return jnp.concatenate(parts, axis=0)

    for copy in loads:
        copy.wait()
    acc[...] = jnp.zeros_like(acc)
    for rg in range(4):
        three[rg, 0].wait_recv()
        three[rg, 1].wait_recv()
        for r in (rg * 2, rg * 2 + 1):
            acc[...] += jnp.dot(
                rows_of(r, pl.ds(0, 256)), w[0, out_place(r, 0)], preferred_element_type=F32
            ) + jnp.dot(
                rows_of(r, pl.ds(256, 256)), w[1, out_place(r, 1)], preferred_element_type=F32
            )
    swaps = []
    for half in range(2):
        rows = pl.ds(half * 256, 256)
        mine[rows] = acc[rows].astype(BF)
        swaps.append(start(56 + half, mine.at[rows], theirs.at[rows], CORE))
    for half in range(2):
        rows = pl.ds(half * 256, 256)
        swaps[half].wait_recv()
        tb[rows] = (mine[rows].astype(F32) + theirs[rows].astype(F32)).astype(BF)

    def scatter(stage, key, src, dst):
        rg, kind = key
        return start(32 + stage * 8 + rg * 2 + kind, src, dst, STAGES[kind][2 - stage])

    one, two, three = {}, {}, {}
    for rg in range(4):
        group = pl.ds(rg * 2, 2)
        for r in (rg * 2, rg * 2 + 1):
            part = lax.dot_general(
                tb[...],
                w[1, out_place(r, 1)],
                (((1,), (1,)), ((), ())),
                preferred_element_type=F32,
            ).astype(BF)
            for kind in range(2):
                cs[kind, r] = part[kind * 256 : kind * 256 + 256].reshape(8, 32, 256)
        for kind in range(2):
            one[rg, kind] = scatter(
                0, (rg, kind), cs.at[kind, group, pl.ds(4, 4)], c1.at[kind, group]
            )

    def added(key, n, ref):
        rg, kind = key
        group = pl.ds(rg * 2, 2)
        cs[kind, group, pl.ds(0, n)] = (
            cs[kind, group, pl.ds(0, n)].astype(F32) + ref[kind, group].astype(F32)
        ).astype(BF)

    def output_grad(r):
        mz, ml = r // 2, r % 2
        block = lax.dot_general(
            rows_of(r, pl.ds(0, 256)),
            tb[...],
            (((0,), (0,)), ((), ())),
            preferred_element_type=F32,
        ).astype(BF)
        for kind in range(2):
            gp[kind, z_place(mz, kind), ml] = block[:, kind * 512 : kind * 512 + 512]

    def second(key):
        rg, kind = key
        one[key].wait_recv()
        added(key, 4, c1)
        group = pl.ds(rg * 2, 2)
        two[key] = scatter(1, key, cs.at[kind, group, pl.ds(2, 2)], c2.at[kind, group])

    def third(key):
        rg, kind = key
        two[key].wait_recv()
        added(key, 2, c2)
        group = pl.ds(rg * 2, 2)
        three[key] = scatter(2, key, cs.at[kind, group, pl.ds(1, 1)], c3.at[kind, group])

    for n, key in enumerate(order):
        second(key)
        if n >= 1:
            third(order[n - 1])
        output_grad(n)
    third(order[7])
    back = {}
    for rg in range(4):
        for kind in range(2):
            three[rg, kind].wait_recv()
            added((rg, kind), 1, c3)
        for r in (rg * 2, rg * 2 + 1):
            if r:
                back[r] = start(r + 58, cs.at[:, r, 0], cot.at[place], same_core_masks(r))
    cot[place] = cs[:, 0, 0]
    gp_copy = pltpu.make_async_copy(gp, gp_out, load.at[2])
    gp_copy.start()
    for r in range(1, 8):
        back[r].wait_recv()
    for copy in copies:
        copy.wait_send()
    gp_copy.wait()


def output_side(query, tangent, key_states, values, allowed, cos_twice, sin_signed, wall):
    shape = jax.ShapeDtypeStruct
    return pl.pallas_call(
        output_kernel,
        out_shape=(
            shape((8, 2, 32, 256), BF),
            shape((2, 4, 2, 256, 512), BF),
            shape((4, 256, 256), F32),
        ),
        in_specs=vmem_specs(7) + any_specs(1),
        out_specs=tuple(vmem_specs(1) + any_specs(1) + vmem_specs(1)),
        scratch_shapes=[
            pltpu.VMEM((8, 2, 32, 512), BF),
            pltpu.VMEM((2, 8, 256, 1024), BF),
            pltpu.VMEM((2, 8, 8, 32, 512), BF),
            pltpu.VMEM((512, 1024), F32),
            pltpu.VMEM((512, 1024), BF),
            pltpu.VMEM((512, 1024), BF),
            pltpu.VMEM((512, 1024), BF),
            pltpu.VMEM((2, 8, 8, 32, 256), BF),
            pltpu.VMEM((2, 8, 4, 32, 256), BF),
            pltpu.VMEM((2, 8, 2, 32, 256), BF),
            pltpu.VMEM((2, 8, 1, 32, 256), BF),
            pltpu.VMEM((2, 4, 2, 256, 512), BF),
            pltpu.SemaphoreType.DMA((3,)),
            pltpu.SemaphoreType.DMA((66,)),
            pltpu.SemaphoreType.DMA((66,)),
        ],
        compiler_params=pltpu.CompilerParams(
            collective_id=3, has_side_effects=True, vmem_limit_bytes=VMEM_BYTES
        ),
        name="output_side",
    )(query, tangent, key_states, values, allowed, cos_twice, sin_signed, wall)


def tail_kernel(
    factor, count, normed_hbm, cot_heads, k, v, probs, cos_twice, sin_signed, gp, gram, vec_q, vec_o,
    next_q, next_o, coeffs, cot, normed, part, r1, r2, r3, own, z1, z2, y1, vq, vo, gq, go, facc,
    s1, s2, u1, u2, load, sent, got,
):
    here = position()
    xy_own = here[0] * 4 + here[1] * 2 + here[3]
    zc_own = here[2] * 2 + here[4]
    loads = []

    def fetch(src, dst):
        copy = pltpu.make_async_copy(src, dst, load.at[len(loads)])
        copy.start()
        loads.append(copy)

    fetch(gp, own)
    fetch(normed_hbm, normed)
    greet(here, XY_PEERS + ZC_PEERS)
    greeted(XY_PEERS + ZC_PEERS)
    copies = []

    def keep(copy):
        copies.append(copy)
        return copy

    def rows_at(j):
        return pl.ds(j // 2 * 64, 64)

    def start_out(stage, j, src, dst):
        at = 24 + stage * 8 + j
        masks = ((Z3, Z1)[j % 2], (Z1, Z3)[j % 2], YL)[stage]
        return keep(send(src, dst, sent.at[at], got.at[at], here, masks))

    z_high, z_low, over_y = {}, {}, {}

    def out_high(j):
        kind, rows = j % 2, rows_at(j)
        z_high[j] = start_out(0, j, own.at[kind, pl.ds(2, 2), :, rows], z1.at[kind, :, :, rows])

    def out_low(j):
        kind, rows = j % 2, rows_at(j)
        z_high[j].wait_recv()
        if j + 4 < 8:
            out_high(j + 4)
        own[kind, pl.ds(0, 2), :, rows] = (
            own[kind, pl.ds(0, 2), :, rows].astype(F32) + z1[kind, :, :, rows].astype(F32)
        ).astype(BF)
        z_low[j] = start_out(1, j, own.at[kind, 1, :, rows], z2.at[kind, :, rows])

    def out_y(j):
        kind, rows = j % 2, rows_at(j)
        z_low[j].wait_recv()
        own[kind, 0, :, rows] = (
            own[kind, 0, :, rows].astype(F32) + z2[kind, :, rows].astype(F32)
        ).astype(BF)
        over_y[j] = start_out(2, j, own.at[kind, 0, 1, rows], y1.at[kind, rows])

    def against(g, v, row0, tiles, col0, col_tiles):
        def step(i, state):
            rows = pl.ds(pl.multiple_of(row0 + i * 16, 16), 16)
            for h in range(col_tiles):
                cols = pl.ds(col0 + h * 128, 128)
                here_g = g[rows, cols]
                out = []
                for j in range(K):
                    p = here_g * v[j, rows, cols].astype(F32)
                    out.append(state[j] + (p[:8] + p[8:]))
                state = tuple(out)
            return state

        state = lax.fori_loop(0, tiles, step, tuple(facc[j] for j in range(K)))
        for j in range(K):
            facc[j] = state[j]

    def out_end(j):
        kind, rows = j % 2, rows_at(j)
        over_y[j].wait_recv()
        go[rows, pl.ds(kind * 512, 512)] = own[kind, 0, 0, rows].astype(F32) + y1[
            kind, rows
        ].astype(F32)
        against(go, vo, j // 2 * 64, 4, kind * 512, 4)

    def product(low, mid, high):
        source = dp_source(here, (low, mid, high), STAGES[0])
        cols = pl.ds(pl.multiple_of(source * 1024, 1024), 1024)
        block = jnp.dot(cot[...], normed[:, cols], preferred_element_type=F32) * factor
        block = block.astype(BF)
        for c in range(8):
            place = low + 2 * mid + 4 * high if c % 2 == 0 else high + 2 * mid + 4 * low
            part[c, place] = block[:, c * 128 : (c + 1) * 128]

    def start(stage, c, src, dst):
        at = stage * 8 + c
        return keep(send(src, dst, sent.at[at], got.at[at], here, STAGES[c % 2][2 - stage]))

    one, two, three = {}, {}, {}

    def q_one(c):
        one[c] = start(0, c, part.at[c, pl.ds(4, 4)], r1.at[c])

    loads[0].wait()
    for j in range(4):
        out_high(j)
    attend_back(cot_heads, k, v, probs, cos_twice, sin_signed, cot)
    loads[1].wait()
    fetch(vec_q, vq)
    fetch(vec_o, vo)
    product(1, 0, 1)
    product(1, 1, 1)
    product(0, 0, 1)
    product(0, 1, 1)
    q_one(0)
    q_one(2)
    product(1, 0, 0)
    product(1, 1, 0)
    q_one(1)
    q_one(3)
    product(0, 0, 0)
    product(0, 1, 0)
    facc[...] = jnp.zeros_like(facc)

    def added(c, n, ref):
        part[c, pl.ds(0, n)] = (
            part[c, pl.ds(0, n)].astype(F32) + ref[c].astype(F32)
        ).astype(BF)

    def q_two(c):
        one[c].wait_recv()
        if c + 4 < 8:
            q_one(c + 4)
        added(c, 4, r1)
        two[c] = start(1, c, part.at[c, pl.ds(2, 2)], r2.at[c])

    def q_three(c):
        two[c].wait_recv()
        added(c, 2, r2)
        three[c] = start(2, c, part.at[c, pl.ds(1, 1)], r3.at[c])

    def q_end(c):
        three[c].wait_recv()
        total = part[c, 0].astype(F32) + r3[c, 0].astype(F32)
        gq[pl.ds(c * 128, 128), :] = total.T
        against(gq, vq, c * 128, 8, 0, 2)

    lagged = ((q_two, 0), (q_three, 2), (out_low, 1), (out_y, 3), (q_end, 4), (out_end, 5))
    for n in range(8 + 5):
        if n == 2:
            loads[2].wait()
            loads[3].wait()
        for action, lag in lagged:
            if 0 <= n - lag < 8:
                action(n - lag)

    def exchange(slots, own_slot, peers, base):
        ref = slots.at[own_slot]
        return [
            keep(send(ref, ref, sent.at[base + n], got.at[base + n], here, masks))
            for n, masks in enumerate(peers)
        ]

    def sum_over(over_xy, over_zc, base):
        for copy in exchange(over_xy, xy_own, XY_PEERS, base):
            copy.wait_recv()
        total = over_xy[0]
        for n in range(1, 16):
            total = total + over_xy[n]
        over_zc[zc_own] = total
        for copy in exchange(over_zc, zc_own, ZC_PEERS, base + 15):
            copy.wait_recv()
        total = over_zc[0]
        for n in range(1, 8):
            total = total + over_zc[n]
        return total

    for j in range(K):
        s1[xy_own, pl.ds(j, 1)] = jnp.sum(facc[j], axis=0, keepdims=True)
    first = jnp.sum(sum_over(s1, s2, 48), axis=1, keepdims=True) / count
    second = first
    for i in range(K):
        second = second - gram[:, pl.ds(i, 1)] * first[i : i + 1]
    both = first + second
    weights = [jnp.broadcast_to(both[j : j + 1], (16, 128)) for j in range(K)]

    def cleaned(g, v, c, row_tiles, col_tiles, state):
        def step(r, state):
            rows = pl.ds(pl.multiple_of(r * 16, 16), 16)
            for h in range(col_tiles):
                cols = pl.ds(h * 128, 128)
                value = g[rows, cols]
                for j in range(K):
                    value = value - weights[j] * v[j, rows, cols].astype(F32)
                c[rows, cols] = value
                p = value * value
                state = state + (p[:8] + p[8:])
            return state

        return lax.fori_loop(0, row_tiles, step, state)

    state = cleaned(gq, vq, gq, 64, 2, jnp.zeros((8, 128), F32))
    u1[xy_own] = cleaned(go, vo, go, 16, 8, state)
    squares = sum_over(u1, u2, 70)
    squares = jnp.sum(jnp.sum(squares, axis=1, keepdims=True), axis=0, keepdims=True) / count
    beta = jnp.sqrt(squares + BETA_EPS)
    scale = 1.0 / beta
    next_q[...] = (gq[...] * scale).astype(BF)
    next_o[...] = (go[...] * scale).astype(BF)
    coeffs[pl.ds(0, 8)] = jnp.broadcast_to(both, (8, 128))
    coeffs[pl.ds(8, 8)] = jnp.broadcast_to(beta, (8, 128))
    for copy in copies:
        copy.wait_send()


def tail(
    normed, cot_heads, key_states, values, probs, cos_twice, sin_signed,
    partials, gram, basis_query, basis_output, factor, count,
):
    shape = jax.ShapeDtypeStruct
    return pl.pallas_call(
        functools.partial(tail_kernel, factor, count),
        out_shape=(shape((1024, 256), BF), shape((256, 1024), BF), shape((16, 128), F32)),
        in_specs=any_specs(1) + vmem_specs(6) + any_specs(1) + vmem_specs(1) + any_specs(2),
        out_specs=tuple(vmem_specs(3)),
        scratch_shapes=[
            pltpu.VMEM((256, 512), BF),
            pltpu.VMEM((512, D), BF),
            pltpu.VMEM((8, 8, 256, 128), BF),
            pltpu.VMEM((8, 4, 256, 128), BF),
            pltpu.VMEM((8, 2, 256, 128), BF),
            pltpu.VMEM((8, 1, 256, 128), BF),
            pltpu.VMEM((2, 4, 2, 256, 512), BF),
            pltpu.VMEM((2, 2, 2, 256, 512), BF),
            pltpu.VMEM((2, 2, 256, 512), BF),
            pltpu.VMEM((2, 256, 512), BF),
            pltpu.VMEM((K, 1024, 256), BF),
            pltpu.VMEM((K, 256, 1024), BF),
            pltpu.VMEM((1024, 256), F32),
            pltpu.VMEM((256, 1024), F32),
            pltpu.VMEM((K, 8, 128), F32),
            pltpu.VMEM((16, 8, 128), F32),
            pltpu.VMEM((8, 8, 128), F32),
            pltpu.VMEM((16, 8, 128), F32),
            pltpu.VMEM((8, 8, 128), F32),
            pltpu.SemaphoreType.DMA((4,)),
            pltpu.SemaphoreType.DMA((92,)),
            pltpu.SemaphoreType.DMA((92,)),
        ],
        compiler_params=pltpu.CompilerParams(
            collective_id=1, has_side_effects=True, vmem_limit_bytes=VMEM_BYTES
        ),
        name="tail",
    )(
        normed, cot_heads, key_states, values, probs, cos_twice, sin_signed,
        partials, gram, basis_query, basis_output,
    )


def body(tokens, segments, norm_gain, q_weight, kv_weight, o_weight, basis_query, basis_output):
    groups = lax.axis_size(DP)
    seq_count, length, model_width = tokens.shape
    row_count = seq_count * length
    qwidth = QH * HD
    query_scale = D ** (-0.5)
    gn_scale = qwidth / (row_count * groups)
    param_count = 2.0 * D * qwidth
    query, tangent, key_states, values, normed, gram, wall = project(
        tokens.reshape(row_count, model_width),
        norm_gain.reshape(1, model_width),
        q_weight,
        basis_query,
        kv_weight,
        basis_output,
        o_weight,
        param_count,
    )
    allowed = allowed_pairs(segments).astype(jnp.bfloat16)
    cosine, sine = rope_tables(length, HD)
    cos_twice = jnp.concatenate([cosine, cosine], axis=1)
    sin_signed = jnp.concatenate([-sine, sine], axis=1)
    cot_heads, partials, probs = output_side(
        query, tangent, key_states, values, allowed, cos_twice, sin_signed, wall
    )
    next_query, next_output, lines = tail(
        normed,
        cot_heads,
        key_states,
        values,
        probs,
        cos_twice,
        sin_signed,
        partials,
        gram,
        basis_query,
        basis_output,
        gn_scale * query_scale,
        param_count,
    )
    return (next_query, next_output, lines[:9, 0])


def solution(mesh):
    finer = Mesh(
        mesh.devices.reshape(4, 2, 4, 2, 2), ("dp_0", "dp_1", "tensor_0", "tensor_1", "tensor_2")
    )
    placed = (
        P(DP, None, None),
        P(DP, None),
        P(),
        P(DP, TENSOR),
        P(None, DP, None),
        P(TENSOR, DP),
        P(None, DP, TENSOR),
        P(None, TENSOR, DP),
    )
    return jax.shard_map(
        body,
        mesh=finer,
        in_specs=placed,
        out_specs=(P(DP, TENSOR), P(TENSOR, DP), P()),
        check_vma=False,
    )
```

```python
import functools
import math

import jax
import jax.numpy as jnp
import numpy as np
from jax import lax
from jax.experimental import pallas as pl
from jax.experimental.pallas import tpu as pltpu
from jax.sharding import Mesh
from jax.sharding import PartitionSpec as P

D = 8192
HD = 128
QH = 32
KVH = 4
K = 8
DP = ("dp_0", "dp_1")
TENSOR = ("tensor_0", "tensor_1", "tensor_2")
DP_TENSOR = ("dp_0", "dp_1", "tensor_0", "tensor_1", "tensor_2")


PRECISE = lax.Precision.HIGHEST
ROPE_BASE = 500000.0
NORM_EPS = 1e-05
BETA_EPS = 1e-06


MESH = pl.DeviceIdType.MESH
VMEM_BYTES = 58 * 1024 * 1024
X1, X3, X2, YH = (1, 0, 0, 0, 0), (3, 0, 0, 0, 0), (2, 0, 0, 0, 0), (0, 1, 0, 0, 0)
Z1, Z3, YL, CORE = (0, 0, 1, 0, 0), (0, 0, 3, 0, 0), (0, 0, 0, 1, 0), (0, 0, 0, 0, 1)
BF = jnp.bfloat16
F32 = jnp.float32


def position():
    return [lax.axis_index(a) for a in DP_TENSOR]


def flipped(value, mask):
    if mask == 0:
        return value
    if mask == 1:
        return value + 1 - 2 * lax.rem(value, 2)
    if mask == 2:
        return lax.rem(value + 2, 4)
    return 3 - value


def peer(here, masks):
    return tuple(flipped(v, m) for v, m in zip(here, masks))


def greet(here, peers):
    barrier = pltpu.get_barrier_semaphore()
    for masks in peers:
        pl.semaphore_signal(barrier, inc=1, device_id=peer(here, masks), device_id_type=MESH)


def greeted(peers):
    pl.semaphore_wait(pltpu.get_barrier_semaphore(), len(peers))


def send(src, dst, send_sem, recv_sem, here, masks):
    copy = pltpu.make_async_remote_copy(
        src_ref=src,
        dst_ref=dst,
        send_sem=send_sem,
        recv_sem=recv_sem,
        device_id=peer(here, masks),
        device_id_type=MESH,
    )
    copy.start()
    return copy


def dp_source(here, bits, stages):
    x, yh = here[0], here[1]
    for bit, masks in zip(bits, stages):
        if masks[0] == 1:
            x = x + bit * (1 - 2 * lax.rem(x, 2))
        elif masks[0] == 3:
            x = x + bit * (3 - 2 * x)
        else:
            yh = yh + bit * (1 - 2 * yh)
    return x * 2 + yh


STAGES = ((X1, YH, X3), (X3, YH, X1))
IN_STAGES = ((X1, YH, X3), (X3, YH, X1), (X1, YH, X3), (X3, YH, X1))
OUT_STAGES = ((YL, Z1, Z3), (YL, Z3, Z1))


XY_PEERS = [
    (x, yh, 0, yl, 0) for x in range(4) for yh in range(2) for yl in range(2) if x or yh or yl
]
ZC_PEERS = [(0, 0, z, 0, c) for z in range(4) for c in range(2) if z or c]


def z_place(mask, kind):
    one, three = {0: (0, 0), 1: (1, 0), 3: (0, 1), 2: (1, 1)}[mask]
    return one + 2 * three if kind == 0 else three + 2 * one


def out_place(r, kind):
    mz, ml = r // 2, r % 2
    return ml + 2 * z_place(mz, kind)


def same_core_masks(r):
    return (0, 0, r // 2, r % 2, 0)


def rope_tables(length, head_width):
    half_width = head_width // 2
    frequency = np.exp(
        np.arange(half_width, dtype=np.float32) * np.float32(-2.0 * math.log(ROPE_BASE) / head_width)
    ).astype(np.float32)
    angles = np.arange(length, dtype=np.float32)[:, None] * frequency[None, :]
    cosine, sine = np.cos(angles), np.sin(angles)
    return (np.concatenate([cosine, cosine], axis=1), np.concatenate([-sine, sine], axis=1))


def rotated(vectors, cos_twice, sin_signed):
    return vectors * cos_twice + pltpu.roll(vectors, HD // 2, 1) * sin_signed


def rotated_back(vectors, cos_twice, sin_signed):
    return vectors * cos_twice - pltpu.roll(vectors, HD // 2, 1) * sin_signed


def dot_wide(a, b, a_dim, b_dim):
    return lax.dot_general(
        a, b, (((a_dim,), (b_dim,)), ((), ())), precision=PRECISE, preferred_element_type=F32
    )


def attend_both(s, q, t, k, v, segments, cos_twice, sin_signed, h, probs):
    scale = HD ** (-0.5)
    rows = pl.ds(s * 256, 256)
    keys = rotated(k[rows].astype(F32), cos_twice[...], sin_signed[...])
    values = v[rows].astype(F32)
    across = jnp.broadcast_to(segments[pl.ds(s, 1)].astype(F32), (256, 256))
    row = lax.broadcasted_iota(jnp.int32, (256, 256), 0)
    column = lax.broadcasted_iota(jnp.int32, (256, 256), 1)
    mask = jnp.logical_and(across == across.T, row >= column)
    for head in range(2):
        cols = pl.ds(head * HD, HD)
        moving = rotated(q[rows, cols].astype(F32), cos_twice[...], sin_signed[...])
        along = rotated(t[rows, cols].astype(F32), cos_twice[...], sin_signed[...])
        scores = jnp.where(mask, dot_wide(moving, keys, 1, 1) * scale, -1e30)
        weights = jnp.exp(scores - jnp.max(scores, axis=1, keepdims=True))
        p = weights / jnp.sum(weights, axis=1, keepdims=True)
        probs[2 * s + head] = p
        slope = jnp.where(mask, dot_wide(along, keys, 1, 1) * scale, 0.0)
        dp = p * (slope - jnp.sum(p * slope, axis=1, keepdims=True))
        heads = dot_wide(p, values, 1, 0).astype(BF).astype(F32) * ((QH * HD) ** (-0.5))
        tangents = dot_wide(dp, values, 1, 0)
        h[s, :, :, cols] = heads.astype(BF).reshape(8, 32, HD)
        h[s, :, :, pl.ds(256 + head * HD, HD)] = tangents.astype(BF).reshape(8, 32, HD)


def attend_back(cot, k, v, probs, cos_twice, sin_signed, out):
    scale = HD ** (-0.5)
    for s in range(2):
        rows = pl.ds(s * 256, 256)
        keys = rotated(k[rows].astype(F32), cos_twice[...], sin_signed[...])
        values = v[rows].astype(F32)
        for head in range(2):
            cols = pl.ds(head * HD, HD)
            given = cot[s, :, :, cols].reshape(256, HD).astype(F32)
            p = probs[2 * s + head]
            slope = dot_wide(given, values, 1, 1)
            ds = p * (slope - jnp.sum(p * slope, axis=1, keepdims=True))
            moving = rotated_back(dot_wide(ds, keys, 1, 0) * scale, cos_twice[...], sin_signed[...])
            out[cols, rows] = moving.T.astype(BF)


SUPER = (0, 1) * 4 + (2, 3) * 4
PIECE = (0, 0, 1, 1, 2, 2, 3, 3) * 2


def project_kernel(
    count, tok, gain, q_w, vec_q, kv_w, vec_o, o_w,
    q_out, t_out, k_out, v_out, normed_out, gram_out, wall,
    x, buf, acc, mine, theirs, vq, vo, w, g1, g2, load, sent, got,
):
    here = position()
    core = here[4]
    kv_head = here[2]
    for_rows = []
    for s in range(4):
        rows = pl.ds(s * 256, 256)
        kv_cols = pl.ds(pl.multiple_of(kv_head * HD, HD), HD)
        parts = (
            (q_w.at[rows], buf.at[s, 0, :, pl.ds(0, 256)]),
            (vec_q.at[K - 1, rows], buf.at[s, 0, :, pl.ds(256, 256)]),
            (kv_w.at[core, rows, kv_cols], buf.at[s, 0, :, pl.ds(512, 128)]),
        )
        for n, (src, dst) in enumerate(parts):
            copy = pltpu.make_async_copy(src, dst, load.at[3 * s + n])
            copy.start()
            for_rows.append(copy)
    own_out = []
    for kind, src in enumerate((vec_o.at[K - 1], o_w)):
        copy = pltpu.make_async_copy(src, w.at[kind, 0], load.at[16 + kind])
        copy.start()
        own_out.append(copy)
    greet(here, XY_PEERS + ZC_PEERS)
    greeted(XY_PEERS + ZC_PEERS)
    for copy in for_rows:
        copy.wait()

    def start_stage(stage, k):
        s, rows = SUPER[k], pl.ds(PIECE[k] * 64, 64)
        n = 1 << stage
        at = stage * 16 + k
        return send(
            buf.at[s, pl.ds(0, n), rows],
            buf.at[s, pl.ds(n, n), rows],
            sent.at[at],
            got.at[at],
            here,
            IN_STAGES[s][stage],
        )

    out_copies = {}

    def start_out(stage, kind, piece):
        n = 1 << stage
        rows = pl.ds(piece * 64, 64)
        at = 49 + stage * 8 + kind * 4 + piece
        out_copies[stage, kind, piece] = send(
            w.at[kind, pl.ds(0, n), rows],
            w.at[kind, pl.ds(n, n), rows],
            sent.at[at],
            got.at[at],
            here,
            OUT_STAGES[kind][stage],
        )

    def next_out(stage, piece):
        for kind in range(2):
            out_copies[stage, kind, piece].wait_recv()
            start_out(stage + 1, kind, piece)

    for copy in own_out:
        copy.wait()
    for kind in range(2):
        start_out(0, kind, 0)
    first = [start_stage(0, k) for k in range(16)]
    tok_copy = pltpu.make_async_copy(tok, x, load.at[12])
    tok_copy.start()
    vq_copy = pltpu.make_async_copy(vec_q, vq, load.at[13])
    vq_copy.start()
    vo_copy = pltpu.make_async_copy(vec_o, vo, load.at[14])
    vo_copy.start()
    wall_copies = []

    def keep_wall(kind, lo):
        copy = pltpu.make_async_copy(
            w.at[kind, pl.ds(lo, 4)], wall.at[kind, pl.ds(lo, 4)], load.at[18 + kind + lo // 2]
        )
        copy.start()
        wall_copies.append(copy)

    xy_own = here[0] * 4 + here[1] * 2 + here[3]
    zc_own = here[2] * 2 + here[4]

    def exchange(slots, own, peers, base):
        ref = slots.at[own]
        return [
            send(ref, ref, sent.at[base + n], got.at[base + n], here, masks)
            for n, masks in enumerate(peers)
        ]

    def norm_rows(lo, hi):
        def step(i, carry):
            rows = pl.ds(pl.multiple_of(i * 16, 16), 16)
            total = jnp.zeros((16, 1), F32)
            for c in range(8):
                part = x[rows, pl.ds(c * 1024, 1024)].astype(F32)
                total += jnp.sum(part * part, axis=1, keepdims=True)
            inv = lax.rsqrt(total / D + NORM_EPS)
            for c in range(8):
                cols = pl.ds(c * 1024, 1024)
                x[rows, cols] = (x[rows, cols].astype(F32) * inv * gain[:, cols]).astype(BF)
            return carry

        lax.fori_loop(lo // 16, hi // 16, step, 0)

    def dots(s, lo, hi):
        def step(p, carry):
            bits = (lax.rem(p, 2), lax.rem(p // 2, 2), p // 4)
            source = dp_source(here, bits, IN_STAGES[s])
            cols = pl.ds(pl.multiple_of(source * 1024 + s * 256, 256), 256)
            acc[...] += jnp.dot(x[:, cols], buf[s, p], preferred_element_type=F32)
            return carry

        lax.fori_loop(lo, hi, step, 0)

    def gram():
        pairs = [(i, j) for i in range(K) for j in range(i, K)]

        def tile(ref, rows, cols, carry):
            b = [ref[j, rows, cols].astype(F32) for j in range(K)]
            out = []
            for (i, j), a in zip(pairs, carry):
                p = b[i] * b[j]
                out.append(a + (p[:8] + p[8:]))
            return tuple(out)

        def step_q(r, carry):
            rows = pl.ds(pl.multiple_of(r * 16, 16), 16)
            for h in range(2):
                carry = tile(vq, rows, pl.ds(h * 128, 128), carry)
            return carry

        def step_o(r, carry):
            rows = pl.ds(pl.multiple_of(r * 16, 16), 16)
            for h in range(8):
                carry = tile(vo, rows, pl.ds(h * 128, 128), carry)
            return carry

        carry = tuple(jnp.zeros((8, 128), F32) for _ in pairs)
        carry = lax.fori_loop(0, 64, step_q, carry)
        carry = lax.fori_loop(0, 16, step_o, carry)
        lane = lax.broadcasted_iota(jnp.int32, (8, 128), 1)
        row = lax.broadcasted_iota(jnp.int32, (8, 128), 0)
        tile_sum = jnp.zeros((8, 128), F32)
        for (i, j), a in zip(pairs, carry):
            value = jnp.sum(jnp.sum(a, axis=0, keepdims=True), axis=1, keepdims=True)
            hit = jnp.logical_or(
                jnp.logical_and(lane == i, row == j), jnp.logical_and(lane == j, row == i)
            )
            tile_sum = tile_sum + jnp.where(hit, value, 0.0)
        g1[xy_own] = tile_sum

    acc[...] = jnp.zeros_like(acc)
    second, third = [], []
    out_steps = {
        1: (0, 0), 2: (0, 1), 4: (0, 2), 6: (0, 3), 3: (1, 0), 5: (1, 1), 7: (1, 2), 9: (1, 3)
    }
    for k in range(16):
        first[k].wait_recv()
        second.append(start_stage(1, k))
        if k >= 1:
            second[k - 1].wait_recv()
            third.append(start_stage(2, k - 1))
        if k in out_steps:
            stage, piece = out_steps[k]
            next_out(stage, piece)
        if k in (0, 2, 4):
            start_out(0, 0, k // 2 + 1)
            start_out(0, 1, k // 2 + 1)
        if k == 0:
            tok_copy.wait()
            norm_rows(0, 256)
        if k == 1:
            norm_rows(256, 512)
            out_copy = pltpu.make_async_copy(x, normed_out, load.at[15])
            out_copy.start()
        if k == 2:
            vq_copy.wait()
            vo_copy.wait()
            gram()
            over_xy = exchange(g1, xy_own, XY_PEERS, 73)
        if k == 8:
            dots(0, 0, 4)
        if k == 9:
            dots(1, 0, 4)
        if k == 10:
            keep_wall(0, 0)
            keep_wall(1, 0)
            for copy in over_xy:
                copy.wait_recv()
            total = g1[0]
            for n in range(1, 16):
                total = total + g1[n]
            g2[zc_own] = total
            over_zc = exchange(g2, zc_own, ZC_PEERS, 88)
        if k == 13:
            for n in (0, 2, 4, 6):
                third[n].wait_recv()
            dots(0, 4, 8)
        if k == 14:
            for n in (1, 3, 5, 7):
                third[n].wait_recv()
            dots(1, 4, 8)
        if k == 15:
            dots(2, 0, 4)
    second[15].wait_recv()
    third.append(start_stage(2, 15))
    dots(3, 0, 4)
    for s in (2, 3):
        for n in range(8, 16):
            if SUPER[n] == s:
                third[n].wait_recv()
        dots(s, 4, 8)
    mine[...] = acc[:, pl.ds(512, 128)].astype(BF)
    swap = send(mine, theirs, sent.at[48], got.at[48], here, CORE)
    q_out[...] = acc[:, pl.ds(0, 256)].astype(BF)
    t_out[...] = (acc[:, pl.ds(256, 256)] * (D ** (-0.5))).astype(BF)
    swap.wait()
    own = mine[...].astype(F32)
    other = theirs[...].astype(F32)
    first_core = core == 0
    k_out[...] = jnp.where(first_core, own, other).astype(BF)
    v_out[...] = jnp.where(first_core, other, own).astype(BF)
    for kind in range(2):
        for piece in range(4):
            out_copies[2, kind, piece].wait_recv()
        keep_wall(kind, 4)
    for copy in over_zc:
        copy.wait_recv()
    total = g2[0]
    for n in range(1, 8):
        total = total + g2[n]
    gram_out[...] = total / count
    for copy in first + second + third + list(out_copies.values()) + over_xy + over_zc:
        copy.wait_send()
    for copy in wall_copies:
        copy.wait()
    out_copy.wait()


def any_specs(n):
    return [pl.BlockSpec(memory_space=pl.ANY) for _ in range(n)]


def vmem_specs(n):
    return [pl.BlockSpec(memory_space=pltpu.VMEM) for _ in range(n)]


def project(tokens, norm_gain, q_weight, basis_query, kv_weight, basis_output, o_weight, count):
    shape = jax.ShapeDtypeStruct
    return pl.pallas_call(
        functools.partial(project_kernel, count),
        out_shape=(
            shape((512, 256), BF),
            shape((512, 256), BF),
            shape((512, HD), BF),
            shape((512, HD), BF),
            shape((512, D), BF),
            shape((8, 128), F32),
            shape((2, 8, 256, 1024), BF),
        ),
        in_specs=any_specs(1) + vmem_specs(1) + any_specs(5),
        out_specs=tuple(vmem_specs(4) + any_specs(1) + vmem_specs(1) + any_specs(1)),
        scratch_shapes=[
            pltpu.VMEM((512, D), BF),
            pltpu.VMEM((4, 8, 256, 640), BF),
            pltpu.VMEM((512, 640), F32),
            pltpu.VMEM((512, HD), BF),
            pltpu.VMEM((512, HD), BF),
            pltpu.VMEM((K, 1024, 256), BF),
            pltpu.VMEM((K, 256, 1024), BF),
            pltpu.VMEM((2, 8, 256, 1024), BF),
            pltpu.VMEM((16, 8, 128), F32),
            pltpu.VMEM((8, 8, 128), F32),
            pltpu.SemaphoreType.DMA((22,)),
            pltpu.SemaphoreType.DMA((95,)),
            pltpu.SemaphoreType.DMA((95,)),
        ],
        compiler_params=pltpu.CompilerParams(
            collective_id=0, has_side_effects=True, vmem_limit_bytes=VMEM_BYTES
        ),
        name="project",
    )(tokens, norm_gain, q_weight, basis_query, kv_weight, basis_output, o_weight)


def output_kernel(
    q, t, k, v, segments, cos_twice, sin_signed, wall, cot, gp_out, probs,
    h, w, g, acc, tb, mine, theirs, cs, c1, c2, c3, gp, load, sent, got,
):
    here = position()
    place = here[2] * 2 + here[3]
    loads = []
    for kind in (0, 1):
        copy = pltpu.make_async_copy(wall.at[kind], w.at[kind], load.at[kind])
        copy.start()
        loads.append(copy)
    peers = [X1, X3, YH, CORE] + [same_core_masks(r) for r in range(1, 8)]
    greet(here, peers)
    copies = []

    def start(at, src, dst, masks):
        copy = send(src, dst, sent.at[at], got.at[at], here, masks)
        copies.append(copy)
        return copy

    def index_of(r):
        z, yl = peer(here[2:4], same_core_masks(r)[2:4])
        return z * 2 + yl

    spread = {}
    for kind in range(2):
        attend_both(kind, q, t, k, v, segments, cos_twice, sin_signed, h, probs)
        if kind == 0:
            greeted(peers)
        for r in range(1, 8):
            spread[r, kind] = start(
                (0, 66)[kind] + r, h.at[kind, index_of(r)], g.at[kind, r, 0], same_core_masks(r)
            )
        g[kind, 0, 0] = h[kind, place]
    def gather(stage, rg, kind):
        n = 1 << stage
        group = pl.ds(rg * 2, 2)
        return start(
            8 + stage * 8 + rg * 2 + kind,
            g.at[kind, group, pl.ds(0, n)],
            g.at[kind, group, pl.ds(n, n)],
            STAGES[kind][stage],
        )

    one, two, three = {}, {}, {}
    for kind in range(2):
        for rg in range(4):
            for r in (rg * 2, rg * 2 + 1):
                if r:
                    spread[r, kind].wait_recv()
            one[rg, kind] = gather(0, rg, kind)
    order = [(rg, kind) for rg in range(4) for kind in range(2)]
    for n, key in enumerate(order):
        one[key].wait_recv()
        two[key] = gather(1, *key)
        if n >= 1:
            two[order[n - 1]].wait_recv()
            three[order[n - 1]] = gather(2, *order[n - 1])
    two[order[7]].wait_recv()
    three[order[7]] = gather(2, *order[7])

    def rows_of(r, cols):
        parts = [g[kind, r, :, :, cols].reshape(256, 256) for kind in range(2)]
        return jnp.concatenate(parts, axis=0)

    for copy in loads:
        copy.wait()
    acc[...] = jnp.zeros_like(acc)
    for rg in range(4):
        three[rg, 0].wait_recv()
        three[rg, 1].wait_recv()
        for r in (rg * 2, rg * 2 + 1):
            acc[...] += jnp.dot(
                rows_of(r, pl.ds(0, 256)), w[0, out_place(r, 0)], preferred_element_type=F32
            ) + jnp.dot(
                rows_of(r, pl.ds(256, 256)), w[1, out_place(r, 1)], preferred_element_type=F32
            )
    swaps = []
    for half in range(2):
        rows = pl.ds(half * 256, 256)
        mine[rows] = acc[rows].astype(BF)
        swaps.append(start(56 + half, mine.at[rows], theirs.at[rows], CORE))
    for half in range(2):
        rows = pl.ds(half * 256, 256)
        swaps[half].wait_recv()
        tb[rows] = (mine[rows].astype(F32) + theirs[rows].astype(F32)).astype(BF)

    def scatter(stage, key, src, dst):
        rg, kind = key
        return start(32 + stage * 8 + rg * 2 + kind, src, dst, STAGES[kind][2 - stage])

    one, two, three = {}, {}, {}
    for rg in range(4):
        group = pl.ds(rg * 2, 2)
        for r in (rg * 2, rg * 2 + 1):
            part = lax.dot_general(
                tb[...],
                w[1, out_place(r, 1)],
                (((1,), (1,)), ((), ())),
                preferred_element_type=F32,
            ).astype(BF)
            for kind in range(2):
                cs[kind, r] = part[kind * 256 : kind * 256 + 256].reshape(8, 32, 256)
        for kind in range(2):
            one[rg, kind] = scatter(
                0, (rg, kind), cs.at[kind, group, pl.ds(4, 4)], c1.at[kind, group]
            )

    def added(key, n, ref):
        rg, kind = key
        group = pl.ds(rg * 2, 2)
        cs[kind, group, pl.ds(0, n)] = (
            cs[kind, group, pl.ds(0, n)].astype(F32) + ref[kind, group].astype(F32)
        ).astype(BF)

    def output_grad(r):
        mz, ml = r // 2, r % 2
        block = lax.dot_general(
            rows_of(r, pl.ds(0, 256)),
            tb[...],
            (((0,), (0,)), ((), ())),
            preferred_element_type=F32,
        ).astype(BF)
        for kind in range(2):
            gp[kind, z_place(mz, kind), ml] = block[:, kind * 512 : kind * 512 + 512]

    def second(key):
        rg, kind = key
        one[key].wait_recv()
        added(key, 4, c1)
        group = pl.ds(rg * 2, 2)
        two[key] = scatter(1, key, cs.at[kind, group, pl.ds(2, 2)], c2.at[kind, group])

    def third(key):
        rg, kind = key
        two[key].wait_recv()
        added(key, 2, c2)
        group = pl.ds(rg * 2, 2)
        three[key] = scatter(2, key, cs.at[kind, group, pl.ds(1, 1)], c3.at[kind, group])

    for n, key in enumerate(order):
        second(key)
        if n >= 1:
            third(order[n - 1])
        output_grad(n)
    third(order[7])
    back = {}
    for rg in range(4):
        for kind in range(2):
            three[rg, kind].wait_recv()
            added((rg, kind), 1, c3)
        for r in (rg * 2, rg * 2 + 1):
            if r:
                back[r] = start(r + 58, cs.at[:, r, 0], cot.at[:, place], same_core_masks(r))
    cot[:, place] = cs[:, 0, 0]
    gp_copy = pltpu.make_async_copy(gp, gp_out, load.at[2])
    gp_copy.start()
    for r in range(1, 8):
        back[r].wait_recv()
    for copy in copies:
        copy.wait_send()
    gp_copy.wait()


def output_side(query, tangent, key_states, values, segments, cos_twice, sin_signed, wall):
    shape = jax.ShapeDtypeStruct
    return pl.pallas_call(
        output_kernel,
        out_shape=(
            shape((2, 8, 32, 256), BF),
            shape((2, 4, 2, 256, 512), BF),
            shape((4, 256, 256), F32),
        ),
        in_specs=vmem_specs(7) + any_specs(1),
        out_specs=tuple(vmem_specs(1) + any_specs(1) + vmem_specs(1)),
        scratch_shapes=[
            pltpu.VMEM((2, 8, 32, 512), BF),
            pltpu.VMEM((2, 8, 256, 1024), BF),
            pltpu.VMEM((2, 8, 8, 32, 512), BF),
            pltpu.VMEM((512, 1024), F32),
            pltpu.VMEM((512, 1024), BF),
            pltpu.VMEM((512, 1024), BF),
            pltpu.VMEM((512, 1024), BF),
            pltpu.VMEM((2, 8, 8, 32, 256), BF),
            pltpu.VMEM((2, 8, 4, 32, 256), BF),
            pltpu.VMEM((2, 8, 2, 32, 256), BF),
            pltpu.VMEM((2, 8, 1, 32, 256), BF),
            pltpu.VMEM((2, 4, 2, 256, 512), BF),
            pltpu.SemaphoreType.DMA((3,)),
            pltpu.SemaphoreType.DMA((74,)),
            pltpu.SemaphoreType.DMA((74,)),
        ],
        compiler_params=pltpu.CompilerParams(
            collective_id=3, has_side_effects=True, vmem_limit_bytes=VMEM_BYTES
        ),
        name="output_side",
    )(query, tangent, key_states, values, segments, cos_twice, sin_signed, wall)


def tail_kernel(
    factor, count, normed_hbm, cot_heads, k, v, probs, cos_twice, sin_signed, gp, gram, vec_q, vec_o,
    next_q, next_o, coeffs, cot, normed, part, r1, r2, r3, own, z1, z2, y1, vq, vo, gq, go, facc,
    s1, s2, u1, u2, load, sent, got,
):
    here = position()
    xy_own = here[0] * 4 + here[1] * 2 + here[3]
    zc_own = here[2] * 2 + here[4]
    loads = []

    def fetch(src, dst):
        copy = pltpu.make_async_copy(src, dst, load.at[len(loads)])
        copy.start()
        loads.append(copy)

    fetch(gp, own)
    fetch(normed_hbm, normed)
    greet(here, XY_PEERS + ZC_PEERS)
    greeted(XY_PEERS + ZC_PEERS)
    copies = []

    def keep(copy):
        copies.append(copy)
        return copy

    def rows_at(j):
        return pl.ds(j // 2 * 64, 64)

    def start_out(stage, j, src, dst):
        at = 24 + stage * 8 + j
        masks = ((Z3, Z1)[j % 2], (Z1, Z3)[j % 2], YL)[stage]
        return keep(send(src, dst, sent.at[at], got.at[at], here, masks))

    z_high, z_low, over_y = {}, {}, {}

    def out_high(j):
        kind, rows = j % 2, rows_at(j)
        z_high[j] = start_out(0, j, own.at[kind, pl.ds(2, 2), :, rows], z1.at[kind, :, :, rows])

    def out_low(j):
        kind, rows = j % 2, rows_at(j)
        z_high[j].wait_recv()
        if j + 4 < 8:
            out_high(j + 4)
        own[kind, pl.ds(0, 2), :, rows] = (
            own[kind, pl.ds(0, 2), :, rows].astype(F32) + z1[kind, :, :, rows].astype(F32)
        ).astype(BF)
        z_low[j] = start_out(1, j, own.at[kind, 1, :, rows], z2.at[kind, :, rows])

    def out_y(j):
        kind, rows = j % 2, rows_at(j)
        z_low[j].wait_recv()
        own[kind, 0, :, rows] = (
            own[kind, 0, :, rows].astype(F32) + z2[kind, :, rows].astype(F32)
        ).astype(BF)
        over_y[j] = start_out(2, j, own.at[kind, 0, 1, rows], y1.at[kind, rows])

    def against(g, v, row0, tiles, col0, col_tiles):
        def step(i, state):
            rows = pl.ds(pl.multiple_of(row0 + i * 16, 16), 16)
            for h in range(col_tiles):
                cols = pl.ds(col0 + h * 128, 128)
                here_g = g[rows, cols]
                out = []
                for j in range(K):
                    p = here_g * v[j, rows, cols].astype(F32)
                    out.append(state[j] + (p[:8] + p[8:]))
                state = tuple(out)
            return state

        state = lax.fori_loop(0, tiles, step, tuple(facc[j] for j in range(K)))
        for j in range(K):
            facc[j] = state[j]

    def out_end(j):
        kind, rows = j % 2, rows_at(j)
        over_y[j].wait_recv()
        go[rows, pl.ds(kind * 512, 512)] = own[kind, 0, 0, rows].astype(F32) + y1[
            kind, rows
        ].astype(F32)
        against(go, vo, j // 2 * 64, 4, kind * 512, 4)

    def product(low, mid, high):
        source = dp_source(here, (low, mid, high), STAGES[0])
        cols = pl.ds(pl.multiple_of(source * 1024, 1024), 1024)
        block = jnp.dot(cot[...], normed[:, cols], preferred_element_type=F32) * factor
        block = block.astype(BF)
        for c in range(8):
            place = low + 2 * mid + 4 * high if c % 2 == 0 else high + 2 * mid + 4 * low
            part[c, place] = block[:, c * 128 : (c + 1) * 128]

    def start(stage, c, src, dst):
        at = stage * 8 + c
        return keep(send(src, dst, sent.at[at], got.at[at], here, STAGES[c % 2][2 - stage]))

    one, two, three = {}, {}, {}

    def q_one(c):
        one[c] = start(0, c, part.at[c, pl.ds(4, 4)], r1.at[c])

    loads[0].wait()
    for j in range(4):
        out_high(j)
    attend_back(cot_heads, k, v, probs, cos_twice, sin_signed, cot)
    loads[1].wait()
    fetch(vec_q, vq)
    fetch(vec_o, vo)
    product(1, 0, 1)
    product(1, 1, 1)
    product(0, 0, 1)
    product(0, 1, 1)
    q_one(0)
    q_one(2)
    product(1, 0, 0)
    product(1, 1, 0)
    q_one(1)
    q_one(3)
    product(0, 0, 0)
    product(0, 1, 0)
    facc[...] = jnp.zeros_like(facc)

    def added(c, n, ref):
        part[c, pl.ds(0, n)] = (
            part[c, pl.ds(0, n)].astype(F32) + ref[c].astype(F32)
        ).astype(BF)

    def q_two(c):
        one[c].wait_recv()
        if c + 4 < 8:
            q_one(c + 4)
        added(c, 4, r1)
        two[c] = start(1, c, part.at[c, pl.ds(2, 2)], r2.at[c])

    def q_three(c):
        two[c].wait_recv()
        added(c, 2, r2)
        three[c] = start(2, c, part.at[c, pl.ds(1, 1)], r3.at[c])

    def q_end(c):
        three[c].wait_recv()
        total = part[c, 0].astype(F32) + r3[c, 0].astype(F32)
        gq[pl.ds(c * 128, 128), :] = total.T
        against(gq, vq, c * 128, 8, 0, 2)

    lagged = ((q_two, 0), (q_three, 2), (out_low, 1), (out_y, 3), (q_end, 4), (out_end, 5))
    for n in range(8 + 5):
        if n == 2:
            loads[2].wait()
            loads[3].wait()
        for action, lag in lagged:
            if 0 <= n - lag < 8:
                action(n - lag)

    def exchange(slots, own_slot, peers, base):
        ref = slots.at[own_slot]
        return [
            keep(send(ref, ref, sent.at[base + n], got.at[base + n], here, masks))
            for n, masks in enumerate(peers)
        ]

    def sum_over(over_xy, over_zc, base):
        for copy in exchange(over_xy, xy_own, XY_PEERS, base):
            copy.wait_recv()
        total = over_xy[0]
        for n in range(1, 16):
            total = total + over_xy[n]
        over_zc[zc_own] = total
        for copy in exchange(over_zc, zc_own, ZC_PEERS, base + 15):
            copy.wait_recv()
        total = over_zc[0]
        for n in range(1, 8):
            total = total + over_zc[n]
        return total

    for j in range(K):
        s1[xy_own, pl.ds(j, 1)] = jnp.sum(facc[j], axis=0, keepdims=True)
    first = jnp.sum(sum_over(s1, s2, 48), axis=1, keepdims=True) / count
    second = first
    for i in range(K):
        second = second - gram[:, pl.ds(i, 1)] * first[i : i + 1]
    both = first + second
    weights = [jnp.broadcast_to(both[j : j + 1], (16, 128)) for j in range(K)]

    def cleaned(g, v, c, row_tiles, col_tiles, state):
        def step(r, state):
            rows = pl.ds(pl.multiple_of(r * 16, 16), 16)
            for h in range(col_tiles):
                cols = pl.ds(h * 128, 128)
                value = g[rows, cols]
                for j in range(K):
                    value = value - weights[j] * v[j, rows, cols].astype(F32)
                c[rows, cols] = value
                p = value * value
                state = state + (p[:8] + p[8:])
            return state

        return lax.fori_loop(0, row_tiles, step, state)

    state = cleaned(gq, vq, gq, 64, 2, jnp.zeros((8, 128), F32))
    u1[xy_own] = cleaned(go, vo, go, 16, 8, state)
    squares = sum_over(u1, u2, 70)
    squares = jnp.sum(jnp.sum(squares, axis=1, keepdims=True), axis=0, keepdims=True) / count
    beta = jnp.sqrt(squares + BETA_EPS)
    scale = 1.0 / beta
    next_q[...] = (gq[...] * scale).astype(BF)
    next_o[...] = (go[...] * scale).astype(BF)
    coeffs[pl.ds(0, 8)] = jnp.broadcast_to(both, (8, 128))
    coeffs[pl.ds(8, 8)] = jnp.broadcast_to(beta, (8, 128))
    for copy in copies:
        copy.wait_send()


def tail(
    normed, cot_heads, key_states, values, probs, cos_twice, sin_signed,
    partials, gram, basis_query, basis_output, factor, count,
):
    shape = jax.ShapeDtypeStruct
    return pl.pallas_call(
        functools.partial(tail_kernel, factor, count),
        out_shape=(shape((1024, 256), BF), shape((256, 1024), BF), shape((16, 128), F32)),
        in_specs=any_specs(1) + vmem_specs(6) + any_specs(1) + vmem_specs(1) + any_specs(2),
        out_specs=tuple(vmem_specs(3)),
        scratch_shapes=[
            pltpu.VMEM((256, 512), BF),
            pltpu.VMEM((512, D), BF),
            pltpu.VMEM((8, 8, 256, 128), BF),
            pltpu.VMEM((8, 4, 256, 128), BF),
            pltpu.VMEM((8, 2, 256, 128), BF),
            pltpu.VMEM((8, 1, 256, 128), BF),
            pltpu.VMEM((2, 4, 2, 256, 512), BF),
            pltpu.VMEM((2, 2, 2, 256, 512), BF),
            pltpu.VMEM((2, 2, 256, 512), BF),
            pltpu.VMEM((2, 256, 512), BF),
            pltpu.VMEM((K, 1024, 256), BF),
            pltpu.VMEM((K, 256, 1024), BF),
            pltpu.VMEM((1024, 256), F32),
            pltpu.VMEM((256, 1024), F32),
            pltpu.VMEM((K, 8, 128), F32),
            pltpu.VMEM((16, 8, 128), F32),
            pltpu.VMEM((8, 8, 128), F32),
            pltpu.VMEM((16, 8, 128), F32),
            pltpu.VMEM((8, 8, 128), F32),
            pltpu.SemaphoreType.DMA((4,)),
            pltpu.SemaphoreType.DMA((92,)),
            pltpu.SemaphoreType.DMA((92,)),
        ],
        compiler_params=pltpu.CompilerParams(
            collective_id=1, has_side_effects=True, vmem_limit_bytes=VMEM_BYTES
        ),
        name="tail",
    )(
        normed, cot_heads, key_states, values, probs, cos_twice, sin_signed,
        partials, gram, basis_query, basis_output,
    )


def finish_kernel(q, o, lines, q_out, o_out, coeffs):
    q_out[...] = q[...]
    o_out[...] = o[...]
    for n in range(K + 1):
        coeffs[n] = lines[n, 0]


def finish(next_query, next_output, lines):
    shape = jax.ShapeDtypeStruct
    return pl.pallas_call(
        finish_kernel,
        out_shape=(shape((1024, 256), BF), shape((256, 1024), BF), shape((K + 1,), F32)),
        in_specs=vmem_specs(2) + [pl.BlockSpec(memory_space=pltpu.SMEM)],
        out_specs=tuple(vmem_specs(2) + [pl.BlockSpec(memory_space=pltpu.SMEM)]),
        name="finish",
    )(next_query, next_output, lines)


def body(tokens, segments, norm_gain, q_weight, kv_weight, o_weight, basis_query, basis_output):
    groups = lax.axis_size(DP)
    seq_count, length, model_width = tokens.shape
    row_count = seq_count * length
    qwidth = QH * HD
    query_scale = D ** (-0.5)
    gn_scale = qwidth / (row_count * groups)
    param_count = 2.0 * D * qwidth
    query, tangent, key_states, values, normed, gram, wall = project(
        tokens.reshape(row_count, model_width),
        norm_gain.reshape(1, model_width),
        q_weight,
        basis_query,
        kv_weight,
        basis_output,
        o_weight,
        param_count,
    )
    cos_twice, sin_signed = (jnp.asarray(table) for table in rope_tables(length, HD))
    cot_heads, partials, probs = output_side(
        query, tangent, key_states, values, segments, cos_twice, sin_signed, wall
    )
    next_query, next_output, lines = tail(
        normed,
        cot_heads,
        key_states,
        values,
        probs,
        cos_twice,
        sin_signed,
        partials,
        gram,
        basis_query,
        basis_output,
        gn_scale * query_scale,
        param_count,
    )
    return finish(next_query, next_output, lines)


def solution(mesh):
    finer = Mesh(
        mesh.devices.reshape(4, 2, 4, 2, 2), ("dp_0", "dp_1", "tensor_0", "tensor_1", "tensor_2")
    )
    placed = (
        P(DP, None, None),
        P(DP, None),
        P(),
        P(DP, TENSOR),
        P(None, DP, None),
        P(TENSOR, DP),
        P(None, DP, TENSOR),
        P(None, TENSOR, DP),
    )
    return jax.shard_map(
        body,
        mesh=finer,
        in_specs=placed,
        out_specs=(P(DP, TENSOR), P(TENSOR, DP), P()),
        check_vma=False,
    )
```

```python
import functools
import math

import jax
import jax.numpy as jnp
import numpy as np
from jax import lax
from jax.experimental import pallas as pl
from jax.experimental.pallas import tpu as pltpu
from jax.sharding import Mesh
from jax.sharding import PartitionSpec as P

D = 8192
HD = 128
QH = 32
KVH = 4
K = 8
DP = ("dp_0", "dp_1")
TENSOR = ("tensor_0", "tensor_1", "tensor_2")
DP_TENSOR = ("dp_0", "dp_1", "tensor_0", "tensor_1", "tensor_2")


PRECISE = lax.Precision.HIGHEST
ROPE_BASE = 500000.0
NORM_EPS = 1e-05
BETA_EPS = 1e-06


MESH = pl.DeviceIdType.MESH
VMEM_BYTES = 58 * 1024 * 1024
X1, X3, X2, YH = (1, 0, 0, 0, 0), (3, 0, 0, 0, 0), (2, 0, 0, 0, 0), (0, 1, 0, 0, 0)
Z1, Z3, YL, CORE = (0, 0, 1, 0, 0), (0, 0, 3, 0, 0), (0, 0, 0, 1, 0), (0, 0, 0, 0, 1)
BF = jnp.bfloat16
F32 = jnp.float32


def position():
    return [lax.axis_index(a) for a in DP_TENSOR]


def flipped(value, mask):
    if mask == 0:
        return value
    if mask == 1:
        return value + 1 - 2 * lax.rem(value, 2)
    if mask == 2:
        return lax.rem(value + 2, 4)
    return 3 - value


def peer(here, masks):
    return tuple(flipped(v, m) for v, m in zip(here, masks))


def greet(here, peers):
    barrier = pltpu.get_barrier_semaphore()
    for masks in peers:
        pl.semaphore_signal(barrier, inc=1, device_id=peer(here, masks), device_id_type=MESH)


def greeted(peers):
    pl.semaphore_wait(pltpu.get_barrier_semaphore(), len(peers))


def send(src, dst, send_sem, recv_sem, here, masks):
    copy = pltpu.make_async_remote_copy(
        src_ref=src,
        dst_ref=dst,
        send_sem=send_sem,
        recv_sem=recv_sem,
        device_id=peer(here, masks),
        device_id_type=MESH,
    )
    copy.start()
    return copy


def dp_source(here, bits, stages):
    x, yh = here[0], here[1]
    for bit, masks in zip(bits, stages):
        if masks[0] == 1:
            x = x + bit * (1 - 2 * lax.rem(x, 2))
        elif masks[0] == 3:
            x = x + bit * (3 - 2 * x)
        else:
            yh = yh + bit * (1 - 2 * yh)
    return x * 2 + yh


STAGES = ((X1, YH, X3), (X3, YH, X1))
IN_STAGES = ((X1, YH, X3), (X3, YH, X1), (X1, YH, X3), (X3, YH, X1))
OUT_STAGES = ((YL, Z1, Z3), (YL, Z3, Z1))


XY_PEERS = [
    (x, yh, 0, yl, 0) for x in range(4) for yh in range(2) for yl in range(2) if x or yh or yl
]
ZC_PEERS = [(0, 0, z, 0, c) for z in range(4) for c in range(2) if z or c]


def z_place(mask, kind):
    one, three = {0: (0, 0), 1: (1, 0), 3: (0, 1), 2: (1, 1)}[mask]
    return one + 2 * three if kind == 0 else three + 2 * one


def out_place(r, kind):
    mz, ml = r // 2, r % 2
    return ml + 2 * z_place(mz, kind)


def same_core_masks(r):
    return (0, 0, r // 2, r % 2, 0)


def rope_tables(length, head_width):
    half_width = head_width // 2
    frequency = np.exp(
        np.arange(half_width, dtype=np.float32) * np.float32(-2.0 * math.log(ROPE_BASE) / head_width)
    ).astype(np.float32)
    angles = np.arange(length, dtype=np.float32)[:, None] * frequency[None, :]
    cosine, sine = np.cos(angles), np.sin(angles)
    return (np.concatenate([cosine, cosine], axis=1), np.concatenate([-sine, sine], axis=1))


def rotated(vectors, cos_twice, sin_signed):
    return vectors * cos_twice + pltpu.roll(vectors, HD // 2, 1) * sin_signed


def rotated_back(vectors, cos_twice, sin_signed):
    return vectors * cos_twice - pltpu.roll(vectors, HD // 2, 1) * sin_signed


def dot_wide(a, b, a_dim, b_dim):
    return lax.dot_general(
        a, b, (((a_dim,), (b_dim,)), ((), ())), precision=PRECISE, preferred_element_type=F32
    )


def attend_both(s, q, t, k, v, segments, cos_twice, sin_signed, h, probs):
    scale = HD ** (-0.5)
    rows = pl.ds(s * 256, 256)
    keys = rotated(k[rows].astype(F32), cos_twice[...], sin_signed[...])
    values = v[rows].astype(F32)
    across = jnp.broadcast_to(segments[pl.ds(s, 1)].astype(F32), (256, 256))
    row = lax.broadcasted_iota(jnp.int32, (256, 256), 0)
    column = lax.broadcasted_iota(jnp.int32, (256, 256), 1)
    mask = jnp.logical_and(across == across.T, row >= column)
    for head in range(2):
        cols = pl.ds(head * HD, HD)
        moving = rotated(q[rows, cols].astype(F32), cos_twice[...], sin_signed[...])
        along = rotated(t[rows, cols].astype(F32), cos_twice[...], sin_signed[...])
        scores = jnp.where(mask, dot_wide(moving, keys, 1, 1) * scale, -1e30)
        weights = jnp.exp(scores - jnp.max(scores, axis=1, keepdims=True))
        p = weights / jnp.sum(weights, axis=1, keepdims=True)
        probs[2 * s + head] = p
        slope = jnp.where(mask, dot_wide(along, keys, 1, 1) * scale, 0.0)
        dp = p * (slope - jnp.sum(p * slope, axis=1, keepdims=True))
        heads = dot_wide(p, values, 1, 0).astype(BF).astype(F32) * ((QH * HD) ** (-0.5))
        tangents = dot_wide(dp, values, 1, 0)
        h[s, :, :, cols] = heads.astype(BF).reshape(8, 32, HD)
        h[s, :, :, pl.ds(256 + head * HD, HD)] = tangents.astype(BF).reshape(8, 32, HD)


def attend_back(cot, k, v, probs, cos_twice, sin_signed, out):
    scale = HD ** (-0.5)
    for s in range(2):
        rows = pl.ds(s * 256, 256)
        keys = rotated(k[rows].astype(F32), cos_twice[...], sin_signed[...])
        values = v[rows].astype(F32)
        for head in range(2):
            cols = pl.ds(head * HD, HD)
            given = cot[s, :, :, cols].reshape(256, HD).astype(F32)
            p = probs[2 * s + head]
            slope = dot_wide(given, values, 1, 1)
            ds = p * (slope - jnp.sum(p * slope, axis=1, keepdims=True))
            moving = rotated_back(dot_wide(ds, keys, 1, 0) * scale, cos_twice[...], sin_signed[...])
            out[cols, rows] = moving.T.astype(BF)


SUPER = (0, 1) * 4 + (2, 3) * 4
PIECE = (0, 0, 1, 1, 2, 2, 3, 3) * 2


def project_kernel(
    count, tok, gain, q_w, vec_q, kv_w, vec_o, o_w,
    q_out, t_out, k_out, v_out, normed_out, gram_out, wall,
    x, buf, acc, mine, theirs, vq, vo, w, g1, g2, pairs_acc, load, sent, got,
):
    here = position()
    core = here[4]
    kv_head = here[2]
    for_rows = []
    for s in range(4):
        rows = pl.ds(s * 256, 256)
        kv_cols = pl.ds(pl.multiple_of(kv_head * HD, HD), HD)
        parts = (
            (q_w.at[rows], buf.at[s, 0, :, pl.ds(0, 256)]),
            (vec_q.at[K - 1, rows], buf.at[s, 0, :, pl.ds(256, 256)]),
            (kv_w.at[core, rows, kv_cols], buf.at[s, 0, :, pl.ds(512, 128)]),
        )
        for n, (src, dst) in enumerate(parts):
            copy = pltpu.make_async_copy(src, dst, load.at[3 * s + n])
            copy.start()
            for_rows.append(copy)
    own_out = []
    for kind, src in enumerate((vec_o.at[K - 1], o_w)):
        copy = pltpu.make_async_copy(src, w.at[kind, 0], load.at[16 + kind])
        copy.start()
        own_out.append(copy)
    greet(here, XY_PEERS + ZC_PEERS)
    greeted(XY_PEERS + ZC_PEERS)
    for copy in for_rows:
        copy.wait()

    def start_stage(stage, k):
        s, rows = SUPER[k], pl.ds(PIECE[k] * 64, 64)
        n = 1 << stage
        at = stage * 16 + k
        return send(
            buf.at[s, pl.ds(0, n), rows],
            buf.at[s, pl.ds(n, n), rows],
            sent.at[at],
            got.at[at],
            here,
            IN_STAGES[s][stage],
        )

    out_copies = {}

    def start_out(stage, kind, piece):
        n = 1 << stage
        rows = pl.ds(piece * 64, 64)
        at = 49 + stage * 8 + kind * 4 + piece
        out_copies[stage, kind, piece] = send(
            w.at[kind, pl.ds(0, n), rows],
            w.at[kind, pl.ds(n, n), rows],
            sent.at[at],
            got.at[at],
            here,
            OUT_STAGES[kind][stage],
        )

    def next_out(stage, piece):
        for kind in range(2):
            out_copies[stage, kind, piece].wait_recv()
            start_out(stage + 1, kind, piece)

    for copy in own_out:
        copy.wait()
    for piece in range(2):
        for kind in range(2):
            start_out(0, kind, piece)
    first = [start_stage(0, k) for k in range(6)]
    tok_copy = pltpu.make_async_copy(tok, x, load.at[12])
    tok_copy.start()
    vq_copy = pltpu.make_async_copy(vec_q, vq, load.at[13])
    vq_copy.start()
    vo_copy = pltpu.make_async_copy(vec_o, vo, load.at[14])
    vo_copy.start()
    wall_copies = []

    def keep_wall(kind, lo):
        copy = pltpu.make_async_copy(
            w.at[kind, pl.ds(lo, 4)], wall.at[kind, pl.ds(lo, 4)], load.at[18 + kind + lo // 2]
        )
        copy.start()
        wall_copies.append(copy)

    xy_own = here[0] * 4 + here[1] * 2 + here[3]
    zc_own = here[2] * 2 + here[4]

    def exchange(slots, own, peers, base):
        ref = slots.at[own]
        return [
            send(ref, ref, sent.at[base + n], got.at[base + n], here, masks)
            for n, masks in enumerate(peers)
        ]

    def norm_rows(lo, hi):
        def step(i, carry):
            rows = pl.ds(pl.multiple_of(i * 16, 16), 16)
            total = jnp.zeros((16, 1), F32)
            for c in range(8):
                part = x[rows, pl.ds(c * 1024, 1024)].astype(F32)
                total += jnp.sum(part * part, axis=1, keepdims=True)
            inv = lax.rsqrt(total / D + NORM_EPS)
            for c in range(8):
                cols = pl.ds(c * 1024, 1024)
                x[rows, cols] = (x[rows, cols].astype(F32) * inv * gain[:, cols]).astype(BF)
            return carry

        lax.fori_loop(lo // 16, hi // 16, step, 0)

    def dots(s, lo, hi):
        def step(p, carry):
            bits = (lax.rem(p, 2), lax.rem(p // 2, 2), p // 4)
            source = dp_source(here, bits, IN_STAGES[s])
            cols = pl.ds(pl.multiple_of(source * 1024 + s * 256, 256), 256)
            acc[...] += jnp.dot(x[:, cols], buf[s, p], preferred_element_type=F32)
            return carry

        lax.fori_loop(lo, hi, step, 0)

    pairs = [(i, j) for i in range(K) for j in range(i, K)]

    def gram(part):
        def tile(ref, rows, cols, carry):
            b = [ref[j, rows, cols].astype(F32) for j in range(K)]
            out = []
            for (i, j), a in zip(pairs, carry):
                p = b[i] * b[j]
                out.append(a + (p[:8] + p[8:]))
            return tuple(out)

        def step_q(r, carry):
            rows = pl.ds(pl.multiple_of(r * 16, 16), 16)
            for h in range(2):
                carry = tile(vq, rows, pl.ds(h * 128, 128), carry)
            return carry

        def step_o(r, carry):
            rows = pl.ds(pl.multiple_of(r * 16, 16), 16)
            for h in range(8):
                carry = tile(vo, rows, pl.ds(h * 128, 128), carry)
            return carry

        carry = tuple(pairs_acc[n] for n in range(len(pairs)))
        carry = lax.fori_loop(part * 8, part * 8 + 8, step_q, carry)
        carry = lax.fori_loop(part * 2, part * 2 + 2, step_o, carry)
        for n, a in enumerate(carry):
            pairs_acc[n] = a

    def gram_end():
        lane = lax.broadcasted_iota(jnp.int32, (8, 128), 1)
        row = lax.broadcasted_iota(jnp.int32, (8, 128), 0)
        tile_sum = jnp.zeros((8, 128), F32)
        for n, (i, j) in enumerate(pairs):
            value = jnp.sum(
                jnp.sum(pairs_acc[n], axis=0, keepdims=True), axis=1, keepdims=True
            )
            hit = jnp.logical_or(
                jnp.logical_and(lane == i, row == j), jnp.logical_and(lane == j, row == i)
            )
            tile_sum = tile_sum + jnp.where(hit, value, 0.0)
        g1[xy_own] = tile_sum

    acc[...] = jnp.zeros_like(acc)
    pairs_acc[...] = jnp.zeros_like(pairs_acc)
    second, third = [], []
    out_steps = {
        1: (0, 0), 2: (0, 1), 4: (0, 2), 6: (0, 3), 3: (1, 0), 5: (1, 1), 7: (1, 2), 9: (1, 3)
    }
    for k in range(16):
        first[k].wait_recv()
        second.append(start_stage(1, k))
        if k + 6 < 16:
            first.append(start_stage(0, k + 6))
        if k >= 3:
            second[k - 3].wait_recv()
            third.append(start_stage(2, k - 3))
        if k in out_steps:
            stage, piece = out_steps[k]
            next_out(stage, piece)
        if k in (1, 3):
            start_out(0, 0, k // 2 + 2)
            start_out(0, 1, k // 2 + 2)
        if k == 0:
            tok_copy.wait()
        if k < 8:
            norm_rows(k * 64, k * 64 + 64)
        if k == 7:
            out_copy = pltpu.make_async_copy(x, normed_out, load.at[15])
            out_copy.start()
        if k == 2:
            vq_copy.wait()
            vo_copy.wait()
        if 2 <= k < 10:
            gram(k - 2)
        if k == 10:
            gram_end()
            over_xy = exchange(g1, xy_own, XY_PEERS, 73)
        if k == 11:
            dots(0, 0, 4)
        if k == 12:
            dots(1, 0, 4)
        if k == 13:
            keep_wall(0, 0)
            keep_wall(1, 0)
            for copy in over_xy:
                copy.wait_recv()
            total = g1[0]
            for n in range(1, 16):
                total = total + g1[n]
            g2[zc_own] = total
            over_zc = exchange(g2, zc_own, ZC_PEERS, 88)
        if k == 13:
            for n in (0, 2, 4, 6):
                third[n].wait_recv()
            dots(0, 4, 8)
        if k == 14:
            for n in (1, 3, 5, 7):
                third[n].wait_recv()
            dots(1, 4, 8)
    for k in range(16 - 3, 16):
        second[k].wait_recv()
        third.append(start_stage(2, k))
    dots(2, 0, 4)
    dots(3, 0, 4)
    for s in (2, 3):
        for n in range(8, 16):
            if SUPER[n] == s:
                third[n].wait_recv()
        dots(s, 4, 8)
    mine[...] = acc[:, pl.ds(512, 128)].astype(BF)
    swap = send(mine, theirs, sent.at[48], got.at[48], here, CORE)
    q_out[...] = acc[:, pl.ds(0, 256)].astype(BF)
    t_out[...] = (acc[:, pl.ds(256, 256)] * (D ** (-0.5))).astype(BF)
    swap.wait()
    own = mine[...].astype(F32)
    other = theirs[...].astype(F32)
    first_core = core == 0
    k_out[...] = jnp.where(first_core, own, other).astype(BF)
    v_out[...] = jnp.where(first_core, other, own).astype(BF)
    for kind in range(2):
        for piece in range(4):
            out_copies[2, kind, piece].wait_recv()
        keep_wall(kind, 4)
    for copy in over_zc:
        copy.wait_recv()
    total = g2[0]
    for n in range(1, 8):
        total = total + g2[n]
    gram_out[...] = total / count
    for copy in first + second + third + list(out_copies.values()) + over_xy + over_zc:
        copy.wait_send()
    for copy in wall_copies:
        copy.wait()
    out_copy.wait()


def any_specs(n):
    return [pl.BlockSpec(memory_space=pl.ANY) for _ in range(n)]


def vmem_specs(n):
    return [pl.BlockSpec(memory_space=pltpu.VMEM) for _ in range(n)]


def project(tokens, norm_gain, q_weight, basis_query, kv_weight, basis_output, o_weight, count):
    shape = jax.ShapeDtypeStruct
    return pl.pallas_call(
        functools.partial(project_kernel, count),
        out_shape=(
            shape((512, 256), BF),
            shape((512, 256), BF),
            shape((512, HD), BF),
            shape((512, HD), BF),
            shape((512, D), BF),
            shape((8, 128), F32),
            shape((2, 8, 256, 1024), BF),
        ),
        in_specs=any_specs(1) + vmem_specs(1) + any_specs(5),
        out_specs=tuple(vmem_specs(4) + any_specs(1) + vmem_specs(1) + any_specs(1)),
        scratch_shapes=[
            pltpu.VMEM((512, D), BF),
            pltpu.VMEM((4, 8, 256, 640), BF),
            pltpu.VMEM((512, 640), F32),
            pltpu.VMEM((512, HD), BF),
            pltpu.VMEM((512, HD), BF),
            pltpu.VMEM((K, 1024, 256), BF),
            pltpu.VMEM((K, 256, 1024), BF),
            pltpu.VMEM((2, 8, 256, 1024), BF),
            pltpu.VMEM((16, 8, 128), F32),
            pltpu.VMEM((8, 8, 128), F32),
            pltpu.VMEM((36, 8, 128), F32),
            pltpu.SemaphoreType.DMA((22,)),
            pltpu.SemaphoreType.DMA((95,)),
            pltpu.SemaphoreType.DMA((95,)),
        ],
        compiler_params=pltpu.CompilerParams(
            collective_id=0, has_side_effects=True, vmem_limit_bytes=VMEM_BYTES
        ),
        name="project",
    )(tokens, norm_gain, q_weight, basis_query, kv_weight, basis_output, o_weight)


def output_kernel(
    q, t, k, v, segments, cos_twice, sin_signed, wall, cot, gp_out, probs,
    h, w, g, acc, tb, mine, theirs, cs, c1, c2, c3, gp, load, sent, got,
):
    here = position()
    place = here[2] * 2 + here[3]
    loads = []
    for kind in (0, 1):
        copy = pltpu.make_async_copy(wall.at[kind], w.at[kind], load.at[kind])
        copy.start()
        loads.append(copy)
    peers = [X1, X3, YH, CORE] + [same_core_masks(r) for r in range(1, 8)]
    greet(here, peers)
    copies = []

    def start(at, src, dst, masks):
        copy = send(src, dst, sent.at[at], got.at[at], here, masks)
        copies.append(copy)
        return copy

    def index_of(r):
        z, yl = peer(here[2:4], same_core_masks(r)[2:4])
        return z * 2 + yl

    spread = {}
    for kind in range(2):
        attend_both(kind, q, t, k, v, segments, cos_twice, sin_signed, h, probs)
        if kind == 0:
            greeted(peers)
        for r in range(1, 8):
            spread[r, kind] = start(
                (0, 66)[kind] + r, h.at[kind, index_of(r)], g.at[kind, r, 0], same_core_masks(r)
            )
        g[kind, 0, 0] = h[kind, place]
    def gather(stage, rg, kind):
        n = 1 << stage
        group = pl.ds(rg * 2, 2)
        return start(
            8 + stage * 8 + rg * 2 + kind,
            g.at[kind, group, pl.ds(0, n)],
            g.at[kind, group, pl.ds(n, n)],
            STAGES[kind][stage],
        )

    one, two, three = {}, {}, {}
    for kind in range(2):
        for rg in range(4):
            for r in (rg * 2, rg * 2 + 1):
                if r:
                    spread[r, kind].wait_recv()
            one[rg, kind] = gather(0, rg, kind)
    order = [(rg, kind) for rg in range(4) for kind in range(2)]
    for n, key in enumerate(order):
        one[key].wait_recv()
        two[key] = gather(1, *key)
        if n >= 3:
            two[order[n - 3]].wait_recv()
            three[order[n - 3]] = gather(2, *order[n - 3])
    for key in order[8 - 3 :]:
        two[key].wait_recv()
        three[key] = gather(2, *key)

    def rows_of(r, cols):
        parts = [g[kind, r, :, :, cols].reshape(256, 256) for kind in range(2)]
        return jnp.concatenate(parts, axis=0)

    for copy in loads:
        copy.wait()
    acc[...] = jnp.zeros_like(acc)
    for rg in range(4):
        three[rg, 0].wait_recv()
        three[rg, 1].wait_recv()
        for r in (rg * 2, rg * 2 + 1):
            acc[...] += jnp.dot(
                rows_of(r, pl.ds(0, 256)), w[0, out_place(r, 0)], preferred_element_type=F32
            ) + jnp.dot(
                rows_of(r, pl.ds(256, 256)), w[1, out_place(r, 1)], preferred_element_type=F32
            )
    swaps = []
    for half in range(2):
        rows = pl.ds(half * 256, 256)
        mine[rows] = acc[rows].astype(BF)
        swaps.append(start(56 + half, mine.at[rows], theirs.at[rows], CORE))
    for half in range(2):
        rows = pl.ds(half * 256, 256)
        swaps[half].wait_recv()
        tb[rows] = (mine[rows].astype(F32) + theirs[rows].astype(F32)).astype(BF)

    def scatter(stage, key, src, dst):
        rg, kind = key
        return start(32 + stage * 8 + rg * 2 + kind, src, dst, STAGES[kind][2 - stage])

    one, two, three = {}, {}, {}
    for rg in range(4):
        group = pl.ds(rg * 2, 2)
        for r in (rg * 2, rg * 2 + 1):
            part = lax.dot_general(
                tb[...],
                w[1, out_place(r, 1)],
                (((1,), (1,)), ((), ())),
                preferred_element_type=F32,
            ).astype(BF)
            for kind in range(2):
                cs[kind, r] = part[kind * 256 : kind * 256 + 256].reshape(8, 32, 256)
        for kind in range(2):
            one[rg, kind] = scatter(
                0, (rg, kind), cs.at[kind, group, pl.ds(4, 4)], c1.at[kind, group]
            )

    def added(key, n, ref):
        rg, kind = key
        group = pl.ds(rg * 2, 2)
        cs[kind, group, pl.ds(0, n)] = (
            cs[kind, group, pl.ds(0, n)].astype(F32) + ref[kind, group].astype(F32)
        ).astype(BF)

    def output_grad(r):
        mz, ml = r // 2, r % 2
        block = lax.dot_general(
            rows_of(r, pl.ds(0, 256)),
            tb[...],
            (((0,), (0,)), ((), ())),
            preferred_element_type=F32,
        ).astype(BF)
        for kind in range(2):
            gp[kind, z_place(mz, kind), ml] = block[:, kind * 512 : kind * 512 + 512]

    def second(key):
        rg, kind = key
        one[key].wait_recv()
        added(key, 4, c1)
        group = pl.ds(rg * 2, 2)
        two[key] = scatter(1, key, cs.at[kind, group, pl.ds(2, 2)], c2.at[kind, group])

    def third(key):
        rg, kind = key
        two[key].wait_recv()
        added(key, 2, c2)
        group = pl.ds(rg * 2, 2)
        three[key] = scatter(2, key, cs.at[kind, group, pl.ds(1, 1)], c3.at[kind, group])

    for n, key in enumerate(order):
        second(key)
        if n >= 3:
            third(order[n - 3])
        output_grad(n)
    for key in order[8 - 3 :]:
        third(key)
    back = {}
    for rg in range(4):
        for kind in range(2):
            three[rg, kind].wait_recv()
            added((rg, kind), 1, c3)
        for r in (rg * 2, rg * 2 + 1):
            if r:
                back[r] = start(r + 58, cs.at[:, r, 0], cot.at[:, place], same_core_masks(r))
    cot[:, place] = cs[:, 0, 0]
    gp_copy = pltpu.make_async_copy(gp, gp_out, load.at[2])
    gp_copy.start()
    for r in range(1, 8):
        back[r].wait_recv()
    for copy in copies:
        copy.wait_send()
    gp_copy.wait()


def output_side(query, tangent, key_states, values, segments, cos_twice, sin_signed, wall):
    shape = jax.ShapeDtypeStruct
    return pl.pallas_call(
        output_kernel,
        out_shape=(
            shape((2, 8, 32, 256), BF),
            shape((2, 4, 2, 256, 512), BF),
            shape((4, 256, 256), F32),
        ),
        in_specs=vmem_specs(7) + any_specs(1),
        out_specs=tuple(vmem_specs(1) + any_specs(1) + vmem_specs(1)),
        scratch_shapes=[
            pltpu.VMEM((2, 8, 32, 512), BF),
            pltpu.VMEM((2, 8, 256, 1024), BF),
            pltpu.VMEM((2, 8, 8, 32, 512), BF),
            pltpu.VMEM((512, 1024), F32),
            pltpu.VMEM((512, 1024), BF),
            pltpu.VMEM((512, 1024), BF),
            pltpu.VMEM((512, 1024), BF),
            pltpu.VMEM((2, 8, 8, 32, 256), BF),
            pltpu.VMEM((2, 8, 4, 32, 256), BF),
            pltpu.VMEM((2, 8, 2, 32, 256), BF),
            pltpu.VMEM((2, 8, 1, 32, 256), BF),
            pltpu.VMEM((2, 4, 2, 256, 512), BF),
            pltpu.SemaphoreType.DMA((3,)),
            pltpu.SemaphoreType.DMA((74,)),
            pltpu.SemaphoreType.DMA((74,)),
        ],
        compiler_params=pltpu.CompilerParams(
            collective_id=3, has_side_effects=True, vmem_limit_bytes=VMEM_BYTES
        ),
        name="output_side",
    )(query, tangent, key_states, values, segments, cos_twice, sin_signed, wall)


def tail_kernel(
    factor, count, normed_hbm, cot_heads, k, v, probs, cos_twice, sin_signed, gp, gram, vec_q, vec_o,
    next_q, next_o, coeffs, cot, normed, part, r1, r2, r3, own, z1, z2, y1, vq, vo, gq, go, facc,
    s1, s2, u1, u2, load, sent, got,
):
    here = position()
    xy_own = here[0] * 4 + here[1] * 2 + here[3]
    zc_own = here[2] * 2 + here[4]
    loads = []

    def fetch(src, dst):
        copy = pltpu.make_async_copy(src, dst, load.at[len(loads)])
        copy.start()
        loads.append(copy)

    fetch(gp, own)
    fetch(normed_hbm, normed)
    greet(here, XY_PEERS + ZC_PEERS)
    greeted(XY_PEERS + ZC_PEERS)
    copies = []

    def keep(copy):
        copies.append(copy)
        return copy

    def rows_at(j):
        return pl.ds(j // 2 * 64, 64)

    def start_out(stage, j, src, dst):
        at = 24 + stage * 8 + j
        masks = ((Z3, Z1)[j % 2], (Z1, Z3)[j % 2], YL)[stage]
        return keep(send(src, dst, sent.at[at], got.at[at], here, masks))

    z_high, z_low, over_y = {}, {}, {}

    def out_high(j):
        kind, rows = j % 2, rows_at(j)
        z_high[j] = start_out(0, j, own.at[kind, pl.ds(2, 2), :, rows], z1.at[kind, :, :, rows])

    def out_low(j):
        kind, rows = j % 2, rows_at(j)
        z_high[j].wait_recv()
        if j + 4 < 8:
            out_high(j + 4)
        own[kind, pl.ds(0, 2), :, rows] = (
            own[kind, pl.ds(0, 2), :, rows].astype(F32) + z1[kind, :, :, rows].astype(F32)
        ).astype(BF)
        z_low[j] = start_out(1, j, own.at[kind, 1, :, rows], z2.at[kind, :, rows])

    def out_y(j):
        kind, rows = j % 2, rows_at(j)
        z_low[j].wait_recv()
        own[kind, 0, :, rows] = (
            own[kind, 0, :, rows].astype(F32) + z2[kind, :, rows].astype(F32)
        ).astype(BF)
        over_y[j] = start_out(2, j, own.at[kind, 0, 1, rows], y1.at[kind, rows])

    def against(g, v, row0, tiles, col0, col_tiles):
        def step(i, state):
            rows = pl.ds(pl.multiple_of(row0 + i * 16, 16), 16)
            for h in range(col_tiles):
                cols = pl.ds(col0 + h * 128, 128)
                here_g = g[rows, cols]
                out = []
                for j in range(K):
                    p = here_g * v[j, rows, cols].astype(F32)
                    out.append(state[j] + (p[:8] + p[8:]))
                state = tuple(out)
            return state

        state = lax.fori_loop(0, tiles, step, tuple(facc[j] for j in range(K)))
        for j in range(K):
            facc[j] = state[j]

    def out_end(j):
        kind, rows = j % 2, rows_at(j)
        over_y[j].wait_recv()
        go[rows, pl.ds(kind * 512, 512)] = own[kind, 0, 0, rows].astype(F32) + y1[
            kind, rows
        ].astype(F32)
        against(go, vo, j // 2 * 64, 4, kind * 512, 4)

    def product(low, mid, high):
        source = dp_source(here, (low, mid, high), STAGES[0])
        cols = pl.ds(pl.multiple_of(source * 1024, 1024), 1024)
        block = jnp.dot(cot[...], normed[:, cols], preferred_element_type=F32) * factor
        block = block.astype(BF)
        for c in range(8):
            place = low + 2 * mid + 4 * high if c % 2 == 0 else high + 2 * mid + 4 * low
            part[c, place] = block[:, c * 128 : (c + 1) * 128]

    def start(stage, c, src, dst):
        at = stage * 8 + c
        return keep(send(src, dst, sent.at[at], got.at[at], here, STAGES[c % 2][2 - stage]))

    one, two, three = {}, {}, {}

    def q_one(c):
        one[c] = start(0, c, part.at[c, pl.ds(4, 4)], r1.at[c])

    loads[0].wait()
    for j in range(4):
        out_high(j)
    attend_back(cot_heads, k, v, probs, cos_twice, sin_signed, cot)
    loads[1].wait()
    fetch(vec_q, vq)
    fetch(vec_o, vo)
    product(1, 0, 1)
    product(1, 1, 1)
    product(0, 0, 1)
    product(0, 1, 1)
    q_one(0)
    q_one(2)
    product(1, 0, 0)
    product(1, 1, 0)
    q_one(1)
    q_one(3)
    product(0, 0, 0)
    product(0, 1, 0)
    facc[...] = jnp.zeros_like(facc)

    def added(c, n, ref):
        part[c, pl.ds(0, n)] = (
            part[c, pl.ds(0, n)].astype(F32) + ref[c].astype(F32)
        ).astype(BF)

    def q_two(c):
        one[c].wait_recv()
        if c + 4 < 8:
            q_one(c + 4)
        added(c, 4, r1)
        two[c] = start(1, c, part.at[c, pl.ds(2, 2)], r2.at[c])

    def q_three(c):
        two[c].wait_recv()
        added(c, 2, r2)
        three[c] = start(2, c, part.at[c, pl.ds(1, 1)], r3.at[c])

    def q_end(c):
        three[c].wait_recv()
        total = part[c, 0].astype(F32) + r3[c, 0].astype(F32)
        gq[pl.ds(c * 128, 128), :] = total.T
        against(gq, vq, c * 128, 8, 0, 2)

    lagged = ((q_two, 0), (q_three, 2), (out_low, 1), (out_y, 3), (q_end, 4), (out_end, 5))
    for n in range(8 + 5):
        if n == 2:
            loads[2].wait()
            loads[3].wait()
        for action, lag in lagged:
            if 0 <= n - lag < 8:
                action(n - lag)

    def exchange(slots, own_slot, peers, base):
        ref = slots.at[own_slot]
        return [
            keep(send(ref, ref, sent.at[base + n], got.at[base + n], here, masks))
            for n, masks in enumerate(peers)
        ]

    def sum_over(over_xy, over_zc, base):
        for copy in exchange(over_xy, xy_own, XY_PEERS, base):
            copy.wait_recv()
        total = over_xy[0]
        for n in range(1, 16):
            total = total + over_xy[n]
        over_zc[zc_own] = total
        for copy in exchange(over_zc, zc_own, ZC_PEERS, base + 15):
            copy.wait_recv()
        total = over_zc[0]
        for n in range(1, 8):
            total = total + over_zc[n]
        return total

    for j in range(K):
        s1[xy_own, pl.ds(j, 1)] = jnp.sum(facc[j], axis=0, keepdims=True)
    first = jnp.sum(sum_over(s1, s2, 48), axis=1, keepdims=True) / count
    second = first
    for i in range(K):
        second = second - gram[:, pl.ds(i, 1)] * first[i : i + 1]
    both = first + second
    weights = [jnp.broadcast_to(both[j : j + 1], (16, 128)) for j in range(K)]

    def cleaned(g, v, c, row_tiles, col_tiles, state):
        def step(r, state):
            rows = pl.ds(pl.multiple_of(r * 16, 16), 16)
            for h in range(col_tiles):
                cols = pl.ds(h * 128, 128)
                value = g[rows, cols]
                for j in range(K):
                    value = value - weights[j] * v[j, rows, cols].astype(F32)
                c[rows, cols] = value
                p = value * value
                state = state + (p[:8] + p[8:])
            return state

        return lax.fori_loop(0, row_tiles, step, state)

    state = cleaned(gq, vq, gq, 64, 2, jnp.zeros((8, 128), F32))
    u1[xy_own] = cleaned(go, vo, go, 16, 8, state)
    squares = sum_over(u1, u2, 70)
    squares = jnp.sum(jnp.sum(squares, axis=1, keepdims=True), axis=0, keepdims=True) / count
    beta = jnp.sqrt(squares + BETA_EPS)
    scale = 1.0 / beta
    next_q[...] = (gq[...] * scale).astype(BF)
    next_o[...] = (go[...] * scale).astype(BF)
    coeffs[pl.ds(0, 8)] = jnp.broadcast_to(both, (8, 128))
    coeffs[pl.ds(8, 8)] = jnp.broadcast_to(beta, (8, 128))
    for copy in copies:
        copy.wait_send()


def tail(
    normed, cot_heads, key_states, values, probs, cos_twice, sin_signed,
    partials, gram, basis_query, basis_output, factor, count,
):
    shape = jax.ShapeDtypeStruct
    return pl.pallas_call(
        functools.partial(tail_kernel, factor, count),
        out_shape=(shape((1024, 256), BF), shape((256, 1024), BF), shape((16, 128), F32)),
        in_specs=any_specs(1) + vmem_specs(6) + any_specs(1) + vmem_specs(1) + any_specs(2),
        out_specs=tuple(vmem_specs(3)),
        scratch_shapes=[
            pltpu.VMEM((256, 512), BF),
            pltpu.VMEM((512, D), BF),
            pltpu.VMEM((8, 8, 256, 128), BF),
            pltpu.VMEM((8, 4, 256, 128), BF),
            pltpu.VMEM((8, 2, 256, 128), BF),
            pltpu.VMEM((8, 1, 256, 128), BF),
            pltpu.VMEM((2, 4, 2, 256, 512), BF),
            pltpu.VMEM((2, 2, 2, 256, 512), BF),
            pltpu.VMEM((2, 2, 256, 512), BF),
            pltpu.VMEM((2, 256, 512), BF),
            pltpu.VMEM((K, 1024, 256), BF),
            pltpu.VMEM((K, 256, 1024), BF),
            pltpu.VMEM((1024, 256), F32),
            pltpu.VMEM((256, 1024), F32),
            pltpu.VMEM((K, 8, 128), F32),
            pltpu.VMEM((16, 8, 128), F32),
            pltpu.VMEM((8, 8, 128), F32),
            pltpu.VMEM((16, 8, 128), F32),
            pltpu.VMEM((8, 8, 128), F32),
            pltpu.SemaphoreType.DMA((4,)),
            pltpu.SemaphoreType.DMA((92,)),
            pltpu.SemaphoreType.DMA((92,)),
        ],
        compiler_params=pltpu.CompilerParams(
            collective_id=1, has_side_effects=True, vmem_limit_bytes=VMEM_BYTES
        ),
        name="tail",
    )(
        normed, cot_heads, key_states, values, probs, cos_twice, sin_signed,
        partials, gram, basis_query, basis_output,
    )


def finish_kernel(q, o, lines, q_out, o_out, coeffs):
    q_out[...] = q[...]
    o_out[...] = o[...]
    for n in range(K + 1):
        coeffs[n] = lines[n, 0]


def finish(next_query, next_output, lines):
    shape = jax.ShapeDtypeStruct
    return pl.pallas_call(
        finish_kernel,
        out_shape=(shape((1024, 256), BF), shape((256, 1024), BF), shape((K + 1,), F32)),
        in_specs=vmem_specs(2) + [pl.BlockSpec(memory_space=pltpu.SMEM)],
        out_specs=tuple(vmem_specs(2) + [pl.BlockSpec(memory_space=pltpu.SMEM)]),
        name="finish",
    )(next_query, next_output, lines)


def body(tokens, segments, norm_gain, q_weight, kv_weight, o_weight, basis_query, basis_output):
    groups = lax.axis_size(DP)
    seq_count, length, model_width = tokens.shape
    row_count = seq_count * length
    qwidth = QH * HD
    query_scale = D ** (-0.5)
    gn_scale = qwidth / (row_count * groups)
    param_count = 2.0 * D * qwidth
    query, tangent, key_states, values, normed, gram, wall = project(
        tokens.reshape(row_count, model_width),
        norm_gain.reshape(1, model_width),
        q_weight,
        basis_query,
        kv_weight,
        basis_output,
        o_weight,
        param_count,
    )
    cos_twice, sin_signed = (jnp.asarray(table) for table in rope_tables(length, HD))
    cot_heads, partials, probs = output_side(
        query, tangent, key_states, values, segments, cos_twice, sin_signed, wall
    )
    next_query, next_output, lines = tail(
        normed,
        cot_heads,
        key_states,
        values,
        probs,
        cos_twice,
        sin_signed,
        partials,
        gram,
        basis_query,
        basis_output,
        gn_scale * query_scale,
        param_count,
    )
    return finish(next_query, next_output, lines)


def solution(mesh):
    finer = Mesh(
        mesh.devices.reshape(4, 2, 4, 2, 2), ("dp_0", "dp_1", "tensor_0", "tensor_1", "tensor_2")
    )
    placed = (
        P(DP, None, None),
        P(DP, None),
        P(),
        P(DP, TENSOR),
        P(None, DP, None),
        P(TENSOR, DP),
        P(None, DP, TENSOR),
        P(None, TENSOR, DP),
    )
    return jax.shard_map(
        body,
        mesh=finer,
        in_specs=placed,
        out_specs=(P(DP, TENSOR), P(TENSOR, DP), P()),
        check_vma=False,
    )
```

```python
import functools
import math

import jax
import jax.numpy as jnp
import numpy as np
from jax import lax
from jax.experimental import pallas as pl
from jax.experimental.pallas import tpu as pltpu
from jax.sharding import Mesh
from jax.sharding import PartitionSpec as P

D = 8192
HD = 128
QH = 32
KVH = 4
K = 8
DP = ("dp_0", "dp_1")
TENSOR = ("tensor_0", "tensor_1", "tensor_2")
DP_TENSOR = ("dp_0", "dp_1", "tensor_0", "tensor_1", "tensor_2")


PRECISE = lax.Precision.HIGHEST
ROPE_BASE = 500000.0
NORM_EPS = 1e-05
BETA_EPS = 1e-06


MESH = pl.DeviceIdType.MESH
VMEM_BYTES = 58 * 1024 * 1024
X1, X3, X2, YH = (1, 0, 0, 0, 0), (3, 0, 0, 0, 0), (2, 0, 0, 0, 0), (0, 1, 0, 0, 0)
Z1, Z3, YL, CORE = (0, 0, 1, 0, 0), (0, 0, 3, 0, 0), (0, 0, 0, 1, 0), (0, 0, 0, 0, 1)
BF = jnp.bfloat16
F32 = jnp.float32


def position():
    return [lax.axis_index(a) for a in DP_TENSOR]


def flipped(value, mask):
    if mask == 0:
        return value
    if mask == 1:
        return value + 1 - 2 * lax.rem(value, 2)
    if mask == 2:
        return lax.rem(value + 2, 4)
    return 3 - value


def peer(here, masks):
    return tuple(flipped(v, m) for v, m in zip(here, masks))


def greet(here, peers):
    barrier = pltpu.get_barrier_semaphore()
    for masks in peers:
        pl.semaphore_signal(barrier, inc=1, device_id=peer(here, masks), device_id_type=MESH)


def greeted(peers):
    pl.semaphore_wait(pltpu.get_barrier_semaphore(), len(peers))


def send(src, dst, send_sem, recv_sem, here, masks):
    copy = pltpu.make_async_remote_copy(
        src_ref=src,
        dst_ref=dst,
        send_sem=send_sem,
        recv_sem=recv_sem,
        device_id=peer(here, masks),
        device_id_type=MESH,
    )
    copy.start()
    return copy


def dp_source(here, bits, stages):
    x, yh = here[0], here[1]
    for bit, masks in zip(bits, stages):
        if masks[0] == 1:
            x = x + bit * (1 - 2 * lax.rem(x, 2))
        elif masks[0] == 3:
            x = x + bit * (3 - 2 * x)
        else:
            yh = yh + bit * (1 - 2 * yh)
    return x * 2 + yh


STAGES = ((X1, YH, X3), (X3, YH, X1))
IN_STAGES = ((X1, YH, X3), (X3, YH, X1), (X1, YH, X3), (X3, YH, X1))
OUT_STAGES = ((YL, Z1, Z3), (YL, Z3, Z1))


XY_PEERS = [
    (x, yh, 0, yl, 0) for x in range(4) for yh in range(2) for yl in range(2) if x or yh or yl
]
ZC_PEERS = [(0, 0, z, 0, c) for z in range(4) for c in range(2) if z or c]


def z_place(mask, kind):
    one, three = {0: (0, 0), 1: (1, 0), 3: (0, 1), 2: (1, 1)}[mask]
    return one + 2 * three if kind == 0 else three + 2 * one


def out_place(r, kind):
    mz, ml = r // 2, r % 2
    return ml + 2 * z_place(mz, kind)


def same_core_masks(r):
    return (0, 0, r // 2, r % 2, 0)


def rope_tables(length, head_width):
    half_width = head_width // 2
    frequency = np.exp(
        np.arange(half_width, dtype=np.float32) * np.float32(-2.0 * math.log(ROPE_BASE) / head_width)
    ).astype(np.float32)
    angles = np.arange(length, dtype=np.float32)[:, None] * frequency[None, :]
    cosine, sine = np.cos(angles), np.sin(angles)
    return (np.concatenate([cosine, cosine], axis=1), np.concatenate([-sine, sine], axis=1))


def rotated(vectors, cos_twice, sin_signed):
    return vectors * cos_twice + pltpu.roll(vectors, HD // 2, 1) * sin_signed


def rotated_back(vectors, cos_twice, sin_signed):
    return vectors * cos_twice - pltpu.roll(vectors, HD // 2, 1) * sin_signed


def dot_wide(a, b, a_dim, b_dim):
    return lax.dot_general(
        a, b, (((a_dim,), (b_dim,)), ((), ())), precision=PRECISE, preferred_element_type=F32
    )


def attend_both(s, q, t, k, v, segments, cos_twice, sin_signed, h, probs):
    scale = HD ** (-0.5)
    rows = pl.ds(s * 256, 256)
    keys = rotated(k[rows].astype(F32), cos_twice[...], sin_signed[...])
    values = v[rows].astype(F32)
    across = jnp.broadcast_to(segments[pl.ds(s, 1)].astype(F32), (256, 256))
    row = lax.broadcasted_iota(jnp.int32, (256, 256), 0)
    column = lax.broadcasted_iota(jnp.int32, (256, 256), 1)
    mask = jnp.logical_and(across == across.T, row >= column)
    for head in range(2):
        cols = pl.ds(head * HD, HD)
        moving = rotated(q[rows, cols].astype(F32), cos_twice[...], sin_signed[...])
        along = rotated(t[rows, cols].astype(F32), cos_twice[...], sin_signed[...])
        scores = jnp.where(mask, dot_wide(moving, keys, 1, 1) * scale, -1e30)
        weights = jnp.exp(scores - jnp.max(scores, axis=1, keepdims=True))
        p = weights / jnp.sum(weights, axis=1, keepdims=True)
        probs[2 * s + head] = p
        slope = jnp.where(mask, dot_wide(along, keys, 1, 1) * scale, 0.0)
        dp = p * (slope - jnp.sum(p * slope, axis=1, keepdims=True))
        heads = dot_wide(p, values, 1, 0).astype(BF).astype(F32) * ((QH * HD) ** (-0.5))
        tangents = dot_wide(dp, values, 1, 0)
        h[s, :, :, cols] = heads.astype(BF).reshape(8, 32, HD)
        h[s, :, :, pl.ds(256 + head * HD, HD)] = tangents.astype(BF).reshape(8, 32, HD)


def attend_back(cot, k, v, probs, cos_twice, sin_signed, out):
    scale = HD ** (-0.5)
    for s in range(2):
        rows = pl.ds(s * 256, 256)
        keys = rotated(k[rows].astype(F32), cos_twice[...], sin_signed[...])
        values = v[rows].astype(F32)
        for head in range(2):
            cols = pl.ds(head * HD, HD)
            given = cot[s, :, :, cols].reshape(256, HD).astype(F32)
            p = probs[2 * s + head]
            slope = dot_wide(given, values, 1, 1)
            ds = p * (slope - jnp.sum(p * slope, axis=1, keepdims=True))
            moving = rotated_back(dot_wide(ds, keys, 1, 0) * scale, cos_twice[...], sin_signed[...])
            out[cols, rows] = moving.T.astype(BF)


SUPER = (0, 1) * 4 + (2, 3) * 4
PIECE = (0, 0, 1, 1, 2, 2, 3, 3) * 2


def project_kernel(
    count, tok, gain, q_w, vec_q, kv_w, vec_o, o_w,
    q_out, t_out, k_out, v_out, normed_out, gram_out, wall,
    x, buf, acc, mine, theirs, vq, vo, w, g1, g2, pairs_acc, load, sent, got,
):
    here = position()
    core = here[4]
    kv_head = here[2]
    for_rows = []
    for s in range(4):
        rows = pl.ds(s * 256, 256)
        kv_cols = pl.ds(pl.multiple_of(kv_head * HD, HD), HD)
        parts = (
            (q_w.at[rows], buf.at[s, 0, :, pl.ds(0, 256)]),
            (vec_q.at[K - 1, rows], buf.at[s, 0, :, pl.ds(256, 256)]),
            (kv_w.at[core, rows, kv_cols], buf.at[s, 0, :, pl.ds(512, 128)]),
        )
        for n, (src, dst) in enumerate(parts):
            copy = pltpu.make_async_copy(src, dst, load.at[3 * s + n])
            copy.start()
            for_rows.append(copy)
    own_out = []
    for kind, src in enumerate((vec_o.at[K - 1], o_w)):
        copy = pltpu.make_async_copy(src, w.at[kind, 0], load.at[16 + kind])
        copy.start()
        own_out.append(copy)
    greet(here, XY_PEERS + ZC_PEERS)
    greeted(XY_PEERS + ZC_PEERS)
    for copy in for_rows:
        copy.wait()

    def start_stage(stage, k):
        s, rows = SUPER[k], pl.ds(PIECE[k] * 64, 64)
        n = 1 << stage
        at = stage * 16 + k
        return send(
            buf.at[s, pl.ds(0, n), rows],
            buf.at[s, pl.ds(n, n), rows],
            sent.at[at],
            got.at[at],
            here,
            IN_STAGES[s][stage],
        )

    out_copies = {}

    def start_out(stage, kind, piece):
        n = 1 << stage
        rows = pl.ds(piece * 64, 64)
        at = 49 + stage * 8 + kind * 4 + piece
        out_copies[stage, kind, piece] = send(
            w.at[kind, pl.ds(0, n), rows],
            w.at[kind, pl.ds(n, n), rows],
            sent.at[at],
            got.at[at],
            here,
            OUT_STAGES[kind][stage],
        )

    def next_out(stage, piece):
        for kind in range(2):
            out_copies[stage, kind, piece].wait_recv()
            start_out(stage + 1, kind, piece)

    for copy in own_out:
        copy.wait()
    for piece in range(2):
        for kind in range(2):
            start_out(0, kind, piece)
    first = [start_stage(0, k) for k in range(6)]
    tok_copy = pltpu.make_async_copy(tok, x, load.at[12])
    tok_copy.start()
    vq_copy = pltpu.make_async_copy(vec_q, vq, load.at[13])
    vq_copy.start()
    vo_copy = pltpu.make_async_copy(vec_o, vo, load.at[14])
    vo_copy.start()
    wall_copies = []

    def keep_wall(kind, lo):
        copy = pltpu.make_async_copy(
            w.at[kind, pl.ds(lo, 4)], wall.at[kind, pl.ds(lo, 4)], load.at[18 + kind + lo // 2]
        )
        copy.start()
        wall_copies.append(copy)

    xy_own = here[0] * 4 + here[1] * 2 + here[3]
    zc_own = here[2] * 2 + here[4]

    def exchange(slots, own, peers, base):
        ref = slots.at[own]
        return [
            send(ref, ref, sent.at[base + n], got.at[base + n], here, masks)
            for n, masks in enumerate(peers)
        ]

    def norm_rows(lo, hi):
        def step(i, carry):
            rows = pl.ds(pl.multiple_of(i * 16, 16), 16)
            total = jnp.zeros((16, 1), F32)
            for c in range(8):
                part = x[rows, pl.ds(c * 1024, 1024)].astype(F32)
                total += jnp.sum(part * part, axis=1, keepdims=True)
            inv = lax.rsqrt(total / D + NORM_EPS)
            for c in range(8):
                cols = pl.ds(c * 1024, 1024)
                x[rows, cols] = (x[rows, cols].astype(F32) * inv * gain[:, cols]).astype(BF)
            return carry

        lax.fori_loop(lo // 16, hi // 16, step, 0)

    def dots(s, lo, hi):
        def step(p, carry):
            bits = (lax.rem(p, 2), lax.rem(p // 2, 2), p // 4)
            source = dp_source(here, bits, IN_STAGES[s])
            cols = pl.ds(pl.multiple_of(source * 1024 + s * 256, 256), 256)
            acc[...] += jnp.dot(x[:, cols], buf[s, p], preferred_element_type=F32)
            return carry

        lax.fori_loop(lo, hi, step, 0)

    pairs = [(i, j) for i in range(K) for j in range(i, K)]

    def gram(part):
        def tile(ref, rows, cols, carry):
            b = [ref[j, rows, cols].astype(F32) for j in range(K)]
            out = []
            for (i, j), a in zip(pairs, carry):
                p = b[i] * b[j]
                out.append(a + (p[:8] + p[8:]))
            return tuple(out)

        def step_q(r, carry):
            rows = pl.ds(pl.multiple_of(r * 16, 16), 16)
            for h in range(2):
                carry = tile(vq, rows, pl.ds(h * 128, 128), carry)
            return carry

        def step_o(r, carry):
            rows = pl.ds(pl.multiple_of(r * 16, 16), 16)
            for h in range(8):
                carry = tile(vo, rows, pl.ds(h * 128, 128), carry)
            return carry

        carry = tuple(pairs_acc[n] for n in range(len(pairs)))
        carry = lax.fori_loop(part * 8, part * 8 + 8, step_q, carry)
        carry = lax.fori_loop(part * 2, part * 2 + 2, step_o, carry)
        for n, a in enumerate(carry):
            pairs_acc[n] = a

    def gram_end():
        lane = lax.broadcasted_iota(jnp.int32, (8, 128), 1)
        row = lax.broadcasted_iota(jnp.int32, (8, 128), 0)
        tile_sum = jnp.zeros((8, 128), F32)
        for n, (i, j) in enumerate(pairs):
            value = jnp.sum(
                jnp.sum(pairs_acc[n], axis=0, keepdims=True), axis=1, keepdims=True
            )
            hit = jnp.logical_or(
                jnp.logical_and(lane == i, row == j), jnp.logical_and(lane == j, row == i)
            )
            tile_sum = tile_sum + jnp.where(hit, value, 0.0)
        g1[xy_own] = tile_sum

    acc[...] = jnp.zeros_like(acc)
    pairs_acc[...] = jnp.zeros_like(pairs_acc)
    second, third = [], []
    out_steps = {
        1: (0, 0), 2: (0, 1), 4: (0, 2), 6: (0, 3), 3: (1, 0), 5: (1, 1), 7: (1, 2), 9: (1, 3)
    }
    for k in range(16):
        first[k].wait_recv()
        second.append(start_stage(1, k))
        if k + 6 < 16:
            first.append(start_stage(0, k + 6))
        if k >= 3:
            second[k - 3].wait_recv()
            third.append(start_stage(2, k - 3))
        if k in out_steps:
            stage, piece = out_steps[k]
            next_out(stage, piece)
        if k in (1, 3):
            start_out(0, 0, k // 2 + 2)
            start_out(0, 1, k // 2 + 2)
        if k == 0:
            tok_copy.wait()
        if k < 8:
            norm_rows(k * 64, k * 64 + 64)
        if k == 7:
            out_copy = pltpu.make_async_copy(x, normed_out, load.at[15])
            out_copy.start()
        if k == 2:
            vq_copy.wait()
            vo_copy.wait()
        if 2 <= k < 10:
            gram(k - 2)
        if k == 10:
            gram_end()
            over_xy = exchange(g1, xy_own, XY_PEERS, 73)
        if k == 11:
            dots(0, 0, 4)
        if k == 12:
            dots(1, 0, 4)
        if k == 13:
            keep_wall(0, 0)
            keep_wall(1, 0)
            for copy in over_xy:
                copy.wait_recv()
            total = g1[0]
            for n in range(1, 16):
                total = total + g1[n]
            g2[zc_own] = total
            over_zc = exchange(g2, zc_own, ZC_PEERS, 88)
        if k == 13:
            for n in (0, 2, 4, 6):
                third[n].wait_recv()
            dots(0, 4, 8)
        if k == 14:
            for n in (1, 3, 5, 7):
                third[n].wait_recv()
            dots(1, 4, 8)
    for k in range(16 - 3, 16):
        second[k].wait_recv()
        third.append(start_stage(2, k))
    dots(2, 0, 4)
    dots(3, 0, 4)
    for kind in range(2):
        for piece in range(4):
            out_copies[2, kind, piece].wait_recv()
        keep_wall(kind, 4)
    for s in (2, 3):
        for n in range(8, 16):
            if SUPER[n] == s:
                third[n].wait_recv()
        dots(s, 4, 8)
    mine[...] = acc[:, pl.ds(512, 128)].astype(BF)
    swap = send(mine, theirs, sent.at[48], got.at[48], here, CORE)
    q_out[...] = acc[:, pl.ds(0, 256)].astype(BF)
    t_out[...] = (acc[:, pl.ds(256, 256)] * (D ** (-0.5))).astype(BF)
    swap.wait()
    own = mine[...].astype(F32)
    other = theirs[...].astype(F32)
    first_core = core == 0
    k_out[...] = jnp.where(first_core, own, other).astype(BF)
    v_out[...] = jnp.where(first_core, other, own).astype(BF)
    for copy in over_zc:
        copy.wait_recv()
    total = g2[0]
    for n in range(1, 8):
        total = total + g2[n]
    gram_out[...] = total / count
    for copy in first + second + third + list(out_copies.values()) + over_xy + over_zc:
        copy.wait_send()
    for copy in wall_copies:
        copy.wait()
    out_copy.wait()


def any_specs(n):
    return [pl.BlockSpec(memory_space=pl.ANY) for _ in range(n)]


def vmem_specs(n):
    return [pl.BlockSpec(memory_space=pltpu.VMEM) for _ in range(n)]


def project(tokens, norm_gain, q_weight, basis_query, kv_weight, basis_output, o_weight, count):
    shape = jax.ShapeDtypeStruct
    return pl.pallas_call(
        functools.partial(project_kernel, count),
        out_shape=(
            shape((512, 256), BF),
            shape((512, 256), BF),
            shape((512, HD), BF),
            shape((512, HD), BF),
            shape((512, D), BF),
            shape((8, 128), F32),
            shape((2, 8, 256, 1024), BF),
        ),
        in_specs=any_specs(1) + vmem_specs(1) + any_specs(5),
        out_specs=tuple(vmem_specs(4) + any_specs(1) + vmem_specs(1) + any_specs(1)),
        scratch_shapes=[
            pltpu.VMEM((512, D), BF),
            pltpu.VMEM((4, 8, 256, 640), BF),
            pltpu.VMEM((512, 640), F32),
            pltpu.VMEM((512, HD), BF),
            pltpu.VMEM((512, HD), BF),
            pltpu.VMEM((K, 1024, 256), BF),
            pltpu.VMEM((K, 256, 1024), BF),
            pltpu.VMEM((2, 8, 256, 1024), BF),
            pltpu.VMEM((16, 8, 128), F32),
            pltpu.VMEM((8, 8, 128), F32),
            pltpu.VMEM((36, 8, 128), F32),
            pltpu.SemaphoreType.DMA((22,)),
            pltpu.SemaphoreType.DMA((95,)),
            pltpu.SemaphoreType.DMA((95,)),
        ],
        compiler_params=pltpu.CompilerParams(
            collective_id=0, has_side_effects=True, vmem_limit_bytes=VMEM_BYTES
        ),
        name="project",
    )(tokens, norm_gain, q_weight, basis_query, kv_weight, basis_output, o_weight)


def output_kernel(
    q, t, k, v, segments, cos_twice, sin_signed, wall, cot, gp_out, probs,
    h, w, g, acc, tb, mine, theirs, cs, c1, c2, c3, gp, load, sent, got,
):
    here = position()
    place = here[2] * 2 + here[3]
    loads = []
    for kind in (0, 1):
        copy = pltpu.make_async_copy(wall.at[kind], w.at[kind], load.at[kind])
        copy.start()
        loads.append(copy)
    peers = [X1, X3, YH, CORE] + [same_core_masks(r) for r in range(1, 8)]
    greet(here, peers)
    copies = []

    def start(at, src, dst, masks):
        copy = send(src, dst, sent.at[at], got.at[at], here, masks)
        copies.append(copy)
        return copy

    def index_of(r):
        z, yl = peer(here[2:4], same_core_masks(r)[2:4])
        return z * 2 + yl

    spread = {}
    for kind in range(2):
        attend_both(kind, q, t, k, v, segments, cos_twice, sin_signed, h, probs)
        if kind == 0:
            greeted(peers)
        for r in range(1, 8):
            spread[r, kind] = start(
                (0, 66)[kind] + r, h.at[kind, index_of(r)], g.at[kind, r, 0], same_core_masks(r)
            )
        g[kind, 0, 0] = h[kind, place]
    def gather(stage, rg, kind):
        n = 1 << stage
        group = pl.ds(rg * 2, 2)
        return start(
            8 + stage * 8 + rg * 2 + kind,
            g.at[kind, group, pl.ds(0, n)],
            g.at[kind, group, pl.ds(n, n)],
            STAGES[kind][stage],
        )

    one, two, three = {}, {}, {}
    for kind in range(2):
        for rg in range(4):
            for r in (rg * 2, rg * 2 + 1):
                if r:
                    spread[r, kind].wait_recv()
            one[rg, kind] = gather(0, rg, kind)
    order = [(rg, kind) for rg in range(4) for kind in range(2)]
    for n, key in enumerate(order):
        one[key].wait_recv()
        two[key] = gather(1, *key)
        if n >= 3:
            two[order[n - 3]].wait_recv()
            three[order[n - 3]] = gather(2, *order[n - 3])
    for key in order[8 - 3 :]:
        two[key].wait_recv()
        three[key] = gather(2, *key)

    def rows_of(r, cols):
        parts = [g[kind, r, :, :, cols].reshape(256, 256) for kind in range(2)]
        return jnp.concatenate(parts, axis=0)

    for copy in loads:
        copy.wait()
    acc[...] = jnp.zeros_like(acc)
    for rg in range(4):
        three[rg, 0].wait_recv()
        three[rg, 1].wait_recv()
        for r in (rg * 2, rg * 2 + 1):
            acc[...] += jnp.dot(
                rows_of(r, pl.ds(0, 256)), w[0, out_place(r, 0)], preferred_element_type=F32
            ) + jnp.dot(
                rows_of(r, pl.ds(256, 256)), w[1, out_place(r, 1)], preferred_element_type=F32
            )
    swaps = []
    for half in range(2):
        rows = pl.ds(half * 256, 256)
        mine[rows] = acc[rows].astype(BF)
        swaps.append(start(56 + half, mine.at[rows], theirs.at[rows], CORE))
    for half in range(2):
        rows = pl.ds(half * 256, 256)
        swaps[half].wait_recv()
        tb[rows] = (mine[rows].astype(F32) + theirs[rows].astype(F32)).astype(BF)

    def scatter(stage, key, src, dst):
        rg, kind = key
        return start(32 + stage * 8 + rg * 2 + kind, src, dst, STAGES[kind][2 - stage])

    one, two, three = {}, {}, {}
    for rg in range(4):
        group = pl.ds(rg * 2, 2)
        for r in (rg * 2, rg * 2 + 1):
            part = lax.dot_general(
                tb[...],
                w[1, out_place(r, 1)],
                (((1,), (1,)), ((), ())),
                preferred_element_type=F32,
            ).astype(BF)
            for kind in range(2):
                cs[kind, r] = part[kind * 256 : kind * 256 + 256].reshape(8, 32, 256)
        for kind in range(2):
            one[rg, kind] = scatter(
                0, (rg, kind), cs.at[kind, group, pl.ds(4, 4)], c1.at[kind, group]
            )

    def added(key, n, ref):
        rg, kind = key
        group = pl.ds(rg * 2, 2)
        cs[kind, group, pl.ds(0, n)] = (
            cs[kind, group, pl.ds(0, n)].astype(F32) + ref[kind, group].astype(F32)
        ).astype(BF)

    def output_grad(r):
        mz, ml = r // 2, r % 2
        block = lax.dot_general(
            rows_of(r, pl.ds(0, 256)),
            tb[...],
            (((0,), (0,)), ((), ())),
            preferred_element_type=F32,
        ).astype(BF)
        for kind in range(2):
            gp[kind, z_place(mz, kind), ml] = block[:, kind * 512 : kind * 512 + 512]

    def second(key):
        rg, kind = key
        one[key].wait_recv()
        added(key, 4, c1)
        group = pl.ds(rg * 2, 2)
        two[key] = scatter(1, key, cs.at[kind, group, pl.ds(2, 2)], c2.at[kind, group])

    def third(key):
        rg, kind = key
        two[key].wait_recv()
        added(key, 2, c2)
        group = pl.ds(rg * 2, 2)
        three[key] = scatter(2, key, cs.at[kind, group, pl.ds(1, 1)], c3.at[kind, group])

    for n, key in enumerate(order):
        second(key)
        if n >= 3:
            third(order[n - 3])
        output_grad(n)
    gp_copy = pltpu.make_async_copy(gp, gp_out, load.at[2])
    gp_copy.start()
    for key in order[8 - 3 :]:
        third(key)
    back = {}
    for rg in range(4):
        for kind in range(2):
            three[rg, kind].wait_recv()
            added((rg, kind), 1, c3)
        for r in (rg * 2, rg * 2 + 1):
            if r:
                back[r] = start(r + 58, cs.at[:, r, 0], cot.at[:, place], same_core_masks(r))
    cot[:, place] = cs[:, 0, 0]
    for r in range(1, 8):
        back[r].wait_recv()
    for copy in copies:
        copy.wait_send()
    gp_copy.wait()


def output_side(query, tangent, key_states, values, segments, cos_twice, sin_signed, wall):
    shape = jax.ShapeDtypeStruct
    return pl.pallas_call(
        output_kernel,
        out_shape=(
            shape((2, 8, 32, 256), BF),
            shape((2, 4, 2, 256, 512), BF),
            shape((4, 256, 256), F32),
        ),
        in_specs=vmem_specs(7) + any_specs(1),
        out_specs=tuple(vmem_specs(1) + any_specs(1) + vmem_specs(1)),
        scratch_shapes=[
            pltpu.VMEM((2, 8, 32, 512), BF),
            pltpu.VMEM((2, 8, 256, 1024), BF),
            pltpu.VMEM((2, 8, 8, 32, 512), BF),
            pltpu.VMEM((512, 1024), F32),
            pltpu.VMEM((512, 1024), BF),
            pltpu.VMEM((512, 1024), BF),
            pltpu.VMEM((512, 1024), BF),
            pltpu.VMEM((2, 8, 8, 32, 256), BF),
            pltpu.VMEM((2, 8, 4, 32, 256), BF),
            pltpu.VMEM((2, 8, 2, 32, 256), BF),
            pltpu.VMEM((2, 8, 1, 32, 256), BF),
            pltpu.VMEM((2, 4, 2, 256, 512), BF),
            pltpu.SemaphoreType.DMA((3,)),
            pltpu.SemaphoreType.DMA((74,)),
            pltpu.SemaphoreType.DMA((74,)),
        ],
        compiler_params=pltpu.CompilerParams(
            collective_id=3, has_side_effects=True, vmem_limit_bytes=VMEM_BYTES
        ),
        name="output_side",
    )(query, tangent, key_states, values, segments, cos_twice, sin_signed, wall)


def tail_kernel(
    factor, count, normed_hbm, cot_heads, k, v, probs, cos_twice, sin_signed, gp, gram, vec_q, vec_o,
    next_q, next_o, coeffs, cot, normed, part, r1, r2, r3, own, z1, z2, y1, vq, vo, gq, go, facc,
    s1, s2, u1, u2, load, sent, got,
):
    here = position()
    xy_own = here[0] * 4 + here[1] * 2 + here[3]
    zc_own = here[2] * 2 + here[4]
    loads = []

    def fetch(src, dst):
        copy = pltpu.make_async_copy(src, dst, load.at[len(loads)])
        copy.start()
        loads.append(copy)

    fetch(gp, own)
    fetch(normed_hbm, normed)
    greet(here, XY_PEERS + ZC_PEERS)
    greeted(XY_PEERS + ZC_PEERS)
    copies = []

    def keep(copy):
        copies.append(copy)
        return copy

    def rows_at(j):
        return pl.ds(j // 2 * 64, 64)

    def start_out(stage, j, src, dst):
        at = 24 + stage * 8 + j
        masks = ((Z3, Z1)[j % 2], (Z1, Z3)[j % 2], YL)[stage]
        return keep(send(src, dst, sent.at[at], got.at[at], here, masks))

    z_high, z_low, over_y = {}, {}, {}

    def out_high(j):
        kind, rows = j % 2, rows_at(j)
        z_high[j] = start_out(0, j, own.at[kind, pl.ds(2, 2), :, rows], z1.at[kind, :, :, rows])

    def out_low(j):
        kind, rows = j % 2, rows_at(j)
        z_high[j].wait_recv()
        if j + 4 < 8:
            out_high(j + 4)
        own[kind, pl.ds(0, 2), :, rows] = (
            own[kind, pl.ds(0, 2), :, rows].astype(F32) + z1[kind, :, :, rows].astype(F32)
        ).astype(BF)
        z_low[j] = start_out(1, j, own.at[kind, 1, :, rows], z2.at[kind, :, rows])

    def out_y(j):
        kind, rows = j % 2, rows_at(j)
        z_low[j].wait_recv()
        own[kind, 0, :, rows] = (
            own[kind, 0, :, rows].astype(F32) + z2[kind, :, rows].astype(F32)
        ).astype(BF)
        over_y[j] = start_out(2, j, own.at[kind, 0, 1, rows], y1.at[kind, rows])

    def against(g, v, row0, tiles, col0, col_tiles):
        def step(i, state):
            rows = pl.ds(pl.multiple_of(row0 + i * 16, 16), 16)
            for h in range(col_tiles):
                cols = pl.ds(col0 + h * 128, 128)
                here_g = g[rows, cols]
                out = []
                for j in range(K):
                    p = here_g * v[j, rows, cols].astype(F32)
                    out.append(state[j] + (p[:8] + p[8:]))
                state = tuple(out)
            return state

        state = lax.fori_loop(0, tiles, step, tuple(facc[j] for j in range(K)))
        for j in range(K):
            facc[j] = state[j]

    def out_end(j):
        kind, rows = j % 2, rows_at(j)
        over_y[j].wait_recv()
        go[rows, pl.ds(kind * 512, 512)] = own[kind, 0, 0, rows].astype(F32) + y1[
            kind, rows
        ].astype(F32)
        against(go, vo, j // 2 * 64, 4, kind * 512, 4)

    def product(low, mid, high):
        source = dp_source(here, (low, mid, high), STAGES[0])
        cols = pl.ds(pl.multiple_of(source * 1024, 1024), 1024)
        block = jnp.dot(cot[...], normed[:, cols], preferred_element_type=F32) * factor
        block = block.astype(BF)
        for c in range(8):
            place = low + 2 * mid + 4 * high if c % 2 == 0 else high + 2 * mid + 4 * low
            part[c, place] = block[:, c * 128 : (c + 1) * 128]

    def start(stage, c, src, dst):
        at = stage * 8 + c
        return keep(send(src, dst, sent.at[at], got.at[at], here, STAGES[c % 2][2 - stage]))

    one, two, three = {}, {}, {}

    def q_one(c):
        one[c] = start(0, c, part.at[c, pl.ds(4, 4)], r1.at[c])

    loads[0].wait()
    for j in range(4):
        out_high(j)
    attend_back(cot_heads, k, v, probs, cos_twice, sin_signed, cot)
    loads[1].wait()
    fetch(vec_q, vq)
    fetch(vec_o, vo)
    product(1, 0, 1)
    product(1, 1, 1)
    product(0, 0, 1)
    product(0, 1, 1)
    q_one(0)
    q_one(2)
    product(1, 0, 0)
    product(1, 1, 0)
    q_one(1)
    q_one(3)
    product(0, 0, 0)
    product(0, 1, 0)
    facc[...] = jnp.zeros_like(facc)

    def added(c, n, ref):
        part[c, pl.ds(0, n)] = (
            part[c, pl.ds(0, n)].astype(F32) + ref[c].astype(F32)
        ).astype(BF)

    def q_two(c):
        one[c].wait_recv()
        if c + 4 < 8:
            q_one(c + 4)
        added(c, 4, r1)
        two[c] = start(1, c, part.at[c, pl.ds(2, 2)], r2.at[c])

    def q_three(c):
        two[c].wait_recv()
        added(c, 2, r2)
        three[c] = start(2, c, part.at[c, pl.ds(1, 1)], r3.at[c])

    def q_end(c):
        three[c].wait_recv()
        total = part[c, 0].astype(F32) + r3[c, 0].astype(F32)
        gq[pl.ds(c * 128, 128), :] = total.T
        against(gq, vq, c * 128, 8, 0, 2)

    lagged = ((q_two, 0), (q_three, 2), (out_low, 1), (out_y, 3), (q_end, 4), (out_end, 5))
    for n in range(8 + 5):
        if n == 2:
            loads[2].wait()
            loads[3].wait()
        for action, lag in lagged:
            if 0 <= n - lag < 8:
                action(n - lag)

    def exchange(slots, own_slot, peers, base):
        ref = slots.at[own_slot]
        return [
            keep(send(ref, ref, sent.at[base + n], got.at[base + n], here, masks))
            for n, masks in enumerate(peers)
        ]

    def sum_over(over_xy, over_zc, base):
        for copy in exchange(over_xy, xy_own, XY_PEERS, base):
            copy.wait_recv()
        total = over_xy[0]
        for n in range(1, 16):
            total = total + over_xy[n]
        over_zc[zc_own] = total
        for copy in exchange(over_zc, zc_own, ZC_PEERS, base + 15):
            copy.wait_recv()
        total = over_zc[0]
        for n in range(1, 8):
            total = total + over_zc[n]
        return total

    for j in range(K):
        s1[xy_own, pl.ds(j, 1)] = jnp.sum(facc[j], axis=0, keepdims=True)
    first = jnp.sum(sum_over(s1, s2, 48), axis=1, keepdims=True) / count
    second = first
    for i in range(K):
        second = second - gram[:, pl.ds(i, 1)] * first[i : i + 1]
    both = first + second
    weights = [jnp.broadcast_to(both[j : j + 1], (16, 128)) for j in range(K)]

    def cleaned(g, v, c, row_tiles, col_tiles, state):
        def step(r, state):
            rows = pl.ds(pl.multiple_of(r * 16, 16), 16)
            for h in range(col_tiles):
                cols = pl.ds(h * 128, 128)
                value = g[rows, cols]
                for j in range(K):
                    value = value - weights[j] * v[j, rows, cols].astype(F32)
                c[rows, cols] = value
                p = value * value
                state = state + (p[:8] + p[8:])
            return state

        return lax.fori_loop(0, row_tiles, step, state)

    state = cleaned(gq, vq, gq, 64, 2, jnp.zeros((8, 128), F32))
    u1[xy_own] = cleaned(go, vo, go, 16, 8, state)
    squares = sum_over(u1, u2, 70)
    squares = jnp.sum(jnp.sum(squares, axis=1, keepdims=True), axis=0, keepdims=True) / count
    beta = jnp.sqrt(squares + BETA_EPS)
    scale = 1.0 / beta
    next_q[...] = (gq[...] * scale).astype(BF)
    next_o[...] = (go[...] * scale).astype(BF)
    coeffs[pl.ds(0, 8)] = jnp.broadcast_to(both, (8, 128))
    coeffs[pl.ds(8, 8)] = jnp.broadcast_to(beta, (8, 128))
    for copy in copies:
        copy.wait_send()


def tail(
    normed, cot_heads, key_states, values, probs, cos_twice, sin_signed,
    partials, gram, basis_query, basis_output, factor, count,
):
    shape = jax.ShapeDtypeStruct
    return pl.pallas_call(
        functools.partial(tail_kernel, factor, count),
        out_shape=(shape((1024, 256), BF), shape((256, 1024), BF), shape((16, 128), F32)),
        in_specs=any_specs(1) + vmem_specs(6) + any_specs(1) + vmem_specs(1) + any_specs(2),
        out_specs=tuple(vmem_specs(3)),
        scratch_shapes=[
            pltpu.VMEM((256, 512), BF),
            pltpu.VMEM((512, D), BF),
            pltpu.VMEM((8, 8, 256, 128), BF),
            pltpu.VMEM((8, 4, 256, 128), BF),
            pltpu.VMEM((8, 2, 256, 128), BF),
            pltpu.VMEM((8, 1, 256, 128), BF),
            pltpu.VMEM((2, 4, 2, 256, 512), BF),
            pltpu.VMEM((2, 2, 2, 256, 512), BF),
            pltpu.VMEM((2, 2, 256, 512), BF),
            pltpu.VMEM((2, 256, 512), BF),
            pltpu.VMEM((K, 1024, 256), BF),
            pltpu.VMEM((K, 256, 1024), BF),
            pltpu.VMEM((1024, 256), F32),
            pltpu.VMEM((256, 1024), F32),
            pltpu.VMEM((K, 8, 128), F32),
            pltpu.VMEM((16, 8, 128), F32),
            pltpu.VMEM((8, 8, 128), F32),
            pltpu.VMEM((16, 8, 128), F32),
            pltpu.VMEM((8, 8, 128), F32),
            pltpu.SemaphoreType.DMA((4,)),
            pltpu.SemaphoreType.DMA((92,)),
            pltpu.SemaphoreType.DMA((92,)),
        ],
        compiler_params=pltpu.CompilerParams(
            collective_id=1, has_side_effects=True, vmem_limit_bytes=VMEM_BYTES
        ),
        name="tail",
    )(
        normed, cot_heads, key_states, values, probs, cos_twice, sin_signed,
        partials, gram, basis_query, basis_output,
    )


def finish_kernel(q, o, lines, q_out, o_out, coeffs):
    q_out[...] = q[...]
    o_out[...] = o[...]
    for n in range(K + 1):
        coeffs[n] = lines[n, 0]


def finish(next_query, next_output, lines):
    shape = jax.ShapeDtypeStruct
    return pl.pallas_call(
        finish_kernel,
        out_shape=(shape((1024, 256), BF), shape((256, 1024), BF), shape((K + 1,), F32)),
        in_specs=vmem_specs(2) + [pl.BlockSpec(memory_space=pltpu.SMEM)],
        out_specs=tuple(vmem_specs(2) + [pl.BlockSpec(memory_space=pltpu.SMEM)]),
        name="finish",
    )(next_query, next_output, lines)


def body(tokens, segments, norm_gain, q_weight, kv_weight, o_weight, basis_query, basis_output):
    groups = lax.axis_size(DP)
    seq_count, length, model_width = tokens.shape
    row_count = seq_count * length
    qwidth = QH * HD
    query_scale = D ** (-0.5)
    gn_scale = qwidth / (row_count * groups)
    param_count = 2.0 * D * qwidth
    query, tangent, key_states, values, normed, gram, wall = project(
        tokens.reshape(row_count, model_width),
        norm_gain.reshape(1, model_width),
        q_weight,
        basis_query,
        kv_weight,
        basis_output,
        o_weight,
        param_count,
    )
    cos_twice, sin_signed = (jnp.asarray(table) for table in rope_tables(length, HD))
    cot_heads, partials, probs = output_side(
        query, tangent, key_states, values, segments, cos_twice, sin_signed, wall
    )
    next_query, next_output, lines = tail(
        normed,
        cot_heads,
        key_states,
        values,
        probs,
        cos_twice,
        sin_signed,
        partials,
        gram,
        basis_query,
        basis_output,
        gn_scale * query_scale,
        param_count,
    )
    return finish(next_query, next_output, lines)


def solution(mesh):
    finer = Mesh(
        mesh.devices.reshape(4, 2, 4, 2, 2), ("dp_0", "dp_1", "tensor_0", "tensor_1", "tensor_2")
    )
    placed = (
        P(DP, None, None),
        P(DP, None),
        P(),
        P(DP, TENSOR),
        P(None, DP, None),
        P(TENSOR, DP),
        P(None, DP, TENSOR),
        P(None, TENSOR, DP),
    )
    return jax.shard_map(
        body,
        mesh=finer,
        in_specs=placed,
        out_specs=(P(DP, TENSOR), P(TENSOR, DP), P()),
        check_vma=False,
    )
```
